32 devices in a mesh: exp: 8 (over z, x), rep: 4 (over y, core).
Axes of the slice: x: 2, y: 2, z: 4, core: 2. Of those that a mesh axis runs over, the one named last changes fastest.
Arguments:
- tokens: bfloat16 [18432, 768], P(('exp', 'rep')), may hold values from -6 to 6
- ln1_gain: bfloat16 [768], P(('exp', 'rep')), may hold values from 0.3984375 to 1.59375
- ln1_bias: bfloat16 [768], P(('exp', 'rep')), may hold values from -1.1953125 to 1.1953125
- w_qkv: bfloat16 [768, 2304], P(('exp', 'rep')), may hold values from -0.21875 to 0.21875
- w_out: bfloat16 [768, 768], P(('exp', 'rep')), may hold values from -2.5 to 2.5
- ln2_gain: bfloat16 [768], P(('exp', 'rep')), may hold values from 0.3984375 to 1.59375
- ln2_bias: bfloat16 [768], P(('exp', 'rep')), may hold values from -0.59765625 to 0.59765625
- w_router: bfloat16 [768, 8], P(('exp', 'rep')), may hold values from -0.109375 to 0.109375
- w_in: bfloat16 [8, 768, 3072], P('exp'), may hold values from -0.21875 to 0.21875
- b_in: bfloat16 [8, 3072], P('exp'), may hold values from -1.796875 to 1.796875
- w_back: bfloat16 [8, 3072, 768], P('exp'), may hold values from -0.625 to 0.625
- b_back: bfloat16 [8, 768], P('exp'), may hold values from -2.390625 to 2.390625
- lengths: int32 [32, 3], P(('exp', 'rep')), may hold values from 1 to 400, 576 in all within a row
- routes: int32 [18432, 2], P(('exp', 'rep')), may hold values from 0 to 7, all different within a row
- priority: int32 [18432], P(('exp', 'rep')), may hold values from 0 to 575, as said below
- padding: int32 [18432], P(('exp', 'rep')), may hold values 0 or 1
- cotangent: bfloat16 [18432, 768], P(('exp', 'rep')), may hold values from -6 to 6
Outputs:
- output: bfloat16 [18432, 768], P(('exp', 'rep'))
- grad_tokens: float32 [18432, 768], P(('exp', 'rep'))
- grad_ln1_gain: float32 [768], P(('exp', 'rep'))
- grad_ln1_bias: float32 [768], P(('exp', 'rep'))
- grad_w_qkv: float32 [768, 2304], P(('exp', 'rep'))
- grad_w_out: float32 [768, 768], P(('exp', 'rep'))
- grad_ln2_gain: float32 [768], P(('exp', 'rep'))
- grad_ln2_bias: float32 [768], P(('exp', 'rep'))
- grad_w_router: float32 [768, 8], P(('exp', 'rep'))
- grad_w_in: float32 [8, 768, 3072], P('exp')
- grad_b_in: float32 [8, 3072], P('exp')
- grad_w_back: float32 [8, 3072, 768], P('exp')
- grad_b_back: float32 [8, 768], P('exp')
The draws below stay inside these ranges and needn't reach their ends.
Inputs may be any that keep to these rules, and one draw needn't show every extreme that they name: `routes`: each row names two different experts. `priority`: in each aligned group of 576 patches every value 0 to 575 appears once. `lengths`: each row sums to 576; its largest entry is 400.
All inputs are finite; a program needn't handle non-finite values. No bound on the sum of `padding` on one device may be relied on, other than what follows from the above.
Results may differ from the reference program's by a relative error of at most 0.014.
Values may be sent and summed in bfloat16 or wider, within the bound.
A program may use at most 192 MiB of HBM per device.

```python
import math
import jax
import jax.numpy as jnp
import numpy as np
from jax import lax

D = 768
HEADS = 12
HEAD = 64
FF = 3072
SLOTS = 576
IMGS = 3
LONGEST = 400
ROWS_DEV = 1
EXPERTS = 8
TOK_DEV = 576
ROWS = 32
TOKENS = 18432
CAP = 152


def draw_priority(key, part):
    keys = jax.random.split(key, TOKENS // TOK_DEV)
    orders = jax.vmap(lambda single: jax.random.permutation(single, TOK_DEV))(keys)
    return orders.reshape(TOKENS).astype(jnp.int32)


def place_ends(array, key, smallest, high):
    dims = array.shape
    index_at = [jax.random.randint(jax.random.fold_in(key, axis), (), 0, dims[axis]) for axis in range(len(dims))]
    array = array.at[tuple(index_at)].set(smallest)
    longest = dims.index(max(dims))
    index_at[longest] = (index_at[longest] + 1) % dims[longest]
    return array.at[tuple(index_at)].set(high)


def shard_levels(own_key, dims, cuts, least, largest):
    def one(position, blocks):
        steps = jax.random.uniform(jax.random.fold_in(jax.random.fold_in(own_key, 6), position), (blocks,), jnp.float32, least / len(cuts), largest / len(cuts))
        return jnp.repeat(jnp.exp(steps), dims[position] // blocks).reshape((-1,) + (1,) * (len(dims) - position - 1))

    level = one(*cuts[0])
    for cut in cuts[1:]:
        level = level * one(*cut)
    return level


def picks_of(rng, rows, number_of, top, lift):
    ranking = jax.random.permutation(jax.random.fold_in(rng, 1), number_of)
    pull = ranking
    for power in range(3):
        pull = pull * pull // number_of
    pull = pull * lift // number_of
    tickets = jax.random.randint(jax.random.fold_in(rng, 2), (rows, number_of), 0, 4096) + pull
    holders = jax.random.permutation(jax.random.fold_in(rng, 3), rows)[jnp.arange(number_of) % rows]
    tickets = jnp.where(jnp.arange(rows)[:, None] == holders[None, :], 1 << 14, tickets)
    score = tickets * number_of + jnp.arange(number_of)
    return lax.top_k(score.astype(jnp.int32), top)[1].astype(jnp.int32)


def profile(number_of, total, most, lean):
    loads = [(1 << 20) // math.isqrt(grade ** lean) + 1 for grade in range(2, number_of + 1)]
    spare, holding = total - most - (number_of - 1), [1] * (number_of - 1)
    while spare > 0:
        candidates = [i for i in range(number_of - 1) if holding[i] < most]
        mass, remaining = sum([loads[i] for i in candidates]), spare
        for i in candidates:
            more = min(most - holding[i], max(1, remaining * loads[i] // mass), spare)
            holding[i] = holding[i] + more
            spare = spare - more
    return np.array([most] + holding)


def ragged(stream_key, amount, total, bound, skew):
    if amount == 2:
        one = jax.random.randint(stream_key, (), max(1, total - bound), min(bound, total - 1) + 1)
        return jnp.stack([one, total - one])
    sizes = jnp.asarray(profile(amount, total, bound, skew), jnp.int32)
    couples = (amount - 1) // 2
    source_of, taker = sizes[1:1 + 2 * couples:2], sizes[2:2 + 2 * couples:2]
    room = jnp.minimum(source_of - 1, bound - taker)
    shifted = jax.random.randint(jax.random.fold_in(stream_key, 1), (couples,), 0, 1 << 20) % (room + 1)
    sizes = sizes.at[1:1 + 2 * couples:2].set(source_of - shifted).at[2:2 + 2 * couples:2].set(taker + shifted)
    return sizes[jax.random.permutation(jax.random.fold_in(stream_key, 2), amount)]


def bell_draw(stream_key, dims, deviation, most, cuts=(), kind=jnp.bfloat16):
    factor_of = shard_levels(stream_key, dims, cuts, -0.22, 0.18) if cuts else 1.0
    drawn = jax.random.normal(stream_key, dims, jnp.float32) * deviation * factor_of
    return jnp.minimum(jnp.maximum(drawn, -most), most).astype(kind)


def setup_inputs(seed: int = 0) -> dict:
    streams_of = jax.random.split(jax.random.key(seed), 18)
    tokens = bell_draw(streams_of[0], (TOKENS, D), 1.0, 6.0, ((0, 32),))
    ln1_gain = jnp.clip(1.0 + 0.12 * jax.random.normal(streams_of[1], (D,), jnp.float32), 0.3984375, 1.59375).astype(jnp.bfloat16)
    ln1_bias = bell_draw(streams_of[2], (D,), 0.2, 1.1953125, ((0, 32),))
    w_qkv = bell_draw(streams_of[3], (D, 3 * D), D ** -0.5, 0.21875, ((0, 32),))
    w_out = bell_draw(streams_of[4], (D, D), (D // 128) ** -0.5, 2.5, ((0, 32),))
    ln2_gain = jnp.clip(1.0 + 0.12 * jax.random.normal(streams_of[5], (D,), jnp.float32), 0.3984375, 1.59375).astype(jnp.bfloat16)
    ln2_bias = bell_draw(streams_of[6], (D,), 0.1, 0.59765625, ((0, 32),))
    w_router = bell_draw(streams_of[7], (D, EXPERTS), (4 * D) ** -0.5, 0.109375, ((0, 32),))
    w_in = bell_draw(streams_of[8], (EXPERTS, D, FF), D ** -0.5, 0.21875, ((0, 8),))
    b_in = bell_draw(streams_of[9], (EXPERTS, FF), 0.3, 1.796875, ((0, 8),))
    w_back = bell_draw(streams_of[10], (EXPERTS, FF, D), (max(1, 2 * FF // (EXPERTS * EXPERTS))) ** -0.5, 0.625, ((0, 8),))
    b_back = bell_draw(streams_of[11], (EXPERTS, D), (EXPERTS / 20), 2.390625, ((0, 8),))
    lengths = jax.vmap(lambda own: ragged(own, IMGS, SLOTS, LONGEST, 1))(jax.random.split(streams_of[12], ROWS)).reshape((ROWS, IMGS)).astype(jnp.int32)
    routes = picks_of(streams_of[13], TOKENS, EXPERTS, 2, 2048)
    priority = draw_priority(jax.random.fold_in(streams_of[17], 71), 0)
    padding = place_ends((jax.random.randint(streams_of[15], (TOKENS,), 0, 8) < 7).astype(jnp.int32), jax.random.fold_in(streams_of[15], 1), 0, 1)
    cotangent = bell_draw(streams_of[16], (TOKENS, D), 1.0, 6.0, ((0, 32),))
    return {"tokens": tokens, "ln1_gain": ln1_gain, "ln1_bias": ln1_bias, "w_qkv": w_qkv, "w_out": w_out, "ln2_gain": ln2_gain, "ln2_bias": ln2_bias, "w_router": w_router, "w_in": w_in, "b_in": b_in, "w_back": w_back, "b_back": b_back, "lengths": lengths, "routes": routes, "priority": priority, "padding": padding, "cotangent": cotangent}


@jax.custom_vjp
def low(v):
    return lax.optimization_barrier(v.astype(jnp.bfloat16)).astype(jnp.float32)

@jax.custom_vjp
def low_back(v):
    return v

def low_keep(v):
    return (low(v), None)

def low_pass(kept, grad):
    return (grad,)

def back_keep(v):
    return (v, None)

def back_low(kept, grad):
    return (low(grad),)
low.defvjp(low_keep, low_pass)
low_back.defvjp(back_keep, back_low)
precise = lax.Precision.HIGHEST

def layer_norm(inputs, gain, offset):
    center = inputs - lax.optimization_barrier(jnp.mean(inputs, axis=-1, keepdims=True))
    return center * lax.rsqrt(lax.optimization_barrier(jnp.mean(center * center, axis=-1, keepdims=True)) + 1e-06) * gain + offset

def segment_ids(lengths_row):
    bounds = jnp.cumsum(lengths_row)
    places = jnp.arange(SLOTS, dtype=jnp.int32)
    return lax.optimization_barrier(jnp.sum((places[:, None] >= bounds[None, :]).astype(jnp.int32), axis=1))

def attend_row(qkv_row, seg_row, pad_row):
    query = qkv_row[:, :D].reshape(SLOTS, HEADS, HEAD)
    keys = qkv_row[:, D:2 * D].reshape(SLOTS, HEADS, HEAD)
    values = qkv_row[:, 2 * D:].reshape(SLOTS, HEADS, HEAD)
    scores = low_back(jnp.einsum('qhc,khc->hqk', query, keys, precision=precise) * HEAD ** (-0.5))
    places = jnp.arange(SLOTS, dtype=jnp.int32)
    allowed = (seg_row[:, None] == seg_row[None, :]) & ((pad_row[None, :] == 1) | (places[:, None] == places[None, :]))
    scores = jnp.where(allowed[None], scores, -1e+30)
    probs = low(jax.nn.softmax(scores, axis=-1))
    mixed = jnp.einsum('hqk,khc->qhc', probs, values, precision=precise)
    return mixed.reshape(SLOTS, D)

def dispatch_tables(routes_block, priority_block, padding_block):
    labels = jnp.arange(EXPERTS, dtype=jnp.int32)
    first_hot = (routes_block[:, 0:1] == labels[None, :]).astype(jnp.int32)
    second_hot = (routes_block[:, 1:2] == labels[None, :]).astype(jnp.int32)
    live = padding_block[:, None]
    earlier = (priority_block[None, :] < priority_block[:, None]).astype(jnp.int32)
    before_first = jnp.dot(earlier, first_hot * live)
    before_second = jnp.dot(earlier, second_hot * live) + lax.optimization_barrier(jnp.sum(first_hot * live, axis=0))[None, :]
    place_first = lax.optimization_barrier(jnp.sum(before_first * first_hot, axis=1))
    place_second = lax.optimization_barrier(jnp.sum(before_second * second_hot, axis=1))
    kept_first = (padding_block == 1) & (place_first < CAP)
    kept_second = (padding_block == 1) & (place_second < CAP)
    slot_labels = jnp.arange(EXPERTS * CAP, dtype=jnp.int32)
    slot_first = routes_block[:, 0] * CAP + place_first
    slot_second = routes_block[:, 1] * CAP + place_second
    pick_first = ((slot_first[:, None] == slot_labels[None, :]) & kept_first[:, None]).astype(jnp.float32)
    pick_second = ((slot_second[:, None] == slot_labels[None, :]) & kept_second[:, None]).astype(jnp.float32)
    return (first_hot.astype(jnp.float32), second_hot.astype(jnp.float32), pick_first, pick_second)

def block_forward(params, block):
    gain_one, bias_one, qkv_weight, out_weight, gain_two, bias_two, router_weight, weight_in, bias_in, weight_back, bias_back = params
    inputs, lengths_block, routes_block, priority_block, padding_block = block
    normed = low(layer_norm(inputs, gain_one, bias_one))
    qkv = low(low_back(jnp.dot(normed, qkv_weight, precision=precise)))
    segments = jax.vmap(segment_ids)(lengths_block)
    mixed = jax.vmap(attend_row)(qkv.reshape(ROWS_DEV, SLOTS, 3 * D), segments, padding_block.reshape(ROWS_DEV, SLOTS))
    mixed = low(low_back(mixed.reshape(TOK_DEV, D)))
    resid = inputs + low_back(jnp.dot(mixed, out_weight, precision=precise))
    routed = low(layer_norm(resid, gain_two, bias_two))
    logits = low_back(jnp.dot(routed, router_weight, precision=precise))
    probs = jax.nn.softmax(logits, axis=-1)
    first_hot, second_hot, pick_first, pick_second = dispatch_tables(routes_block, priority_block, padding_block)
    buffer = low_back(jnp.dot((pick_first + pick_second).T, routed, precision=precise)).reshape(EXPERTS, CAP, D)
    pre = low_back(jnp.einsum('ecd,edf->ecf', buffer, weight_in, precision=precise) + bias_in[:, None, :])
    active = low(jax.nn.gelu(pre, approximate=False))
    result = low(low_back(jnp.einsum('ecf,efd->ecd', active, weight_back, precision=precise) + bias_back[:, None, :]))
    result = result.reshape(EXPERTS * CAP, D)
    gate_first = lax.optimization_barrier(jnp.sum(probs * first_hot, axis=1))
    gate_second = lax.optimization_barrier(jnp.sum(probs * second_hot, axis=1))
    picked_first = jnp.dot(pick_first, result, precision=precise)
    picked_second = jnp.dot(pick_second, result, precision=precise)
    return resid + gate_first[:, None] * picked_first + gate_second[:, None] * picked_second

def reference(tokens, ln1_gain, ln1_bias, w_qkv, w_out, ln2_gain, ln2_bias, w_router, w_in, b_in, w_back, b_back, lengths, routes, priority, padding, cotangent):
    params = (ln1_gain.astype(jnp.float32), ln1_bias.astype(jnp.float32), w_qkv.astype(jnp.float32), w_out.astype(jnp.float32), ln2_gain.astype(jnp.float32), ln2_bias.astype(jnp.float32), w_router.astype(jnp.float32), w_in.astype(jnp.float32), b_in.astype(jnp.float32), w_back.astype(jnp.float32), b_back.astype(jnp.float32))
    groups = TOKENS // TOK_DEV

    def forward(tokens_float, params_float):

        def one_block(block):
            return block_forward(params_float, block)
        blocks_in = (tokens_float.reshape(groups, TOK_DEV, D), lengths.reshape(groups, ROWS_DEV, IMGS), routes.reshape(groups, TOK_DEV, 2), priority.reshape(groups, TOK_DEV), padding.reshape(groups, TOK_DEV))
        return lax.map(jax.checkpoint(one_block), blocks_in).reshape(TOKENS, D)
    output, pullback = jax.vjp(forward, tokens.astype(jnp.float32), params)
    grad_tokens, grads = pullback(cotangent.astype(jnp.float32))
    return (output.astype(jnp.bfloat16), grad_tokens, grads[0], grads[1], grads[2], grads[3], grads[4], grads[5], grads[6], grads[7], grads[8], grads[9], grads[10])
```

```python
import functools

import jax
import jax.numpy as jnp
from jax import lax
from jax.experimental import pallas as pl
from jax.experimental.pallas import tpu as pltpu
from jax.sharding import PartitionSpec as P

D = 768
HEADS = 12
HEAD = 64
SLOTS = 576
ROWS_DEV = 1
TOK_DEV = 576


root_half = 0.7071067811865476
inverse_root_tau = 0.3989422804014327
contract_first = (((0,), (0,)), ((), ()))
contract_last = (((1,), (1,)), ((), ()))


def norm_forward(inputs, gain, offset):
    center = inputs - jnp.mean(inputs, axis=-1, keepdims=True)
    inverse = lax.rsqrt(jnp.mean(center * center, axis=-1, keepdims=True) + 1e-06)
    normal = center * inverse
    return (normal * gain.astype(jnp.float32) + offset.astype(jnp.float32), normal, inverse)


def norm_backward(grad, normal, inverse, gain):
    scaled = grad * gain.astype(jnp.float32)
    grad_in = inverse * (
        scaled
        - jnp.mean(scaled, axis=-1, keepdims=True)
        - normal * jnp.mean(scaled * normal, axis=-1, keepdims=True)
    )
    return (grad_in, jnp.sum(grad * normal, axis=0), jnp.sum(grad, axis=0))


def gelu_slope(pre):
    return 0.5 * (1.0 + lax.erf(pre * root_half)) + pre * inverse_root_tau * jnp.exp(
        -0.5 * pre * pre
    )


def row_masks(lengths, padding):
    bounds = jnp.cumsum(lengths, axis=1)
    places = jnp.arange(SLOTS, dtype=jnp.int32)
    segments = jnp.sum((places[None, :, None] >= bounds[:, None, :]).astype(jnp.int32), axis=2)
    live = padding.reshape(ROWS_DEV, SLOTS) == 1
    same = segments[:, :, None] == segments[:, None, :]
    diagonal = places[:, None] == places[None, :]
    return same & (live[:, None, :] | diagonal[None])


def split_heads(qkv_row):
    query = qkv_row[:, :D].reshape(SLOTS, HEADS, HEAD)
    keys = qkv_row[:, D : 2 * D].reshape(SLOTS, HEADS, HEAD)
    values = qkv_row[:, 2 * D :].reshape(SLOTS, HEADS, HEAD)
    return (query, keys, values)


def masked_scores(query, keys, allowed_row):
    scores = jnp.einsum("qhc,khc->hqk", query, keys, preferred_element_type=jnp.float32) * HEAD ** (
        -0.5
    )
    return jnp.where(allowed_row[None], scores, -1e30)


def attend_forward(qkv_row, allowed_row):
    query, keys, values = split_heads(qkv_row)
    scores = masked_scores(query, keys, allowed_row)
    top = jnp.max(scores, axis=-1, keepdims=True)
    expo = jnp.exp(scores - top)
    total = jnp.sum(expo, axis=-1, keepdims=True)
    probs = (expo / total).astype(jnp.bfloat16)
    mixed = jnp.einsum("hqk,khc->qhc", probs, values, preferred_element_type=jnp.float32)
    return (mixed.reshape(SLOTS, D), top + jnp.log(total))


def attend_backward(qkv_row, allowed_row, lse_row, grad_row):
    query, keys, values = split_heads(qkv_row)
    probs = jnp.exp(masked_scores(query, keys, allowed_row) - lse_row)
    grad_mixed = grad_row.reshape(SLOTS, HEADS, HEAD)
    grad_probs = jnp.einsum("qhc,khc->hqk", grad_mixed, values, preferred_element_type=jnp.float32)
    grad_values = jnp.einsum(
        "hqk,qhc->khc", probs.astype(jnp.bfloat16), grad_mixed, preferred_element_type=jnp.float32
    )
    grad_scores = (
        probs * (grad_probs - jnp.sum(probs * grad_probs, axis=-1, keepdims=True))
    ).astype(jnp.bfloat16)
    grad_query = jnp.einsum(
        "hqk,khc->qhc", grad_scores, keys, preferred_element_type=jnp.float32
    ) * HEAD ** (-0.5)
    grad_keys = jnp.einsum(
        "hqk,qhc->khc", grad_scores, query, preferred_element_type=jnp.float32
    ) * HEAD ** (-0.5)
    joined = jnp.concatenate(
        [grad_query.reshape(SLOTS, D), grad_keys.reshape(SLOTS, D), grad_values.reshape(SLOTS, D)],
        axis=1,
    )
    return joined.astype(jnp.bfloat16)


def dispatch_tables(routes, priority, padding, experts, capacity):
    labels = jnp.arange(experts, dtype=jnp.int32)
    first_hot = (routes[:, 0:1] == labels[None, :]).astype(jnp.bfloat16)
    second_hot = (routes[:, 1:2] == labels[None, :]).astype(jnp.bfloat16)
    live = padding[:, None].astype(jnp.bfloat16)
    earlier = (priority[None, :] < priority[:, None]).astype(jnp.bfloat16)
    before_first = jnp.dot(earlier, first_hot * live, preferred_element_type=jnp.float32)
    first_counts = jnp.sum((first_hot * live).astype(jnp.float32), axis=0)
    before_second = (
        jnp.dot(earlier, second_hot * live, preferred_element_type=jnp.float32)
        + first_counts[None, :]
    )
    place_first = jnp.sum(before_first * first_hot, axis=1).astype(jnp.int32)
    place_second = jnp.sum(before_second * second_hot, axis=1).astype(jnp.int32)
    kept_first = (padding == 1) & (place_first < capacity)
    kept_second = (padding == 1) & (place_second < capacity)
    slot_labels = jnp.arange(experts * capacity, dtype=jnp.int32)
    slot_first = routes[:, 0] * capacity + place_first
    slot_second = routes[:, 1] * capacity + place_second
    pick_first = ((slot_first[:, None] == slot_labels[None, :]) & kept_first[:, None]).astype(
        jnp.bfloat16
    )
    pick_second = ((slot_second[:, None] == slot_labels[None, :]) & kept_second[:, None]).astype(
        jnp.bfloat16
    )
    return (first_hot.astype(jnp.float32), second_hot.astype(jnp.float32), pick_first, pick_second)


LANES = 128
MESH_ID = pl.DeviceIdType.MESH


def bit_count(number):
    return number.bit_length() - 1


def flip(position, bit):
    step = 1 << bit
    return position + (1 - 2 * lax.rem(lax.div(position, step), 2)) * step


def coordinates(position, reps):
    return (lax.div(position, reps), lax.rem(position, reps))


def greet(bits, me, reps):
    barrier = pltpu.get_barrier_semaphore()
    for bit in range(bits):
        pl.semaphore_signal(
            barrier, inc=1, device_id=coordinates(flip(me, bit), reps), device_id_type=MESH_ID
        )
    pl.semaphore_wait(barrier, bits)


def lowest_bit(number):
    return (number & -number).bit_length() - 1


def gather_kernel(devices, reps, own_ref, all_ref, send_sem, recv_sem, local_sem):
    bits = bit_count(devices)
    me = lax.axis_index("exp") * reps + lax.axis_index("rep")
    greet(bits, me, reps)
    local = pltpu.make_async_copy(own_ref, all_ref.at[me], local_sem)
    local.start()

    def owner_of(distance):
        found = me
        for bit in range(bits):
            if distance >> bit & 1:
                found = flip(found, bit)
        return found

    def transfer(source_ref, distance, bit):
        owner = owner_of(distance)
        index = distance + (1 << bit)
        return pltpu.make_async_remote_copy(
            src_ref=source_ref,
            dst_ref=all_ref.at[owner],
            send_sem=send_sem.at[index],
            recv_sem=recv_sem.at[index],
            device_id=coordinates(flip(me, bit), reps),
            device_id_type=MESH_ID,
        )

    def arrival(distance):
        owner = owner_of(distance)
        return pltpu.make_async_remote_copy(
            src_ref=all_ref.at[owner],
            dst_ref=all_ref.at[owner],
            send_sem=send_sem.at[distance],
            recv_sem=recv_sem.at[distance],
            device_id=coordinates(flip(me, lowest_bit(distance)), reps),
            device_id_type=MESH_ID,
        )

    sent = []
    for bit in range(bits):
        copy = transfer(own_ref, 0, bit)
        copy.start()
        sent.append(copy)
    order = sorted(range(1, devices), key=lambda d: (bin(d).count("1"), -d))
    last = []
    for distance in order:
        low = lowest_bit(distance)
        if low == 0:
            last.append(distance)
            continue
        arrival(distance).wait_recv()
        for bit in range(low):
            copy = transfer(all_ref.at[owner_of(distance)], distance, bit)
            copy.start()
            sent.append(copy)
    for distance in last:
        arrival(distance).wait_recv()
    for copy in sent:
        copy.wait_send()
    local.wait()


def gather_blocks(block, devices, reps):
    return pl.pallas_call(
        functools.partial(gather_kernel, devices, reps),
        out_shape=jax.ShapeDtypeStruct((devices,) + block.shape, block.dtype),
        in_specs=[pl.BlockSpec(memory_space=pl.ANY)],
        out_specs=pl.BlockSpec(memory_space=pl.ANY),
        scratch_shapes=[
            pltpu.SemaphoreType.DMA((devices,)),
            pltpu.SemaphoreType.DMA((devices,)),
            pltpu.SemaphoreType.DMA,
        ],
        compiler_params=pltpu.CompilerParams(collective_id=0, has_side_effects=True),
        name="gather_dense",
    )(block)


def scatter_plan(devices, reps):
    bits = bit_count(devices)
    low = min(bit_count(reps) + 1, bits)
    return (bits, low, list(range(low)) + list(range(bits - 1, low - 1, -1)))


def reverse_bits(number, width):
    return sum((number >> bit & 1) << (width - 1 - bit) for bit in range(width))


def scatter_kernel(devices, reps, chunks, arrays, *refs):
    bits, low, plan = scatter_plan(devices, reps)
    ins, outs, refs = (refs[:arrays], refs[arrays : 2 * arrays], refs[2 * arrays :])
    count = len(chunks)
    owns, refs = (refs[:count], refs[count:])
    recvs, refs = ([refs[c * bits : (c + 1) * bits] for c in range(count)], refs[count * bits :])
    send_sem, recv_sem, local_sem = refs
    me = lax.axis_index("exp") * reps + lax.axis_index("rep")
    greet(bits, me, reps)
    high = devices >> low
    rows = owns[0].shape[1]
    my_bit = [lax.rem(lax.div(me, 1 << bit), 2) for bit in range(bits)]
    firsts = 1 << (low - 1)
    stride = firsts + bits - 1

    def first_copies(c):
        array, start, width = chunks[c]
        columns = pl.ds(start, width)
        copies, local = ([], [])
        for rest in range(firsts):
            place = reverse_bits(rest, low - 1) * high
            index = c * stride + rest
            copies.append(
                pltpu.make_async_remote_copy(
                    src_ref=ins[array].at[:, 2 * rest + 1 - my_bit[0], :, columns],
                    dst_ref=recvs[c][0].at[pl.ds(place, high)],
                    send_sem=send_sem.at[index],
                    recv_sem=recv_sem.at[index],
                    device_id=coordinates(flip(me, plan[0]), reps),
                    device_id_type=MESH_ID,
                )
            )
            local.append(
                pltpu.make_async_copy(
                    ins[array].at[:, 2 * rest + my_bit[0], :, columns],
                    owns[c].at[pl.ds(place, high)],
                    local_sem.at[c * firsts + rest],
                )
            )
        return (copies, local)

    def later_copy(c, phase):
        half = devices >> (phase + 1)
        index = c * stride + firsts + phase - 1
        return pltpu.make_async_remote_copy(
            src_ref=recvs[c][phase - 1].at[pl.ds((1 - my_bit[plan[phase]]) * half, half)],
            dst_ref=recvs[c][phase],
            send_sem=send_sem.at[index],
            recv_sem=recv_sem.at[index],
            device_id=coordinates(flip(me, plan[phase]), reps),
            device_id_type=MESH_ID,
        )

    started = [first_copies(c) for c in range(count)]
    for copies, local in started:
        for copy in copies + local:
            copy.start()
    current = [None] * count
    sent = []

    def absorb(c, phase):
        half = devices >> (phase + 1)
        if phase == 0:
            for copy in started[c][0]:
                copy.wait_recv()
            for copy in started[c][1]:
                copy.wait()
            held, base = (owns[c], 0)
        else:
            current[c].wait_recv()
            held, base = (recvs[c][phase - 1], my_bit[plan[phase]] * half)
        into = recvs[c][phase]
        if phase == bits - 1:
            array, start, width = chunks[c]
            outs[array][:, pl.ds(start, width)] = into[0].astype(jnp.float32) + held[base].astype(
                jnp.float32
            )
            return

        def one(i, carry):
            total = into[i].astype(jnp.float32) + held[base + i].astype(jnp.float32)
            into[i] = total.astype(into.dtype)
            return carry

        lax.fori_loop(0, half, one, 0)
        copy = later_copy(c, phase + 1)
        copy.start()
        sent.append(copy)
        current[c] = copy

    for step in range(bits + count - 1):
        for c in range(count):
            phase = step - c
            if 0 <= phase < bits:
                absorb(c, phase)
    for copies, local in started:
        for copy in copies:
            copy.wait_send()
    for copy in sent:
        copy.wait_send()


def scatter_sums(parts, devices, reps):
    bits, low, plan = scatter_plan(devices, reps)
    high = devices >> low
    rows = parts[0].shape[0] // devices
    chunks = []
    for array, part in enumerate(parts):
        width = part.shape[1] if part.shape[1] < D else D
        for start in range(0, part.shape[1], width):
            chunks.append((array, start, width))
    scratch = [pltpu.VMEM((devices // 2, rows, width), jnp.bfloat16) for _, _, width in chunks]
    for _, _, width in chunks:
        for phase in range(bits):
            scratch.append(pltpu.VMEM((devices >> (phase + 1), rows, width), jnp.bfloat16))
    firsts = 1 << (low - 1)
    total = len(chunks) * (firsts + bits - 1)
    return pl.pallas_call(
        functools.partial(scatter_kernel, devices, reps, chunks, len(parts)),
        out_shape=[jax.ShapeDtypeStruct((rows, part.shape[1]), jnp.float32) for part in parts],
        in_specs=[pl.BlockSpec(memory_space=pl.ANY)] * len(parts),
        out_specs=[pl.BlockSpec(memory_space=pltpu.VMEM)] * len(parts),
        scratch_shapes=scratch
        + [
            pltpu.SemaphoreType.DMA((total,)),
            pltpu.SemaphoreType.DMA((total,)),
            pltpu.SemaphoreType.DMA((len(chunks) * firsts,)),
        ],
        compiler_params=pltpu.CompilerParams(
            collective_id=1, has_side_effects=True, vmem_limit_bytes=60 * 1024 * 1024
        ),
        name="scatter_dense",
    )(*[part.reshape(high, 1 << low, rows, part.shape[1]) for part in parts])


def rep_pairs(reps, bit):
    return [(source, source ^ (1 << bit)) for source in range(reps)]


def rep_reduce(partial, reps):
    mine = lax.axis_index("rep")
    for bit in range(bit_count(reps)):
        half = partial.shape[0] // 2
        mine_bit = lax.rem(lax.div(mine, 1 << bit), 2)
        away = lax.dynamic_slice_in_dim(partial, (1 - mine_bit) * half, half, 0)
        kept = lax.dynamic_slice_in_dim(partial, mine_bit * half, half, 0)
        arrived = lax.ppermute(away, "rep", rep_pairs(reps, bit))
        partial = (kept.astype(jnp.float32) + arrived.astype(jnp.float32)).astype(jnp.bfloat16)
    return partial


def rep_spread(piece, reps):
    mine = lax.axis_index("rep")
    for bit in reversed(range(bit_count(reps))):
        mine_bit = lax.rem(lax.div(mine, 1 << bit), 2)
        arrived = lax.ppermute(piece, "rep", rep_pairs(reps, bit))
        piece = jnp.where(
            mine_bit == 0,
            jnp.concatenate([piece, arrived], axis=0),
            jnp.concatenate([arrived, piece], axis=0),
        )
    return piece


def rep_total(small, reps):
    for bit in range(bit_count(reps)):
        arrived = lax.ppermute(small, "rep", rep_pairs(reps, bit))
        small = small + arrived
    return small


def exchange(blocks):
    return lax.all_to_all(blocks, "exp", split_axis=0, concat_axis=0, tiled=True)


def on_device(
    tokens,
    ln1_gain,
    ln1_bias,
    w_qkv,
    w_out,
    ln2_gain,
    ln2_bias,
    w_router,
    w_in,
    b_in,
    w_back,
    b_back,
    lengths,
    routes,
    priority,
    padding,
    cotangent,
):
    experts = lax.axis_size("exp")
    reps = lax.axis_size("rep")
    devices = experts * reps
    capacity = (TOK_DEV * 210 + experts * 100 - 1) // (experts * 100)
    rows = w_qkv.shape[0]
    small = jnp.concatenate(
        [w_router, jnp.stack([ln1_gain, ln1_bias, ln2_gain, ln2_bias], axis=1)], axis=1
    )
    small = jnp.pad(small, ((0, 0), (0, LANES - small.shape[1])))
    packed = jnp.concatenate([w_qkv, w_out, small], axis=1)
    gathered = gather_blocks(packed, devices, reps).reshape(D, packed.shape[1])
    qkv_weight = gathered[:, : 3 * D]
    out_weight = gathered[:, 3 * D : 4 * D]
    router_weight = gathered[:, 4 * D : 4 * D + experts]
    vectors = gathered[:, 4 * D + experts : 4 * D + experts + 4].T
    gain_one, bias_one, gain_two, bias_two = (vectors[0], vectors[1], vectors[2], vectors[3])

    first_hot, second_hot, pick_first, pick_second = dispatch_tables(
        routes, priority, padding, experts, capacity
    )
    picks = pick_first + pick_second
    grad_blocks = lax.dot_general(picks, cotangent, contract_first, preferred_element_type=jnp.float32)
    grad_blocks = grad_blocks.astype(jnp.bfloat16).reshape(experts, capacity, D)
    grad_blocks, gathered_done = lax.optimization_barrier((grad_blocks, qkv_weight))
    qkv_weight = gathered_done
    grad_arrived = exchange(grad_blocks).reshape(experts * capacity, D)

    inputs = tokens.astype(jnp.float32)
    normed, normal_one, inverse_one = norm_forward(inputs, gain_one, bias_one)
    normed_low = normed.astype(jnp.bfloat16)
    qkv = (
        jnp.dot(normed_low, qkv_weight, preferred_element_type=jnp.float32)
        .astype(jnp.bfloat16)
        .reshape(ROWS_DEV, SLOTS, 3 * D)
    )
    allowed = row_masks(lengths, padding)
    mixed, lse = attend_forward(qkv[0], allowed[0])
    mixed_low = mixed.astype(jnp.bfloat16)
    resid = inputs + jnp.dot(mixed_low, out_weight, preferred_element_type=jnp.float32)
    routed_float, normal_two, inverse_two = norm_forward(resid, gain_two, bias_two)
    routed = routed_float.astype(jnp.bfloat16)
    logits = jnp.dot(routed, router_weight, preferred_element_type=jnp.float32)
    probs = jax.nn.softmax(logits, axis=-1)
    gate_first = jnp.sum(probs * first_hot, axis=1)
    gate_second = jnp.sum(probs * second_hot, axis=1)
    buffer = lax.dot_general(picks, routed, contract_first, preferred_element_type=jnp.float32)
    buffer = buffer.astype(jnp.bfloat16).reshape(experts, capacity, D)
    received = exchange(buffer).reshape(experts * capacity, D)
    slot_gates = jnp.sum(
        pick_first.astype(jnp.float32) * gate_first[:, None]
        + pick_second.astype(jnp.float32) * gate_second[:, None],
        axis=0,
    )
    gates = exchange(slot_gates.reshape(experts, capacity)).reshape(experts * capacity, 1)

    first_weight, second_weight = (w_in[0], w_back[0])
    pre = jnp.dot(received, first_weight, preferred_element_type=jnp.float32) + b_in[0].astype(
        jnp.float32
    )
    active = jax.nn.gelu(pre, approximate=False).astype(jnp.bfloat16)
    grad_results = (gates * grad_arrived.astype(jnp.float32)).astype(jnp.bfloat16)
    grad_active = lax.dot_general(
        grad_results, second_weight, contract_last, preferred_element_type=jnp.float32
    )
    grad_pre = (grad_active * gelu_slope(pre)).astype(jnp.bfloat16)
    result = (
        jnp.dot(active, second_weight, preferred_element_type=jnp.float32)
        + b_back[0].astype(jnp.float32)
    ).astype(jnp.bfloat16)
    grad_received = lax.dot_general(
        grad_pre, first_weight, contract_last, preferred_element_type=jnp.float32
    ).astype(jnp.bfloat16)
    slot_grad_gates = jnp.sum(grad_arrived.astype(jnp.float32) * result.astype(jnp.float32), axis=1)
    grad_gate_slots = exchange(slot_grad_gates.reshape(experts, capacity)).reshape(
        1, experts * capacity
    )
    grad_buffer = exchange(grad_received.reshape(experts, capacity, D)).reshape(
        experts * capacity, D
    )
    returned = exchange(result.reshape(experts, capacity, D)).reshape(experts * capacity, D)

    grad_w_back = lax.dot_general(
        active, grad_results, contract_first, preferred_element_type=jnp.float32
    ).astype(jnp.bfloat16)
    grad_w_in = lax.dot_general(
        received, grad_pre, contract_first, preferred_element_type=jnp.float32
    ).astype(jnp.bfloat16)
    grad_b_back = jnp.sum(grad_results.astype(jnp.float32), axis=0)
    grad_b_in = jnp.sum(grad_pre.astype(jnp.float32), axis=0)
    back_total = rep_spread(rep_reduce(grad_w_back, reps), reps).astype(jnp.float32)
    in_total = rep_spread(rep_reduce(grad_w_in, reps), reps).astype(jnp.float32)
    bias_total = rep_total(jnp.concatenate([grad_b_in, grad_b_back]).reshape(-1, LANES), reps)
    bias_total = bias_total.reshape(-1)

    grad_out = cotangent.astype(jnp.float32)
    grad_gate_first = jnp.sum(pick_first.astype(jnp.float32) * grad_gate_slots, axis=1)
    grad_gate_second = jnp.sum(pick_second.astype(jnp.float32) * grad_gate_slots, axis=1)
    grad_probs = grad_gate_first[:, None] * first_hot + grad_gate_second[:, None] * second_hot
    grad_logits = (
        probs * (grad_probs - jnp.sum(probs * grad_probs, axis=1, keepdims=True))
    ).astype(jnp.bfloat16)
    grad_router = lax.dot_general(
        routed, grad_logits, contract_first, preferred_element_type=jnp.float32
    )
    grad_routed = jnp.dot(picks, grad_buffer, preferred_element_type=jnp.float32)
    grad_routed = grad_routed + lax.dot_general(
        grad_logits, router_weight, contract_last, preferred_element_type=jnp.float32
    )
    grad_norm_two, grad_gain_two, grad_bias_two = norm_backward(
        grad_routed, normal_two, inverse_two, gain_two
    )
    grad_resid = grad_out + grad_norm_two
    grad_attn = grad_resid.astype(jnp.bfloat16)
    grad_out_weight = lax.dot_general(
        mixed_low, grad_attn, contract_first, preferred_element_type=jnp.float32
    )
    grad_mixed = lax.dot_general(
        grad_attn, out_weight, contract_last, preferred_element_type=jnp.float32
    )
    grad_mixed = grad_mixed.astype(jnp.bfloat16)
    grad_qkv = attend_backward(qkv[0], allowed[0], lse, grad_mixed)
    grad_qkv_weight = lax.dot_general(
        normed_low, grad_qkv, contract_first, preferred_element_type=jnp.float32
    )
    grad_normed = lax.dot_general(
        grad_qkv, qkv_weight, contract_last, preferred_element_type=jnp.float32
    )
    grad_norm_one, grad_gain_one, grad_bias_one = norm_backward(
        grad_normed, normal_one, inverse_one, gain_one
    )
    grad_tokens = grad_resid + grad_norm_one

    picked_first = jnp.dot(pick_first, returned, preferred_element_type=jnp.float32)
    picked_second = jnp.dot(pick_second, returned, preferred_element_type=jnp.float32)
    output = resid + gate_first[:, None] * picked_first + gate_second[:, None] * picked_second

    grad_small = jnp.concatenate(
        [
            grad_router,
            jnp.stack([grad_gain_one, grad_bias_one, grad_gain_two, grad_bias_two], axis=1),
        ],
        axis=1,
    )
    grad_small = jnp.pad(grad_small, ((0, 0), (0, LANES - grad_small.shape[1])))
    sum_qkv, sum_out, sum_small = scatter_sums(
        [
            grad_qkv_weight.astype(jnp.bfloat16),
            grad_out_weight.astype(jnp.bfloat16),
            grad_small.astype(jnp.bfloat16),
        ],
        devices,
        reps,
    )
    vector_sums = sum_small[:, experts : experts + 4]
    hidden = b_in.shape[1]
    return (
        output.astype(jnp.bfloat16),
        grad_tokens,
        vector_sums[:, 0],
        vector_sums[:, 1],
        sum_qkv,
        sum_out,
        vector_sums[:, 2],
        vector_sums[:, 3],
        sum_small[:, :experts],
        in_total[None],
        bias_total[None, :hidden],
        back_total[None],
        bias_total[None, hidden:],
    )


def solution(mesh):
    return jax.shard_map(
        on_device,
        mesh=mesh,
        in_specs=(
            P(("exp", "rep"), None),
            P(("exp", "rep")),
            P(("exp", "rep")),
            P(("exp", "rep"), None),
            P(("exp", "rep"), None),
            P(("exp", "rep")),
            P(("exp", "rep")),
            P(("exp", "rep"), None),
            P("exp", None, None),
            P("exp", None),
            P("exp", None, None),
            P("exp", None),
            P(("exp", "rep"), None),
            P(("exp", "rep"), None),
            P(("exp", "rep")),
            P(("exp", "rep")),
            P(("exp", "rep"), None),
        ),
        out_specs=(
            P(("exp", "rep"), None),
            P(("exp", "rep"), None),
            P(("exp", "rep")),
            P(("exp", "rep")),
            P(("exp", "rep"), None),
            P(("exp", "rep"), None),
            P(("exp", "rep")),
            P(("exp", "rep")),
            P(("exp", "rep"), None),
            P("exp", None, None),
            P("exp", None),
            P("exp", None, None),
            P("exp", None),
        ),
        check_vma=False,
    )
```

```python
import functools

import jax
import jax.numpy as jnp
from jax import lax
from jax.experimental import pallas as pl
from jax.experimental.pallas import tpu as pltpu
from jax.sharding import PartitionSpec as P

D = 768
HEADS = 12
HEAD = 64
SLOTS = 576
ROWS_DEV = 1
TOK_DEV = 576


root_half = 0.7071067811865476
inverse_root_tau = 0.3989422804014327
contract_first = (((0,), (0,)), ((), ()))
contract_last = (((1,), (1,)), ((), ()))


def norm_forward(inputs, gain, offset):
    center = inputs - jnp.mean(inputs, axis=-1, keepdims=True)
    inverse = lax.rsqrt(jnp.mean(center * center, axis=-1, keepdims=True) + 1e-06)
    normal = center * inverse
    return (normal * gain.astype(jnp.float32) + offset.astype(jnp.float32), normal, inverse)


def norm_backward(grad, normal, inverse, gain):
    scaled = grad * gain.astype(jnp.float32)
    grad_in = inverse * (
        scaled
        - jnp.mean(scaled, axis=-1, keepdims=True)
        - normal * jnp.mean(scaled * normal, axis=-1, keepdims=True)
    )
    return (grad_in, jnp.sum(grad * normal, axis=0), jnp.sum(grad, axis=0))


def gelu_slope(pre):
    return 0.5 * (1.0 + lax.erf(pre * root_half)) + pre * inverse_root_tau * jnp.exp(
        -0.5 * pre * pre
    )


def row_masks(lengths, padding):
    bounds = jnp.cumsum(lengths, axis=1)
    places = jnp.arange(SLOTS, dtype=jnp.int32)
    segments = jnp.sum((places[None, :, None] >= bounds[:, None, :]).astype(jnp.int32), axis=2)
    live = padding.reshape(ROWS_DEV, SLOTS) == 1
    same = segments[:, :, None] == segments[:, None, :]
    diagonal = places[:, None] == places[None, :]
    return same & (live[:, None, :] | diagonal[None])


def split_heads(qkv_row):
    query = qkv_row[:, :D].reshape(SLOTS, HEADS, HEAD)
    keys = qkv_row[:, D : 2 * D].reshape(SLOTS, HEADS, HEAD)
    values = qkv_row[:, 2 * D :].reshape(SLOTS, HEADS, HEAD)
    return (query, keys, values)


def masked_scores(query, keys, allowed_row):
    scores = jnp.einsum("qhc,khc->hqk", query, keys, preferred_element_type=jnp.float32) * HEAD ** (
        -0.5
    )
    return jnp.where(allowed_row[None], scores, -1e30)


def attend_forward(qkv_row, allowed_row):
    query, keys, values = split_heads(qkv_row)
    scores = masked_scores(query, keys, allowed_row)
    top = jnp.max(scores, axis=-1, keepdims=True)
    expo = jnp.exp(scores - top)
    total = jnp.sum(expo, axis=-1, keepdims=True)
    probs = (expo / total).astype(jnp.bfloat16)
    mixed = jnp.einsum("hqk,khc->qhc", probs, values, preferred_element_type=jnp.float32)
    return (mixed.reshape(SLOTS, D), top + jnp.log(total))


def attend_backward(qkv_row, allowed_row, lse_row, grad_row):
    query, keys, values = split_heads(qkv_row)
    probs = jnp.exp(masked_scores(query, keys, allowed_row) - lse_row)
    grad_mixed = grad_row.reshape(SLOTS, HEADS, HEAD)
    grad_probs = jnp.einsum("qhc,khc->hqk", grad_mixed, values, preferred_element_type=jnp.float32)
    grad_values = jnp.einsum(
        "hqk,qhc->khc", probs.astype(jnp.bfloat16), grad_mixed, preferred_element_type=jnp.float32
    )
    grad_scores = (
        probs * (grad_probs - jnp.sum(probs * grad_probs, axis=-1, keepdims=True))
    ).astype(jnp.bfloat16)
    grad_query = jnp.einsum(
        "hqk,khc->qhc", grad_scores, keys, preferred_element_type=jnp.float32
    ) * HEAD ** (-0.5)
    grad_keys = jnp.einsum(
        "hqk,qhc->khc", grad_scores, query, preferred_element_type=jnp.float32
    ) * HEAD ** (-0.5)
    joined = jnp.concatenate(
        [grad_query.reshape(SLOTS, D), grad_keys.reshape(SLOTS, D), grad_values.reshape(SLOTS, D)],
        axis=1,
    )
    return joined.astype(jnp.bfloat16)


def dispatch_tables(routes, priority, padding, experts, capacity, padded):
    labels = jnp.arange(experts, dtype=jnp.int32)
    first_hot = (routes[:, 0:1] == labels[None, :]).astype(jnp.bfloat16)
    second_hot = (routes[:, 1:2] == labels[None, :]).astype(jnp.bfloat16)
    live = padding[:, None].astype(jnp.bfloat16)
    earlier = (priority[None, :] < priority[:, None]).astype(jnp.bfloat16)
    before_first = jnp.dot(earlier, first_hot * live, preferred_element_type=jnp.float32)
    first_counts = jnp.sum((first_hot * live).astype(jnp.float32), axis=0)
    before_second = (
        jnp.dot(earlier, second_hot * live, preferred_element_type=jnp.float32)
        + first_counts[None, :]
    )
    place_first = jnp.sum(before_first * first_hot, axis=1).astype(jnp.int32)
    place_second = jnp.sum(before_second * second_hot, axis=1).astype(jnp.int32)
    kept_first = (padding == 1) & (place_first < capacity)
    kept_second = (padding == 1) & (place_second < capacity)
    slot_labels = jnp.arange(experts * padded, dtype=jnp.int32)
    slot_first = routes[:, 0] * padded + place_first
    slot_second = routes[:, 1] * padded + place_second
    pick_first = ((slot_first[:, None] == slot_labels[None, :]) & kept_first[:, None]).astype(
        jnp.bfloat16
    )
    pick_second = ((slot_second[:, None] == slot_labels[None, :]) & kept_second[:, None]).astype(
        jnp.bfloat16
    )
    return (first_hot.astype(jnp.float32), second_hot.astype(jnp.float32), pick_first, pick_second)


LANES = 128
MESH_ID = pl.DeviceIdType.MESH


def bit_count(number):
    return number.bit_length() - 1


def flip(position, bit):
    step = 1 << bit
    return position + (1 - 2 * lax.rem(lax.div(position, step), 2)) * step


def coordinates(position, reps):
    return (lax.div(position, reps), lax.rem(position, reps))


def greet(bits, me, reps):
    barrier = pltpu.get_barrier_semaphore()
    for bit in range(bits):
        pl.semaphore_signal(
            barrier, inc=1, device_id=coordinates(flip(me, bit), reps), device_id_type=MESH_ID
        )
    pl.semaphore_wait(barrier, bits)


def lowest_bit(number):
    return (number & -number).bit_length() - 1


def gather_kernel(devices, reps, own_ref, all_ref, send_sem, recv_sem, local_sem):
    bits = bit_count(devices)
    me = lax.axis_index("exp") * reps + lax.axis_index("rep")
    greet(bits, me, reps)
    local = pltpu.make_async_copy(own_ref, all_ref.at[me], local_sem)
    local.start()

    def owner_of(distance):
        found = me
        for bit in range(bits):
            if distance >> bit & 1:
                found = flip(found, bit)
        return found

    def transfer(source_ref, distance, bit):
        owner = owner_of(distance)
        index = distance + (1 << bit)
        return pltpu.make_async_remote_copy(
            src_ref=source_ref,
            dst_ref=all_ref.at[owner],
            send_sem=send_sem.at[index],
            recv_sem=recv_sem.at[index],
            device_id=coordinates(flip(me, bit), reps),
            device_id_type=MESH_ID,
        )

    def arrival(distance):
        owner = owner_of(distance)
        return pltpu.make_async_remote_copy(
            src_ref=all_ref.at[owner],
            dst_ref=all_ref.at[owner],
            send_sem=send_sem.at[distance],
            recv_sem=recv_sem.at[distance],
            device_id=coordinates(flip(me, lowest_bit(distance)), reps),
            device_id_type=MESH_ID,
        )

    sent = []
    for bit in range(bits):
        copy = transfer(own_ref, 0, bit)
        copy.start()
        sent.append(copy)
    order = sorted(range(1, devices), key=lambda d: (bin(d).count("1"), -d))
    last = []
    for distance in order:
        low = lowest_bit(distance)
        if low == 0:
            last.append(distance)
            continue
        arrival(distance).wait_recv()
        for bit in range(low):
            copy = transfer(all_ref.at[owner_of(distance)], distance, bit)
            copy.start()
            sent.append(copy)
    for distance in last:
        arrival(distance).wait_recv()
    for copy in sent:
        copy.wait_send()
    local.wait()


def gather_blocks(block, devices, reps):
    return pl.pallas_call(
        functools.partial(gather_kernel, devices, reps),
        out_shape=jax.ShapeDtypeStruct((devices,) + block.shape, block.dtype),
        in_specs=[pl.BlockSpec(memory_space=pl.ANY)],
        out_specs=pl.BlockSpec(memory_space=pl.ANY),
        scratch_shapes=[
            pltpu.SemaphoreType.DMA((devices,)),
            pltpu.SemaphoreType.DMA((devices,)),
            pltpu.SemaphoreType.DMA,
        ],
        compiler_params=pltpu.CompilerParams(collective_id=0, has_side_effects=True),
        name="gather_dense",
    )(block)


def scatter_plan(devices, reps):
    bits = bit_count(devices)
    low = min(bit_count(reps) + 1, bits)
    return (bits, low, list(range(low)) + list(range(bits - 1, low - 1, -1)))


def reverse_bits(number, width):
    return sum((number >> bit & 1) << (width - 1 - bit) for bit in range(width))


def scatter_kernel(devices, reps, chunks, arrays, *refs):
    bits, low, plan = scatter_plan(devices, reps)
    ins, outs, refs = (refs[:arrays], refs[arrays : 2 * arrays], refs[2 * arrays :])
    count = len(chunks)
    owns, refs = (refs[:count], refs[count:])
    recvs, refs = ([refs[c * bits : (c + 1) * bits] for c in range(count)], refs[count * bits :])
    send_sem, recv_sem, local_sem = refs
    me = lax.axis_index("exp") * reps + lax.axis_index("rep")
    greet(bits, me, reps)
    high = devices >> low
    rows = owns[0].shape[1]
    my_bit = [lax.rem(lax.div(me, 1 << bit), 2) for bit in range(bits)]
    firsts = 1 << (low - 1)
    stride = firsts + bits - 1

    def first_copies(c):
        array, start, width = chunks[c]
        columns = pl.ds(start, width)
        copies, local = ([], [])
        for rest in range(firsts):
            place = reverse_bits(rest, low - 1) * high
            index = c * stride + rest
            copies.append(
                pltpu.make_async_remote_copy(
                    src_ref=ins[array].at[:, 2 * rest + 1 - my_bit[0], :, columns],
                    dst_ref=recvs[c][0].at[pl.ds(place, high)],
                    send_sem=send_sem.at[index],
                    recv_sem=recv_sem.at[index],
                    device_id=coordinates(flip(me, plan[0]), reps),
                    device_id_type=MESH_ID,
                )
            )
            local.append(
                pltpu.make_async_copy(
                    ins[array].at[:, 2 * rest + my_bit[0], :, columns],
                    owns[c].at[pl.ds(place, high)],
                    local_sem.at[c * firsts + rest],
                )
            )
        return (copies, local)

    def later_copy(c, phase):
        half = devices >> (phase + 1)
        index = c * stride + firsts + phase - 1
        return pltpu.make_async_remote_copy(
            src_ref=recvs[c][phase - 1].at[pl.ds((1 - my_bit[plan[phase]]) * half, half)],
            dst_ref=recvs[c][phase],
            send_sem=send_sem.at[index],
            recv_sem=recv_sem.at[index],
            device_id=coordinates(flip(me, plan[phase]), reps),
            device_id_type=MESH_ID,
        )

    started = [first_copies(c) for c in range(count)]
    for copies, local in started:
        for copy in copies + local:
            copy.start()
    current = [None] * count
    sent = []

    def absorb(c, phase):
        half = devices >> (phase + 1)
        if phase == 0:
            for copy in started[c][0]:
                copy.wait_recv()
            for copy in started[c][1]:
                copy.wait()
            held, base = (owns[c], 0)
        else:
            current[c].wait_recv()
            held, base = (recvs[c][phase - 1], my_bit[plan[phase]] * half)
        into = recvs[c][phase]
        if phase == bits - 1:
            array, start, width = chunks[c]
            outs[array][:, pl.ds(start, width)] = into[0].astype(jnp.float32) + held[base].astype(
                jnp.float32
            )
            return

        def one(i, carry):
            total = into[i].astype(jnp.float32) + held[base + i].astype(jnp.float32)
            into[i] = total.astype(into.dtype)
            return carry

        lax.fori_loop(0, half, one, 0)
        copy = later_copy(c, phase + 1)
        copy.start()
        sent.append(copy)
        current[c] = copy

    for step in range(bits + count - 1):
        for c in range(count):
            phase = step - c
            if 0 <= phase < bits:
                absorb(c, phase)
    for copies, local in started:
        for copy in copies:
            copy.wait_send()
    for copy in sent:
        copy.wait_send()


def scatter_sums(parts, devices, reps):
    bits, low, plan = scatter_plan(devices, reps)
    high = devices >> low
    rows = parts[0].shape[0] // devices
    chunks = []
    for array, part in enumerate(parts):
        width = part.shape[1] if part.shape[1] < D else D
        for start in range(0, part.shape[1], width):
            chunks.append((array, start, width))
    scratch = [pltpu.VMEM((devices // 2, rows, width), jnp.bfloat16) for _, _, width in chunks]
    for _, _, width in chunks:
        for phase in range(bits):
            scratch.append(pltpu.VMEM((devices >> (phase + 1), rows, width), jnp.bfloat16))
    firsts = 1 << (low - 1)
    total = len(chunks) * (firsts + bits - 1)
    return pl.pallas_call(
        functools.partial(scatter_kernel, devices, reps, chunks, len(parts)),
        out_shape=[jax.ShapeDtypeStruct((rows, part.shape[1]), jnp.float32) for part in parts],
        in_specs=[pl.BlockSpec(memory_space=pl.ANY)] * len(parts),
        out_specs=[pl.BlockSpec(memory_space=pltpu.VMEM)] * len(parts),
        scratch_shapes=scratch
        + [
            pltpu.SemaphoreType.DMA((total,)),
            pltpu.SemaphoreType.DMA((total,)),
            pltpu.SemaphoreType.DMA((len(chunks) * firsts,)),
        ],
        compiler_params=pltpu.CompilerParams(
            collective_id=1, has_side_effects=True, vmem_limit_bytes=60 * 1024 * 1024
        ),
        name="scatter_dense",
    )(*[part.reshape(high, 1 << low, rows, part.shape[1]) for part in parts])


def rep_pairs(reps, bit):
    return [(source, source ^ (1 << bit)) for source in range(reps)]


def rep_reduce(partial, reps):
    mine = lax.axis_index("rep")
    for bit in range(bit_count(reps)):
        half = partial.shape[0] // 2
        mine_bit = lax.rem(lax.div(mine, 1 << bit), 2)
        away = lax.dynamic_slice_in_dim(partial, (1 - mine_bit) * half, half, 0)
        kept = lax.dynamic_slice_in_dim(partial, mine_bit * half, half, 0)
        arrived = lax.ppermute(away, "rep", rep_pairs(reps, bit))
        partial = (kept.astype(jnp.float32) + arrived.astype(jnp.float32)).astype(jnp.bfloat16)
    return partial


def rep_spread(piece, reps):
    mine = lax.axis_index("rep")
    for bit in reversed(range(bit_count(reps))):
        mine_bit = lax.rem(lax.div(mine, 1 << bit), 2)
        arrived = lax.ppermute(piece, "rep", rep_pairs(reps, bit))
        piece = jnp.where(
            mine_bit == 0,
            jnp.concatenate([piece, arrived], axis=0),
            jnp.concatenate([arrived, piece], axis=0),
        )
    return piece


def rep_total(small, reps):
    for bit in range(bit_count(reps)):
        arrived = lax.ppermute(small, "rep", rep_pairs(reps, bit))
        small = small + arrived
    return small


def row_of(column, width):
    count = column.shape[0]
    down = lax.broadcasted_iota(jnp.int32, (count, width), 0)
    across = lax.broadcasted_iota(jnp.int32, (count, width), 1)
    return jnp.sum(jnp.where(down == across, column, 0.0), axis=0, keepdims=True)


def column_of(row, count):
    width = row.shape[1]
    down = lax.broadcasted_iota(jnp.int32, (count, width), 0)
    across = lax.broadcasted_iota(jnp.int32, (count, width), 1)
    return jnp.sum(jnp.where(down == across, row, 0.0), axis=1, keepdims=True)


def three_terms(value):
    high = value.astype(jnp.bfloat16).astype(jnp.float32)
    rest = value - high
    middle = rest.astype(jnp.bfloat16).astype(jnp.float32)
    return (high, middle, rest - middle)


def expert_kernel(
    experts,
    capacity,
    padded,
    block,
    send_ref,
    grad_ref,
    w_in_ref,
    w_back_ref,
    b_in_ref,
    b_back_ref,
    return_ref,
    result_ref,
    sum_back_ref,
    sum_in_ref,
    sum_b_in_ref,
    sum_b_back_ref,
    slots,
    grads,
    gated,
    weight_in,
    weight_back,
    active,
    grad_pre,
    back_rows,
    result_rows,
    result_total,
    back_total,
    stage_back,
    stage_in,
    load_sem,
    send_sem,
    recv_sem,
    return_send_sem,
    return_recv_sem,
    result_sem,
    stage_sem,
):
    mine = lax.axis_index("exp")
    rep = lax.axis_index("rep")
    bits = bit_count(experts)
    groups = experts // 2
    hidden = weight_in.shape[1]
    steps = hidden // block
    lanes = 256 if capacity <= 256 else D
    gate_row = capacity - (padded - 16)

    barrier = pltpu.get_barrier_semaphore()

    def greet_one(step, carry):
        other = lax.rem(mine + step, experts)
        pl.semaphore_signal(barrier, inc=1, device_id=(other, rep), device_id_type=MESH_ID)
        return carry

    lax.fori_loop(1, experts, greet_one, 0)

    def group_of(index):
        half = lax.div(mine, 2)
        found = half
        for bit in range(bits - 1):
            found = found + lax.rem(lax.div(index, 1 << bit), 2) * (
                (1 - 2 * lax.rem(lax.div(half, 1 << bit), 2)) * (1 << bit)
            )
        return found

    def place(expert):
        return pl.ds(pl.multiple_of(expert * padded, 16), padded)

    def outgoing(expert):
        return pltpu.make_async_remote_copy(
            src_ref=send_ref.at[expert],
            dst_ref=slots.at[place(mine)],
            send_sem=send_sem.at[expert],
            recv_sem=recv_sem.at[mine],
            device_id=(expert, rep),
            device_id_type=MESH_ID,
        )

    def incoming(expert):
        return pltpu.make_async_remote_copy(
            src_ref=send_ref.at[mine],
            dst_ref=slots.at[place(expert)],
            send_sem=send_sem.at[expert],
            recv_sem=recv_sem.at[expert],
            device_id=(expert, rep),
            device_id_type=MESH_ID,
        )

    def going_back(expert):
        return pltpu.make_async_remote_copy(
            src_ref=back_rows.at[place(expert)],
            dst_ref=return_ref.at[mine],
            send_sem=return_send_sem.at[expert],
            recv_sem=return_recv_sem.at[mine],
            device_id=(expert, rep),
            device_id_type=MESH_ID,
        )

    def coming_back(expert):
        return pltpu.make_async_remote_copy(
            src_ref=back_rows.at[place(expert)],
            dst_ref=return_ref.at[expert],
            send_sem=return_send_sem.at[expert],
            recv_sem=return_recv_sem.at[expert],
            device_id=(expert, rep),
            device_id_type=MESH_ID,
        )

    neighbour = flip(mine, 0)
    loads = [
        pltpu.make_async_copy(send_ref.at[mine], slots.at[place(mine)], load_sem.at[0]),
        pltpu.make_async_copy(grad_ref, grads, load_sem.at[1]),
        pltpu.make_async_copy(w_in_ref, weight_in, load_sem.at[2]),
        pltpu.make_async_copy(w_back_ref, weight_back, load_sem.at[3]),
    ]
    for copy in loads:
        copy.start()
    pl.semaphore_wait(barrier, experts - 1)

    def send_group(index):
        pair = group_of(index)
        outgoing(2 * pair).start()
        outgoing(2 * pair + 1).start()

    outgoing(neighbour).start()
    if groups > 2:
        send_group(2)
    if groups > 1:
        send_group(1)
    for copy in loads:
        copy.wait()

    def send_back_group(index):
        pair = group_of(index)
        going_back(2 * pair).start()
        going_back(2 * pair + 1).start()

    def gate_columns(expert):
        tail = slots[pl.ds(pl.multiple_of(expert * padded + padded - 16, 16), 16), :].astype(jnp.float32)
        row = jnp.sum(tail[gate_row : gate_row + 3, :lanes], axis=0, keepdims=True)
        return column_of(row, padded)

    def group_step(index, carry):
        pair = group_of(index)

        @pl.when(index == 0)
        def _():
            incoming(neighbour).wait_recv()

        @pl.when(index > 0)
        def _():
            incoming(2 * pair).wait_recv()
            incoming(2 * pair + 1).wait_recv()

        @pl.when(jnp.logical_and(index >= 1, index + 2 < groups))
        def _():
            send_group(index + 2)

        @pl.when(index == 1)
        def _():
            going_back(neighbour).start()

        @pl.when(index > 1)
        def _():
            send_back_group(index - 1)

        here = pl.ds(pl.multiple_of(pair * 2 * padded, 16), 2 * padded)
        for side in range(2):
            spot = place(2 * pair + side)
            gate = gate_columns(2 * pair + side)
            gated[spot, :] = (gate * grads[spot, :].astype(jnp.float32)).astype(jnp.bfloat16)

        def hidden_step(step, inner):
            columns = pl.ds(pl.multiple_of(step * block, block), block)
            pre = (
                jnp.dot(slots[here, :], weight_in[:, columns], preferred_element_type=jnp.float32)
                + b_in_ref[:, columns]
            )
            grad_active = lax.dot_general(
                gated[here, :],
                weight_back[columns, :],
                contract_last,
                preferred_element_type=jnp.float32,
            )
            cumulative = 0.5 * (1.0 + lax.erf(pre * root_half))
            slope = cumulative + pre * inverse_root_tau * jnp.exp(-0.5 * pre * pre)
            active_low = (pre * cumulative).astype(jnp.bfloat16)
            grad_low = (grad_active * slope).astype(jnp.bfloat16)
            active[here, columns] = active_low
            grad_pre[here, columns] = grad_low
            result_part = jnp.dot(
                active_low, weight_back[columns, :], preferred_element_type=jnp.float32
            )
            back_part = lax.dot_general(
                grad_low, weight_in[:, columns], contract_last, preferred_element_type=jnp.float32
            )

            @pl.when(step == 0)
            def _():
                result_total[...] = result_part
                back_total[...] = back_part

            @pl.when(step > 0)
            def _():
                result_total[...] += result_part
                back_total[...] += back_part

            return inner

        lax.fori_loop(0, steps, hidden_step, 0)
        for side in range(2):
            expert = 2 * pair + side
            span = slice(side * padded, (side + 1) * padded)
            spot = place(expert)
            result_low = (result_total[span, :] + b_back_ref[...]).astype(jnp.bfloat16)
            result_rows[spot, :] = result_low
            grad_gate = jnp.sum(
                grads[spot, :].astype(jnp.float32) * result_low.astype(jnp.float32),
                axis=1,
                keepdims=True,
            )
            gate_line = row_of(
                jnp.where(
                    lax.broadcasted_iota(jnp.int32, (padded, 1), 0) < capacity, grad_gate, 0.0
                ),
                lanes,
            )
            if lanes < D:
                gate_line = jnp.concatenate(
                    [gate_line, jnp.zeros((1, D - lanes), jnp.float32)], axis=1
                )
            high, middle, lowest = three_terms(gate_line)
            row = lax.broadcasted_iota(jnp.int32, (padded, D), 0)
            value = back_total[span, :]
            value = jnp.where(row == capacity, high, value)
            value = jnp.where(row == capacity + 1, middle, value)
            value = jnp.where(row == capacity + 2, lowest, value)
            back_rows[spot, :] = value.astype(jnp.bfloat16)
        return carry

    lax.fori_loop(0, groups, group_step, 0)
    if groups > 1:
        send_back_group(groups - 1)
    else:
        going_back(neighbour).start()
    own_back = pltpu.make_async_copy(back_rows.at[place(mine)], return_ref.at[mine], load_sem.at[0])
    own_back.start()
    results = pltpu.make_async_copy(result_rows, result_ref, result_sem)
    results.start()

    sum_b_back_ref[...] = jnp.sum(gated[...].astype(jnp.float32), axis=0, keepdims=True)

    def stages(step, slot):
        columns = pl.ds(pl.multiple_of(step * block, block), block)
        return (
            pltpu.make_async_copy(stage_back.at[slot], sum_back_ref.at[columns, :], stage_sem.at[0, slot]),
            pltpu.make_async_copy(stage_in.at[slot], sum_in_ref.at[:, columns], stage_sem.at[1, slot]),
        )

    def sum_step(step, carry):
        columns = pl.ds(pl.multiple_of(step * block, block), block)
        slot = lax.rem(step, 2)

        @pl.when(step >= 2)
        def _():
            for copy in stages(step - 2, slot):
                copy.wait()

        stage_back[slot] = lax.dot_general(
            active[:, columns], gated[...], contract_first, preferred_element_type=jnp.float32
        ).astype(jnp.bfloat16)
        stage_in[slot] = lax.dot_general(
            slots[...], grad_pre[:, columns], contract_first, preferred_element_type=jnp.float32
        ).astype(jnp.bfloat16)
        sum_b_in_ref[:, columns] = jnp.sum(
            grad_pre[:, columns].astype(jnp.float32), axis=0, keepdims=True
        )
        for copy in stages(step, slot):
            copy.start()
        return carry

    lax.fori_loop(0, steps, sum_step, 0)
    for step in range(max(steps - 2, 0), steps):
        for copy in stages(step, step % 2):
            copy.wait()
    own_back.wait()
    results.wait()

    def finish(step, carry):
        other = lax.rem(mine + step, experts)
        outgoing(other).wait_send()
        going_back(other).wait_send()
        coming_back(other).wait_recv()
        return carry

    lax.fori_loop(1, experts, finish, 0)


def run_experts(buffer, grads, w_in, w_back, b_in, b_back, capacity):
    experts, padded = (buffer.shape[0], buffer.shape[1])
    hidden = w_in.shape[1]
    block = 512
    rows = experts * padded
    low = jnp.bfloat16
    anywhere = pl.BlockSpec(memory_space=pl.ANY)
    inside = pl.BlockSpec(memory_space=pltpu.VMEM)
    return pl.pallas_call(
        functools.partial(expert_kernel, experts, capacity, padded, block),
        out_shape=[
            jax.ShapeDtypeStruct((experts, padded, D), low),
            jax.ShapeDtypeStruct((rows, D), low),
            jax.ShapeDtypeStruct((hidden, D), low),
            jax.ShapeDtypeStruct((D, hidden), low),
            jax.ShapeDtypeStruct((1, hidden), jnp.float32),
            jax.ShapeDtypeStruct((1, D), jnp.float32),
        ],
        in_specs=[anywhere, anywhere, anywhere, anywhere, inside, inside],
        out_specs=[anywhere, anywhere, anywhere, anywhere, inside, inside],
        scratch_shapes=[
            pltpu.VMEM((rows, D), low),
            pltpu.VMEM((rows, D), low),
            pltpu.VMEM((rows, D), low),
            pltpu.VMEM((D, hidden), low),
            pltpu.VMEM((hidden, D), low),
            pltpu.VMEM((rows, hidden), low),
            pltpu.VMEM((rows, hidden), low),
            pltpu.VMEM((rows, D), low),
            pltpu.VMEM((rows, D), low),
            pltpu.VMEM((2 * padded, D), jnp.float32),
            pltpu.VMEM((2 * padded, D), jnp.float32),
            pltpu.VMEM((2, block, D), low),
            pltpu.VMEM((2, D, block), low),
            pltpu.SemaphoreType.DMA((4,)),
            pltpu.SemaphoreType.DMA((experts,)),
            pltpu.SemaphoreType.DMA((experts,)),
            pltpu.SemaphoreType.DMA((experts,)),
            pltpu.SemaphoreType.DMA((experts,)),
            pltpu.SemaphoreType.DMA,
            pltpu.SemaphoreType.DMA((2, 2)),
        ],
        compiler_params=pltpu.CompilerParams(
            collective_id=2, has_side_effects=True, vmem_limit_bytes=60 * 1024 * 1024
        ),
        cost_estimate=pl.CostEstimate(
            flops=12 * rows * D * hidden, bytes_accessed=40 << 20, transcendentals=2 * rows * hidden
        ),
        name="experts",
    )(buffer, grads.reshape(rows, D), w_in, w_back, b_in.astype(jnp.float32), b_back.astype(jnp.float32))


def exchange(blocks):
    return lax.all_to_all(blocks, "exp", split_axis=0, concat_axis=0, tiled=True)


def on_device(
    tokens,
    ln1_gain,
    ln1_bias,
    w_qkv,
    w_out,
    ln2_gain,
    ln2_bias,
    w_router,
    w_in,
    b_in,
    w_back,
    b_back,
    lengths,
    routes,
    priority,
    padding,
    cotangent,
):
    experts = lax.axis_size("exp")
    reps = lax.axis_size("rep")
    devices = experts * reps
    capacity = (TOK_DEV * 210 + experts * 100 - 1) // (experts * 100)
    padded = -(-(capacity + 3) // 16) * 16
    rows = w_qkv.shape[0]
    small = jnp.concatenate(
        [w_router, jnp.stack([ln1_gain, ln1_bias, ln2_gain, ln2_bias], axis=1)], axis=1
    )
    small = jnp.pad(small, ((0, 0), (0, LANES - small.shape[1])))
    packed = jnp.concatenate([w_qkv, w_out, small], axis=1)
    gathered = gather_blocks(packed, devices, reps).reshape(D, packed.shape[1])
    qkv_weight = gathered[:, : 3 * D]
    out_weight = gathered[:, 3 * D : 4 * D]
    router_weight = gathered[:, 4 * D : 4 * D + experts]
    vectors = gathered[:, 4 * D + experts : 4 * D + experts + 4].T
    gain_one, bias_one, gain_two, bias_two = (vectors[0], vectors[1], vectors[2], vectors[3])

    first_hot, second_hot, pick_first, pick_second = dispatch_tables(
        routes, priority, padding, experts, capacity, padded
    )
    picks = pick_first + pick_second
    grad_blocks = lax.dot_general(picks, cotangent, contract_first, preferred_element_type=jnp.float32)
    grad_blocks = grad_blocks.astype(jnp.bfloat16).reshape(experts, padded, D)
    grad_blocks, gathered_done = lax.optimization_barrier((grad_blocks, qkv_weight))
    qkv_weight = gathered_done
    grad_arrived = exchange(grad_blocks)

    inputs = tokens.astype(jnp.float32)
    normed, normal_one, inverse_one = norm_forward(inputs, gain_one, bias_one)
    normed_low = normed.astype(jnp.bfloat16)
    qkv = (
        jnp.dot(normed_low, qkv_weight, preferred_element_type=jnp.float32)
        .astype(jnp.bfloat16)
        .reshape(ROWS_DEV, SLOTS, 3 * D)
    )
    allowed = row_masks(lengths, padding)
    mixed, lse = attend_forward(qkv[0], allowed[0])
    mixed_low = mixed.astype(jnp.bfloat16)
    resid = inputs + jnp.dot(mixed_low, out_weight, preferred_element_type=jnp.float32)
    routed_float, normal_two, inverse_two = norm_forward(resid, gain_two, bias_two)
    routed = routed_float.astype(jnp.bfloat16)
    logits = jnp.dot(routed, router_weight, preferred_element_type=jnp.float32)
    probs = jax.nn.softmax(logits, axis=-1)
    gate_first = jnp.sum(probs * first_hot, axis=1)
    gate_second = jnp.sum(probs * second_hot, axis=1)
    buffer = lax.dot_general(picks, routed, contract_first, preferred_element_type=jnp.float32)
    buffer = buffer.astype(jnp.bfloat16).reshape(experts, padded, D)
    slot_gates = jnp.sum(
        pick_first.astype(jnp.float32) * gate_first[:, None]
        + pick_second.astype(jnp.float32) * gate_second[:, None],
        axis=0,
    ).reshape(experts, padded)[:, :capacity]
    high = lax.reduce_precision(slot_gates, 8, 7)
    middle = lax.reduce_precision(slot_gates - high, 8, 7)
    terms = jnp.stack([high, middle, slot_gates - high - middle], axis=1).astype(jnp.bfloat16)
    terms = jnp.pad(terms, ((0, 0), (0, padded - capacity - 3), (0, D - capacity)))
    buffer = lax.dynamic_update_slice(buffer, terms, (0, capacity, 0))
    grad_buffer, result, grad_w_back, grad_w_in, grad_b_in, grad_b_back = run_experts(
        buffer, grad_arrived, w_in[0], w_back[0], b_in, b_back, capacity
    )
    returned = exchange(result.reshape(experts, padded, D)).reshape(experts * padded, D)
    grad_gate_slots = jnp.sum(
        grad_buffer[:, capacity : capacity + 3, :padded].astype(jnp.float32), axis=1
    ).reshape(1, experts * padded)
    grad_buffer = grad_buffer.reshape(experts * padded, D)
    back_total = rep_spread(rep_reduce(grad_w_back, reps), reps).astype(jnp.float32)
    in_total = rep_spread(rep_reduce(grad_w_in, reps), reps).astype(jnp.float32)
    bias_total = rep_total(jnp.concatenate([grad_b_in[0], grad_b_back[0]]).reshape(-1, LANES), reps)
    bias_total = bias_total.reshape(-1)

    grad_out = cotangent.astype(jnp.float32)
    grad_gate_first = jnp.sum(pick_first.astype(jnp.float32) * grad_gate_slots, axis=1)
    grad_gate_second = jnp.sum(pick_second.astype(jnp.float32) * grad_gate_slots, axis=1)
    grad_probs = grad_gate_first[:, None] * first_hot + grad_gate_second[:, None] * second_hot
    grad_logits = (
        probs * (grad_probs - jnp.sum(probs * grad_probs, axis=1, keepdims=True))
    ).astype(jnp.bfloat16)
    grad_router = lax.dot_general(
        routed, grad_logits, contract_first, preferred_element_type=jnp.float32
    )
    grad_routed = jnp.dot(picks, grad_buffer, preferred_element_type=jnp.float32)
    grad_routed = grad_routed + lax.dot_general(
        grad_logits, router_weight, contract_last, preferred_element_type=jnp.float32
    )
    grad_norm_two, grad_gain_two, grad_bias_two = norm_backward(
        grad_routed, normal_two, inverse_two, gain_two
    )
    grad_resid = grad_out + grad_norm_two
    grad_attn = grad_resid.astype(jnp.bfloat16)
    grad_out_weight = lax.dot_general(
        mixed_low, grad_attn, contract_first, preferred_element_type=jnp.float32
    )
    grad_mixed = lax.dot_general(
        grad_attn, out_weight, contract_last, preferred_element_type=jnp.float32
    )
    grad_mixed = grad_mixed.astype(jnp.bfloat16)
    grad_qkv = attend_backward(qkv[0], allowed[0], lse, grad_mixed)
    grad_qkv_weight = lax.dot_general(
        normed_low, grad_qkv, contract_first, preferred_element_type=jnp.float32
    )
    grad_normed = lax.dot_general(
        grad_qkv, qkv_weight, contract_last, preferred_element_type=jnp.float32
    )
    grad_norm_one, grad_gain_one, grad_bias_one = norm_backward(
        grad_normed, normal_one, inverse_one, gain_one
    )
    grad_tokens = grad_resid + grad_norm_one

    picked_first = jnp.dot(pick_first, returned, preferred_element_type=jnp.float32)
    picked_second = jnp.dot(pick_second, returned, preferred_element_type=jnp.float32)
    output = resid + gate_first[:, None] * picked_first + gate_second[:, None] * picked_second

    grad_small = jnp.concatenate(
        [
            grad_router,
            jnp.stack([grad_gain_one, grad_bias_one, grad_gain_two, grad_bias_two], axis=1),
        ],
        axis=1,
    )
    grad_small = jnp.pad(grad_small, ((0, 0), (0, LANES - grad_small.shape[1])))
    sum_qkv, sum_out, sum_small = scatter_sums(
        [
            grad_qkv_weight.astype(jnp.bfloat16),
            grad_out_weight.astype(jnp.bfloat16),
            grad_small.astype(jnp.bfloat16),
        ],
        devices,
        reps,
    )
    vector_sums = sum_small[:, experts : experts + 4]
    hidden = b_in.shape[1]
    return (
        output.astype(jnp.bfloat16),
        grad_tokens,
        vector_sums[:, 0],
        vector_sums[:, 1],
        sum_qkv,
        sum_out,
        vector_sums[:, 2],
        vector_sums[:, 3],
        sum_small[:, :experts],
        in_total[None],
        bias_total[None, :hidden],
        back_total[None],
        bias_total[None, hidden:],
    )


def solution(mesh):
    return jax.shard_map(
        on_device,
        mesh=mesh,
        in_specs=(
            P(("exp", "rep"), None),
            P(("exp", "rep")),
            P(("exp", "rep")),
            P(("exp", "rep"), None),
            P(("exp", "rep"), None),
            P(("exp", "rep")),
            P(("exp", "rep")),
            P(("exp", "rep"), None),
            P("exp", None, None),
            P("exp", None),
            P("exp", None, None),
            P("exp", None),
            P(("exp", "rep"), None),
            P(("exp", "rep"), None),
            P(("exp", "rep")),
            P(("exp", "rep")),
            P(("exp", "rep"), None),
        ),
        out_specs=(
            P(("exp", "rep"), None),
            P(("exp", "rep"), None),
            P(("exp", "rep")),
            P(("exp", "rep")),
            P(("exp", "rep"), None),
            P(("exp", "rep"), None),
            P(("exp", "rep")),
            P(("exp", "rep")),
            P(("exp", "rep"), None),
            P("exp", None, None),
            P("exp", None),
            P("exp", None, None),
            P("exp", None),
        ),
        check_vma=False,
    )
```

```python
import functools

import jax
import jax.numpy as jnp
from jax import lax
from jax.experimental import pallas as pl
from jax.experimental.pallas import tpu as pltpu
from jax.sharding import PartitionSpec as P

D = 768
HEADS = 12
HEAD = 64
SLOTS = 576
ROWS_DEV = 1
TOK_DEV = 576


root_half = 0.7071067811865476
inverse_root_tau = 0.3989422804014327
contract_first = (((0,), (0,)), ((), ()))
contract_last = (((1,), (1,)), ((), ()))


def norm_forward(inputs, gain, offset):
    center = inputs - jnp.mean(inputs, axis=-1, keepdims=True)
    inverse = lax.rsqrt(jnp.mean(center * center, axis=-1, keepdims=True) + 1e-06)
    normal = center * inverse
    return (normal * gain.astype(jnp.float32) + offset.astype(jnp.float32), normal, inverse)


def dispatch_tables(routes, priority, padding, experts, capacity, padded):
    labels = jnp.arange(experts, dtype=jnp.int32)
    first_hot = (routes[:, 0:1] == labels[None, :]).astype(jnp.bfloat16)
    second_hot = (routes[:, 1:2] == labels[None, :]).astype(jnp.bfloat16)
    live = padding[:, None].astype(jnp.bfloat16)
    earlier = (priority[None, :] < priority[:, None]).astype(jnp.bfloat16)
    before_first = jnp.dot(earlier, first_hot * live, preferred_element_type=jnp.float32)
    first_counts = jnp.sum((first_hot * live).astype(jnp.float32), axis=0)
    before_second = (
        jnp.dot(earlier, second_hot * live, preferred_element_type=jnp.float32)
        + first_counts[None, :]
    )
    place_first = jnp.sum(before_first * first_hot, axis=1).astype(jnp.int32)
    place_second = jnp.sum(before_second * second_hot, axis=1).astype(jnp.int32)
    kept_first = (padding == 1) & (place_first < capacity)
    kept_second = (padding == 1) & (place_second < capacity)
    slot_labels = jnp.arange(experts * padded, dtype=jnp.int32)
    slot_first = routes[:, 0] * padded + place_first
    slot_second = routes[:, 1] * padded + place_second
    pick_first = ((slot_first[:, None] == slot_labels[None, :]) & kept_first[:, None]).astype(
        jnp.bfloat16
    )
    pick_second = ((slot_second[:, None] == slot_labels[None, :]) & kept_second[:, None]).astype(
        jnp.bfloat16
    )
    return (first_hot.astype(jnp.float32), second_hot.astype(jnp.float32), pick_first, pick_second)


LANES = 128
MESH_ID = pl.DeviceIdType.MESH


def bit_count(number):
    return number.bit_length() - 1


def flip(position, bit):
    step = 1 << bit
    return position + (1 - 2 * lax.rem(lax.div(position, step), 2)) * step


def coordinates(position, reps):
    return (lax.div(position, reps), lax.rem(position, reps))


def greet(bits, me, reps):
    barrier = pltpu.get_barrier_semaphore()
    for bit in range(bits):
        pl.semaphore_signal(
            barrier, inc=1, device_id=coordinates(flip(me, bit), reps), device_id_type=MESH_ID
        )
    pl.semaphore_wait(barrier, bits)


def lowest_bit(number):
    return (number & -number).bit_length() - 1


def gather_kernel(devices, reps, own_ref, all_ref, send_sem, recv_sem, local_sem):
    bits = bit_count(devices)
    me = lax.axis_index("exp") * reps + lax.axis_index("rep")
    greet(bits, me, reps)
    local = pltpu.make_async_copy(own_ref, all_ref.at[me], local_sem)
    local.start()

    def owner_of(distance):
        found = me
        for bit in range(bits):
            if distance >> bit & 1:
                found = flip(found, bit)
        return found

    def transfer(source_ref, distance, bit):
        owner = owner_of(distance)
        index = distance + (1 << bit)
        return pltpu.make_async_remote_copy(
            src_ref=source_ref,
            dst_ref=all_ref.at[owner],
            send_sem=send_sem.at[index],
            recv_sem=recv_sem.at[index],
            device_id=coordinates(flip(me, bit), reps),
            device_id_type=MESH_ID,
        )

    def arrival(distance):
        owner = owner_of(distance)
        return pltpu.make_async_remote_copy(
            src_ref=all_ref.at[owner],
            dst_ref=all_ref.at[owner],
            send_sem=send_sem.at[distance],
            recv_sem=recv_sem.at[distance],
            device_id=coordinates(flip(me, lowest_bit(distance)), reps),
            device_id_type=MESH_ID,
        )

    sent = []
    for bit in range(bits):
        copy = transfer(own_ref, 0, bit)
        copy.start()
        sent.append(copy)
    order = sorted(range(1, devices), key=lambda d: (bin(d).count("1"), -d))
    last = []
    for distance in order:
        low = lowest_bit(distance)
        if low == 0:
            last.append(distance)
            continue
        arrival(distance).wait_recv()
        for bit in range(low):
            copy = transfer(all_ref.at[owner_of(distance)], distance, bit)
            copy.start()
            sent.append(copy)
    for distance in last:
        arrival(distance).wait_recv()
    for copy in sent:
        copy.wait_send()
    local.wait()


def gather_blocks(block, devices, reps):
    return pl.pallas_call(
        functools.partial(gather_kernel, devices, reps),
        out_shape=jax.ShapeDtypeStruct((devices,) + block.shape, block.dtype),
        in_specs=[pl.BlockSpec(memory_space=pl.ANY)],
        out_specs=pl.BlockSpec(memory_space=pl.ANY),
        scratch_shapes=[
            pltpu.SemaphoreType.DMA((devices,)),
            pltpu.SemaphoreType.DMA((devices,)),
            pltpu.SemaphoreType.DMA,
        ],
        compiler_params=pltpu.CompilerParams(collective_id=0, has_side_effects=True),
        name="gather_dense",
    )(block)


def row_of(column, width):
    count = column.shape[0]
    down = lax.broadcasted_iota(jnp.int32, (count, width), 0)
    across = lax.broadcasted_iota(jnp.int32, (count, width), 1)
    return jnp.sum(jnp.where(down == across, column, 0.0), axis=0, keepdims=True)


def column_of(row, count):
    width = row.shape[1]
    down = lax.broadcasted_iota(jnp.int32, (count, width), 0)
    across = lax.broadcasted_iota(jnp.int32, (count, width), 1)
    return jnp.sum(jnp.where(down == across, row, 0.0), axis=1, keepdims=True)


def three_terms(value):
    high = value.astype(jnp.bfloat16).astype(jnp.float32)
    rest = value - high
    middle = rest.astype(jnp.bfloat16).astype(jnp.float32)
    return (high, middle, rest - middle)


def expert_kernel(
    experts,
    capacity,
    padded,
    block,
    send_ref,
    grad_ref,
    w_in_ref,
    w_back_ref,
    b_in_ref,
    b_back_ref,
    return_ref,
    result_ref,
    half_back_ref,
    half_in_ref,
    slots,
    grads,
    gated,
    weight_in,
    weight_back,
    active,
    grad_pre,
    back_rows,
    result_rows,
    result_total,
    back_total,
    away_back,
    away_in,
    other_back,
    other_in,
    load_sem,
    send_sem,
    recv_sem,
    return_send_sem,
    return_recv_sem,
    result_sem,
    core_send,
    core_recv,
    stage_sem,
):
    mine = lax.axis_index("exp")
    rep = lax.axis_index("rep")
    bits = bit_count(experts)
    groups = experts // 2
    hidden = weight_in.shape[1]
    steps = hidden // block
    lanes = 256 if capacity <= 256 else D
    gate_row = capacity - (padded - 16)

    barrier = pltpu.get_barrier_semaphore()

    def greet_one(step, carry):
        other = lax.rem(mine + step, experts)
        pl.semaphore_signal(barrier, inc=1, device_id=(other, rep), device_id_type=MESH_ID)
        return carry

    lax.fori_loop(1, experts, greet_one, 0)
    core = lax.rem(rep, 2)
    partner = (mine, flip(rep, 0))
    pl.semaphore_signal(barrier, inc=1, device_id=partner, device_id_type=MESH_ID)

    def group_of(index):
        half = lax.div(mine, 2)
        found = half
        for bit in range(bits - 1):
            found = found + lax.rem(lax.div(index, 1 << bit), 2) * (
                (1 - 2 * lax.rem(lax.div(half, 1 << bit), 2)) * (1 << bit)
            )
        return found

    def place(expert):
        return pl.ds(pl.multiple_of(expert * padded, 16), padded)

    def outgoing(expert):
        return pltpu.make_async_remote_copy(
            src_ref=send_ref.at[expert],
            dst_ref=slots.at[place(mine)],
            send_sem=send_sem.at[expert],
            recv_sem=recv_sem.at[mine],
            device_id=(expert, rep),
            device_id_type=MESH_ID,
        )

    def incoming(expert):
        return pltpu.make_async_remote_copy(
            src_ref=send_ref.at[mine],
            dst_ref=slots.at[place(expert)],
            send_sem=send_sem.at[expert],
            recv_sem=recv_sem.at[expert],
            device_id=(expert, rep),
            device_id_type=MESH_ID,
        )

    def going_back(expert):
        return pltpu.make_async_remote_copy(
            src_ref=back_rows.at[place(expert)],
            dst_ref=return_ref.at[mine],
            send_sem=return_send_sem.at[expert],
            recv_sem=return_recv_sem.at[mine],
            device_id=(expert, rep),
            device_id_type=MESH_ID,
        )

    def coming_back(expert):
        return pltpu.make_async_remote_copy(
            src_ref=back_rows.at[place(expert)],
            dst_ref=return_ref.at[expert],
            send_sem=return_send_sem.at[expert],
            recv_sem=return_recv_sem.at[expert],
            device_id=(expert, rep),
            device_id_type=MESH_ID,
        )

    neighbour = flip(mine, 0)
    loads = [
        pltpu.make_async_copy(send_ref.at[mine], slots.at[place(mine)], load_sem.at[0]),
        pltpu.make_async_copy(grad_ref, grads, load_sem.at[1]),
        pltpu.make_async_copy(w_in_ref, weight_in, load_sem.at[2]),
        pltpu.make_async_copy(w_back_ref, weight_back, load_sem.at[3]),
    ]
    for copy in loads:
        copy.start()
    pl.semaphore_wait(barrier, experts)

    def send_group(index):
        pair = group_of(index)
        outgoing(2 * pair).start()
        outgoing(2 * pair + 1).start()

    outgoing(neighbour).start()
    if groups > 2:
        send_group(2)
    if groups > 1:
        send_group(1)
    for copy in loads:
        copy.wait()

    def send_back_group(index):
        pair = group_of(index)
        going_back(2 * pair).start()
        going_back(2 * pair + 1).start()

    def gate_columns(expert):
        tail = slots[pl.ds(pl.multiple_of(expert * padded + padded - 16, 16), 16), :].astype(jnp.float32)
        row = jnp.sum(tail[gate_row : gate_row + 3, :lanes], axis=0, keepdims=True)
        return column_of(row, padded)

    def group_step(index, carry):
        pair = group_of(index)

        @pl.when(index == 0)
        def _():
            incoming(neighbour).wait_recv()

        @pl.when(index > 0)
        def _():
            incoming(2 * pair).wait_recv()
            incoming(2 * pair + 1).wait_recv()

        @pl.when(jnp.logical_and(index >= 1, index + 2 < groups))
        def _():
            send_group(index + 2)

        @pl.when(index == 1)
        def _():
            going_back(neighbour).start()

        @pl.when(index > 1)
        def _():
            send_back_group(index - 1)

        here = pl.ds(pl.multiple_of(pair * 2 * padded, 16), 2 * padded)
        for side in range(2):
            spot = place(2 * pair + side)
            gate = gate_columns(2 * pair + side)
            gated[spot, :] = (gate * grads[spot, :].astype(jnp.float32)).astype(jnp.bfloat16)

        def hidden_step(step, inner):
            columns = pl.ds(pl.multiple_of(step * block, block), block)
            pre = (
                jnp.dot(slots[here, :], weight_in[:, columns], preferred_element_type=jnp.float32)
                + b_in_ref[:, columns]
            )
            grad_active = lax.dot_general(
                gated[here, :],
                weight_back[columns, :],
                contract_last,
                preferred_element_type=jnp.float32,
            )
            cumulative = 0.5 * (1.0 + lax.erf(pre * root_half))
            slope = cumulative + pre * inverse_root_tau * jnp.exp(-0.5 * pre * pre)
            active_low = (pre * cumulative).astype(jnp.bfloat16)
            grad_low = (grad_active * slope).astype(jnp.bfloat16)
            active[here, columns] = active_low
            grad_pre[here, columns] = grad_low
            result_part = jnp.dot(
                active_low, weight_back[columns, :], preferred_element_type=jnp.float32
            )
            back_part = lax.dot_general(
                grad_low, weight_in[:, columns], contract_last, preferred_element_type=jnp.float32
            )

            @pl.when(step == 0)
            def _():
                result_total[...] = result_part
                back_total[...] = back_part

            @pl.when(step > 0)
            def _():
                result_total[...] += result_part
                back_total[...] += back_part

            return inner

        lax.fori_loop(0, steps, hidden_step, 0)
        for side in range(2):
            expert = 2 * pair + side
            span = slice(side * padded, (side + 1) * padded)
            spot = place(expert)
            result_low = (result_total[span, :] + b_back_ref[...]).astype(jnp.bfloat16)
            result_rows[spot, :] = result_low
            grad_gate = jnp.sum(
                grads[spot, :].astype(jnp.float32) * result_low.astype(jnp.float32),
                axis=1,
                keepdims=True,
            )
            gate_line = row_of(
                jnp.where(
                    lax.broadcasted_iota(jnp.int32, (padded, 1), 0) < capacity, grad_gate, 0.0
                ),
                lanes,
            )
            if lanes < D:
                gate_line = jnp.concatenate(
                    [gate_line, jnp.zeros((1, D - lanes), jnp.float32)], axis=1
                )
            high, middle, lowest = three_terms(gate_line)
            row = lax.broadcasted_iota(jnp.int32, (padded, D), 0)
            value = back_total[span, :]
            value = jnp.where(row == capacity, high, value)
            value = jnp.where(row == capacity + 1, middle, value)
            value = jnp.where(row == capacity + 2, lowest, value)
            back_rows[spot, :] = value.astype(jnp.bfloat16)
        return carry

    lax.fori_loop(0, groups, group_step, 0)
    if groups > 1:
        send_back_group(groups - 1)
    else:
        going_back(neighbour).start()
    own_back = pltpu.make_async_copy(back_rows.at[place(mine)], return_ref.at[mine], load_sem.at[0])
    own_back.start()
    results = pltpu.make_async_copy(result_rows, result_ref, result_sem)
    results.start()

    piece = away_in.shape[2]
    half = away_in.shape[0]
    bias_back = jnp.sum(gated[...].astype(jnp.float32), axis=0, keepdims=True)

    def sums_of(number):
        columns = pl.ds(pl.multiple_of(number * piece, LANES), piece)
        back = lax.dot_general(
            active[:, columns], gated[...], contract_first, preferred_element_type=jnp.float32
        )
        inward = lax.dot_general(
            slots[...], grad_pre[:, columns], contract_first, preferred_element_type=jnp.float32
        )
        bias_in = jnp.sum(grad_pre[:, columns].astype(jnp.float32), axis=0, keepdims=True)
        if piece < D:
            bias_in = jnp.concatenate([bias_in, jnp.zeros((1, D - piece), jnp.float32)], axis=1)
        row = lax.broadcasted_iota(jnp.int32, (16, D), 0)
        extra = jnp.where(row == 0, bias_in, jnp.where(row == 1, bias_back, 0.0))
        return (back, inward, extra)

    def core_copies(index):
        return [
            pltpu.make_async_remote_copy(
                src_ref=source.at[index],
                dst_ref=target.at[index],
                send_sem=core_send.at[kind, index],
                recv_sem=core_recv.at[kind, index],
                device_id=partner,
                device_id_type=MESH_ID,
            )
            for kind, (source, target) in enumerate(
                ((away_back, other_back), (away_in, other_in))
            )
        ]

    def away_step(index, carry):
        back, inward, extra = sums_of(2 * index + 1 - core)
        away_back[index, :piece, :] = back.astype(jnp.bfloat16)
        away_back[index, piece:, :] = extra.astype(jnp.bfloat16)
        away_in[index] = inward.astype(jnp.bfloat16)
        for copy in core_copies(index):
            copy.start()
        return carry

    def kept_copies(index):
        return (
            pltpu.make_async_copy(other_back.at[index], half_back_ref.at[index], stage_sem.at[0, index]),
            pltpu.make_async_copy(other_in.at[index], half_in_ref.at[index], stage_sem.at[1, index]),
        )

    def kept_step(index, carry):
        back, inward, extra = sums_of(2 * index + core)
        for copy in core_copies(index):
            copy.wait_recv()
        other_back[index, :piece, :] = (
            back + other_back[index, :piece, :].astype(jnp.float32)
        ).astype(jnp.bfloat16)
        other_back[index, piece:, :] = (
            extra + other_back[index, piece:, :].astype(jnp.float32)
        ).astype(jnp.bfloat16)
        other_in[index] = (inward + other_in[index].astype(jnp.float32)).astype(jnp.bfloat16)
        for copy in kept_copies(index):
            copy.start()
        return carry

    lax.fori_loop(0, half, away_step, 0)
    lax.fori_loop(0, half, kept_step, 0)
    for index in range(half):
        for copy in kept_copies(index):
            copy.wait()
        for copy in core_copies(index):
            copy.wait_send()
    own_back.wait()
    results.wait()

    def finish(step, carry):
        other = lax.rem(mine + step, experts)
        outgoing(other).wait_send()
        going_back(other).wait_send()
        coming_back(other).wait_recv()
        return carry

    lax.fori_loop(1, experts, finish, 0)


def run_experts(buffer, grads, w_in, w_back, b_in, b_back, capacity, reps):
    experts, padded = (buffer.shape[0], buffer.shape[1])
    hidden = w_in.shape[1]
    block = 512
    rows = experts * padded
    half = reps // 2
    piece = hidden // reps
    low = jnp.bfloat16
    anywhere = pl.BlockSpec(memory_space=pl.ANY)
    inside = pl.BlockSpec(memory_space=pltpu.VMEM)
    return pl.pallas_call(
        functools.partial(expert_kernel, experts, capacity, padded, block),
        out_shape=[
            jax.ShapeDtypeStruct((experts, padded, D), low),
            jax.ShapeDtypeStruct((rows, D), low),
            jax.ShapeDtypeStruct((half, piece + 16, D), low),
            jax.ShapeDtypeStruct((half, D, piece), low),
        ],
        in_specs=[anywhere, anywhere, anywhere, anywhere, inside, inside],
        out_specs=[anywhere, anywhere, anywhere, anywhere],
        scratch_shapes=[
            pltpu.VMEM((rows, D), low),
            pltpu.VMEM((rows, D), low),
            pltpu.VMEM((rows, D), low),
            pltpu.VMEM((D, hidden), low),
            pltpu.VMEM((hidden, D), low),
            pltpu.VMEM((rows, hidden), low),
            pltpu.VMEM((rows, hidden), low),
            pltpu.VMEM((rows, D), low),
            pltpu.VMEM((rows, D), low),
            pltpu.VMEM((2 * padded, D), jnp.float32),
            pltpu.VMEM((2 * padded, D), jnp.float32),
            pltpu.VMEM((half, piece + 16, D), low),
            pltpu.VMEM((half, D, piece), low),
            pltpu.VMEM((half, piece + 16, D), low),
            pltpu.VMEM((half, D, piece), low),
            pltpu.SemaphoreType.DMA((4,)),
            pltpu.SemaphoreType.DMA((experts,)),
            pltpu.SemaphoreType.DMA((experts,)),
            pltpu.SemaphoreType.DMA((experts,)),
            pltpu.SemaphoreType.DMA((experts,)),
            pltpu.SemaphoreType.DMA,
            pltpu.SemaphoreType.DMA((2, half)),
            pltpu.SemaphoreType.DMA((2, half)),
            pltpu.SemaphoreType.DMA((2, half)),
        ],
        compiler_params=pltpu.CompilerParams(
            collective_id=2, has_side_effects=True, vmem_limit_bytes=60 * 1024 * 1024
        ),
        cost_estimate=pl.CostEstimate(
            flops=12 * rows * D * hidden, bytes_accessed=40 << 20, transcendentals=2 * rows * hidden
        ),
        name="experts",
    )(buffer, grads.reshape(rows, D), w_in, w_back, b_in.astype(jnp.float32), b_back.astype(jnp.float32))


def attend_kernel(segment_col, segment_row, live_row, query_ref, keys_ref, values_ref, mixed_ref, bias):
    @pl.when(pl.program_id(0) == 0)
    def _():
        row = lax.broadcasted_iota(jnp.int32, (SLOTS, SLOTS), 0)
        column = lax.broadcasted_iota(jnp.int32, (SLOTS, SLOTS), 1)
        seen = (segment_col[...] == segment_row[...]) & ((live_row[...] == 1) | (row == column))
        bias[...] = jnp.where(seen, 0.0, -1e30)

    for side in range(2):
        lanes = slice(side * HEAD, (side + 1) * HEAD)
        scores = lax.dot_general(
            query_ref[:, lanes], keys_ref[:, lanes], contract_last, preferred_element_type=jnp.float32
        )
        scores = scores * HEAD ** (-0.5) + bias[...]
        expo = jnp.exp(scores - jnp.max(scores, axis=1, keepdims=True))
        total = jnp.sum(expo, axis=1, keepdims=True)
        probs = (expo * (1.0 / total)).astype(jnp.bfloat16)
        mixed = jnp.dot(probs, values_ref[:, lanes], preferred_element_type=jnp.float32)
        mixed_ref[:, lanes] = mixed.astype(jnp.bfloat16)


def attend(qkv, segments, live):
    pairs = HEADS // 2
    return pl.pallas_call(
        attend_kernel,
        grid=(pairs,),
        out_shape=jax.ShapeDtypeStruct((SLOTS, D), jnp.bfloat16),
        in_specs=[
            pl.BlockSpec((SLOTS, 1), lambda i: (0, 0)),
            pl.BlockSpec((1, SLOTS), lambda i: (0, 0)),
            pl.BlockSpec((1, SLOTS), lambda i: (0, 0)),
            pl.BlockSpec((SLOTS, 2 * HEAD), lambda i: (0, i)),
            pl.BlockSpec((SLOTS, 2 * HEAD), lambda i: (0, pairs + i)),
            pl.BlockSpec((SLOTS, 2 * HEAD), lambda i: (0, 2 * pairs + i)),
        ],
        out_specs=pl.BlockSpec((SLOTS, 2 * HEAD), lambda i: (0, i)),
        scratch_shapes=[pltpu.VMEM((SLOTS, SLOTS), jnp.float32)],
        cost_estimate=pl.CostEstimate(
            flops=16 * HEADS * SLOTS * SLOTS * HEAD, bytes_accessed=4 << 20, transcendentals=HEADS * SLOTS * SLOTS
        ),
        name="attend",
    )(segments.reshape(SLOTS, 1), segments.reshape(1, SLOTS), live.reshape(1, SLOTS), qkv, qkv, qkv)


BAND = 48


def fold_rows(values):
    return jnp.sum(values.reshape(BAND // 8, 8, values.shape[1]), axis=0)


def backward_kernel(
    experts,
    reps,
    chunks,
    summed,
    back_ref,
    result_ref,
    first_ref,
    second_ref,
    terms_ref,
    probs_ref,
    routes_ref,
    cotangent_ref,
    resid_ref,
    tokens_ref,
    normed_ref,
    routed_ref,
    qkv_ref,
    mixed_ref,
    weights_ref,
    vectors_ref,
    segment_col,
    segment_row,
    live_col,
    half_back_ref,
    half_in_ref,
    output_ref,
    grad_tokens_ref,
    sum_qkv_ref,
    sum_out_ref,
    sum_small_ref,
    total_back_ref,
    total_in_ref,
    all_back_ref,
    all_in_ref,
    *refs,
):
    devices = experts * reps
    bits = bit_count(devices)
    half = reps // 2
    mine = lax.axis_index("exp")
    rep = lax.axis_index("rep")
    me = mine * reps + rep
    core = lax.rem(rep, 2)
    along = lax.div(rep, 2)
    (
        back,
        first,
        second,
        cotangent,
        resid,
        tokens,
        normed,
        routed,
        qkv,
        mixed,
        weights,
        returned,
        bias,
        wide,
        tall,
        grad_resid,
        grad_attn,
        grad_mixed,
        grad_qkv,
        grad_logits,
        own_back,
        own_in,
        other_back,
        other_in,
        cast_back,
        cast_in,
        full_back,
        full_in,
    ) = refs[:28]
    refs = refs[28:]
    count = len(chunks) if summed else 0
    parts, refs = (refs[:count], refs[count:])
    recvs, refs = ([refs[c * bits : (c + 1) * bits] for c in range(count)], refs[count * bits :])
    (
        load_sem,
        result_send,
        result_recv,
        dense_send,
        dense_recv,
        half_send,
        half_recv,
        all_send,
        all_recv,
        cast_sem,
    ) = refs
    padded = result_ref.shape[0] // experts
    piece = half_in_ref.shape[2]

    barrier = pltpu.get_barrier_semaphore()

    def greet_expert(step, carry):
        other = lax.rem(mine + step, experts)
        pl.semaphore_signal(barrier, inc=1, device_id=(other, rep), device_id_type=MESH_ID)
        return carry

    def greet_rep(step, carry):
        other = lax.rem(rep + step, reps)
        pl.semaphore_signal(barrier, inc=1, device_id=(mine, other), device_id_type=MESH_ID)
        return carry

    lax.fori_loop(1, experts, greet_expert, 0)
    lax.fori_loop(1, reps, greet_rep, 0)

    sources = [
        (back_ref, back),
        (first_ref, first),
        (second_ref, second),
        (routed_ref, routed),
        (weights_ref, weights),
        (resid_ref, resid),
        (cotangent_ref, cotangent),
        (mixed_ref, mixed),
        (qkv_ref, qkv),
        (normed_ref, normed),
        (tokens_ref, tokens),
        (half_back_ref.at[along], own_back),
        (half_in_ref.at[along], own_in),
    ]
    loads = [
        pltpu.make_async_copy(source, target, load_sem.at[i])
        for i, (source, target) in enumerate(sources)
    ]
    for copy in loads:
        copy.start()
    pl.semaphore_wait(barrier, experts - 1 + reps - 1)

    def half_copies(step):
        other = lax.rem(along + step, half)
        came = lax.rem(along + half - step, half)
        device = (mine, 2 * other + core)
        return [
            pltpu.make_async_remote_copy(
                src_ref=source.at[other],
                dst_ref=target.at[step - 1],
                send_sem=half_send.at[kind, step - 1],
                recv_sem=half_recv.at[kind, step - 1],
                device_id=device,
                device_id_type=MESH_ID,
            )
            for kind, (source, target) in enumerate(
                ((half_back_ref, other_back), (half_in_ref, other_in))
            )
        ]

    half_moves = [half_copies(step) for step in range(1, half)]
    for kind in range(2):
        for moves in half_moves:
            moves[kind].start()

    def place(expert):
        return pl.ds(pl.multiple_of(expert * padded, 16), padded)

    def result_copy(step):
        other = lax.rem(mine + step, experts)
        came = lax.rem(mine + experts - step, experts)
        return pltpu.make_async_remote_copy(
            src_ref=result_ref.at[place(other)],
            dst_ref=returned.at[place(mine)],
            send_sem=result_send.at[step],
            recv_sem=result_recv.at[step],
            device_id=(other, rep),
            device_id_type=MESH_ID,
        )

    def start_result(step, carry):
        result_copy(step).start()
        return carry

    own_result = pltpu.make_async_copy(
        result_ref.at[place(mine)], returned.at[place(mine)], result_send.at[0]
    )
    own_result.start()
    lax.fori_loop(1, experts, start_result, 0)

    row = lax.broadcasted_iota(jnp.int32, (SLOTS, SLOTS), 0)
    column = lax.broadcasted_iota(jnp.int32, (SLOTS, SLOTS), 1)
    seen = (segment_col[...] == segment_row[...]) & ((live_col[...] == 1) | (row == column))
    bias[...] = jnp.where(seen, 0.0, -1e30)

    for copy in loads[:5]:
        copy.wait()
    tall[...] = jnp.dot(first[...] + second[...], back[...], preferred_element_type=jnp.float32)
    gates_back = [
        jnp.sum(
            lax.dot_general(
                pick[...], terms_ref[...], contract_last, preferred_element_type=jnp.float32
            ),
            axis=1,
            keepdims=True,
        )
        for pick in (first, second)
    ]
    lane = lax.broadcasted_iota(jnp.int32, (SLOTS, LANES), 1)
    hots = [(lane == routes_ref[:, k : k + 1]).astype(jnp.float32) for k in range(2)]
    grad_probs = gates_back[0] * hots[0] + gates_back[1] * hots[1]
    probs = probs_ref[...]
    grad_logits[...] = (
        probs * (grad_probs - jnp.sum(probs * grad_probs, axis=1, keepdims=True))
    ).astype(jnp.bfloat16)
    tall[...] += lax.dot_general(
        grad_logits[...], weights[:, 4 * D :], contract_last, preferred_element_type=jnp.float32
    )
    for copy in loads[5:]:
        copy.wait()

    def band(step):
        return pl.ds(pl.multiple_of(step * BAND, 16), BAND)

    def norm_back(inputs, grad, gain):
        center = inputs - jnp.mean(inputs, axis=1, keepdims=True)
        inverse = lax.rsqrt(jnp.mean(center * center, axis=1, keepdims=True) + 1e-06)
        normal = center * inverse
        scaled = grad * gain
        grad_in = inverse * (
            scaled
            - jnp.mean(scaled, axis=1, keepdims=True)
            - normal * jnp.mean(scaled * normal, axis=1, keepdims=True)
        )
        return (grad_in, fold_rows(grad * normal), fold_rows(grad))

    zero = jnp.zeros((8, D), jnp.float32)

    def second_norm(step, carry):
        here = band(step)
        grad_in, grad_gain, grad_bias = norm_back(
            resid[here, :], tall[here, :], vectors_ref[2:3, :]
        )
        total = cotangent[here, :].astype(jnp.float32) + grad_in
        grad_resid[here, :] = total
        grad_attn[here, :] = total.astype(jnp.bfloat16)
        return (carry[0] + grad_gain, carry[1] + grad_bias)

    gain_two, bias_two = lax.fori_loop(0, SLOTS // BAND, second_norm, (zero, zero))

    plan = [0] + [bit_count(reps)] + list(range(bits - 1, bit_count(reps), -1))
    plan = plan + list(range(bit_count(reps) - 1, 0, -1))
    my_bit = [lax.rem(lax.div(me, 1 << bit), 2) for bit in range(bits)]
    rows = parts[0].shape[3] if summed else 0
    stride = experts + bits - 1
    outs = (sum_qkv_ref, sum_out_ref, sum_small_ref)

    def fill(c):
        width = chunks[c][2]

        def one(block, carry):
            owner = lax.div(block, reps)
            inner = lax.rem(block, reps)
            parts[c][owner, lax.div(inner, 2), lax.rem(inner, 2)] = wide[
                pl.ds(pl.multiple_of(block * rows, rows), rows), :width
            ].astype(jnp.bfloat16)
            return carry

        lax.fori_loop(0, devices, one, 0)

    def first_copy(c, expert):
        spot = lax.rem(expert, 2) * (devices // 4) + lax.div(expert, 2) * half
        return pltpu.make_async_remote_copy(
            src_ref=parts[c].at[expert, :, 1 - core],
            dst_ref=recvs[c][0].at[pl.ds(spot, half)],
            send_sem=dense_send.at[c * stride + expert],
            recv_sem=dense_recv.at[c * stride + expert],
            device_id=(mine, flip(rep, 0)),
            device_id_type=MESH_ID,
        )

    def later_copy(c, phase):
        size = devices >> (phase + 1)
        index = c * stride + experts + phase - 1
        return pltpu.make_async_remote_copy(
            src_ref=recvs[c][phase - 1].at[pl.ds((1 - my_bit[plan[phase]]) * size, size)],
            dst_ref=recvs[c][phase],
            send_sem=dense_send.at[index],
            recv_sem=dense_recv.at[index],
            device_id=coordinates(flip(me, plan[phase]), reps),
            device_id_type=MESH_ID,
        )

    def send_chunk(c):
        if not summed:
            array, start, width = chunks[c]
            pltpu.sync_copy(wide.at[:, :width], outs[array].at[:, pl.ds(start, width)])
            return
        fill(c)

        def one(expert, carry):
            first_copy(c, expert).start()
            return carry

        lax.fori_loop(0, experts, one, 0)

    def absorb(c, phase):
        if not summed:
            return
        size = devices >> (phase + 1)
        into = recvs[c][phase]
        if phase == 0:

            def arrived(expert, carry):
                first_copy(c, expert).wait_recv()
                return carry

            lax.fori_loop(0, experts, arrived, 0)

            def held(i):
                side = lax.div(i, devices // 4)
                rest = lax.rem(i, devices // 4)
                return parts[c][2 * lax.div(rest, half) + side, lax.rem(rest, half), core]
        else:
            later_copy(c, phase).wait_recv()
            base = my_bit[plan[phase]] * size

            def held(i):
                return recvs[c][phase - 1][base + i]

        if phase == bits - 1:
            array, start, width = chunks[c]
            outs[array][:, pl.ds(start, width)] = into[0].astype(jnp.float32) + held(0).astype(
                jnp.float32
            )
            return

        def one(i, carry):
            into[i] = (into[i].astype(jnp.float32) + held(i).astype(jnp.float32)).astype(
                jnp.bfloat16
            )
            return carry

        lax.fori_loop(0, size, one, 0)
        later_copy(c, phase + 1).start()

    out_chunk = [c for c in range(len(chunks)) if chunks[c][0] == 1][0]
    small_chunk = [c for c in range(len(chunks)) if chunks[c][0] == 2][0]
    qkv_chunks = [c for c in range(len(chunks)) if chunks[c][0] == 0]
    wide[...] = lax.dot_general(
        mixed[...], grad_attn[...], contract_first, preferred_element_type=jnp.float32
    )
    send_chunk(out_chunk)
    grad_mixed[...] = lax.dot_general(
        grad_attn[...], weights[:, 3 * D : 4 * D], contract_last, preferred_element_type=jnp.float32
    ).astype(jnp.bfloat16)

    def attend_back(pair, carry):
        base = pl.multiple_of(pair * 2 * HEAD, 2 * HEAD)
        queries = qkv[:, pl.ds(base, 2 * HEAD)]
        keys = qkv[:, pl.ds(base + D, 2 * HEAD)]
        values = qkv[:, pl.ds(base + 2 * D, 2 * HEAD)]
        grads = grad_mixed[:, pl.ds(base, 2 * HEAD)]
        done = []
        for side in range(2):
            lanes = slice(side * HEAD, (side + 1) * HEAD)
            query, key, value, grad = (
                queries[:, lanes],
                keys[:, lanes],
                values[:, lanes],
                grads[:, lanes],
            )
            scores = lax.dot_general(key, query, contract_last, preferred_element_type=jnp.float32)
            scores = scores * HEAD ** (-0.5) + bias[...]
            expo = jnp.exp(scores - jnp.max(scores, axis=0, keepdims=True))
            weight = expo * (1.0 / jnp.sum(expo, axis=0, keepdims=True))
            grad_weight = lax.dot_general(
                value, grad, contract_last, preferred_element_type=jnp.float32
            )
            product = weight * grad_weight
            delta = jnp.sum(product, axis=0, keepdims=True)
            grad_scores = (product - weight * delta).astype(jnp.bfloat16)
            grad_value = jnp.dot(
                weight.astype(jnp.bfloat16), grad, preferred_element_type=jnp.float32
            )
            grad_key = jnp.dot(grad_scores, query, preferred_element_type=jnp.float32)
            grad_query = lax.dot_general(
                grad_scores, key, contract_first, preferred_element_type=jnp.float32
            )
            done.append(
                (grad_query * HEAD ** (-0.5), grad_key * HEAD ** (-0.5), grad_value)
            )
        for kind in range(3):
            grad_qkv[:, pl.ds(base + kind * D, 2 * HEAD)] = jnp.concatenate(
                [done[0][kind], done[1][kind]], axis=1
            ).astype(jnp.bfloat16)
        return carry

    lax.fori_loop(0, HEADS // 2, attend_back, 0)

    arrays = ((own_back, other_back, all_back_ref), (own_in, other_in, all_in_ref))

    def complete(kind):
        own, others, everywhere = arrays[kind]
        for step in range(1, half):
            half_moves[step - 1][kind].wait_recv()
        size = 16
        steps = own.shape[0] // size

        def one(step, carry):
            here = pl.ds(pl.multiple_of(step * size, 16), size)
            total = own[here, :].astype(jnp.float32)
            for step in range(1, half):
                total = total + others[step - 1, here, :].astype(jnp.float32)
            own[here, :] = total.astype(jnp.bfloat16)
            return carry

        lax.fori_loop(0, steps, one, 0)
        local = pltpu.make_async_copy(own, everywhere.at[rep], cast_sem.at[4 + kind])
        local.start()
        moves = []
        for step in range(1, half):
            other = lax.rem(along + step, half)
            moves.append(spread(kind, own, rep, (mine, 2 * other + core), step))
        moves.append(spread(kind, own, rep, (mine, flip(rep, 0)), 0))
        for move in moves:
            move.start()
        return (local, moves)

    def spread(kind, source, owner, device, step):
        return pltpu.make_async_remote_copy(
            src_ref=source,
            dst_ref=arrays[kind][2].at[owner],
            send_sem=all_send.at[kind, step],
            recv_sem=all_recv.at[kind, step],
            device_id=device,
            device_id_type=MESH_ID,
        )

    finals = [complete(0)]
    for c in qkv_chunks:
        start = chunks[c][1]
        wide[...] = lax.dot_general(
            normed[...], grad_qkv[:, start : start + D], contract_first, preferred_element_type=jnp.float32
        )
        send_chunk(c)
    absorb(out_chunk, 0)
    finals.append(complete(1))
    tall[...] = lax.dot_general(
        grad_qkv[...], weights[:, : 3 * D], contract_last, preferred_element_type=jnp.float32
    )

    def first_norm(step, carry):
        here = band(step)
        grad_in, grad_gain, grad_bias = norm_back(
            tokens[here, :].astype(jnp.float32), tall[here, :], vectors_ref[0:1, :]
        )
        grad_tokens_ref[here, :] = grad_resid[here, :] + grad_in
        return (carry[0] + grad_gain, carry[1] + grad_bias)

    gain_one, bias_one = lax.fori_loop(0, SLOTS // BAND, first_norm, (zero, zero))
    wide[:, :LANES] = lax.dot_general(
        routed[...], grad_logits[...], contract_first, preferred_element_type=jnp.float32
    )
    lines = [jnp.sum(v, axis=0, keepdims=True) for v in (gain_one, bias_one, gain_two, bias_two)]
    lane = lax.broadcasted_iota(jnp.int32, (LANES, LANES), 1)
    for part in range(D // LANES):
        span = slice(part * LANES, (part + 1) * LANES)
        block = wide[span, :LANES]
        for k in range(4):
            block = jnp.where(lane == experts + k, column_of(lines[k][:, span], LANES), block)
        wide[span, :LANES] = block
    send_chunk(small_chunk)

    order = [out_chunk] + qkv_chunks + [small_chunk]
    for step in range(bits + len(order) - 1):
        for position, c in enumerate(order):
            phase = step - position
            if 0 <= phase < bits and not (c == out_chunk and phase == 0):
                absorb(c, phase)

    own_result.wait()

    def result_arrived(step, carry):
        result_copy(step).wait_recv()
        result_copy(step).wait_send()
        return carry

    lax.fori_loop(1, experts, result_arrived, 0)
    lane = lax.broadcasted_iota(jnp.int32, (SLOTS, LANES), 1)
    probs = probs_ref[...]
    gates = [
        jnp.sum(jnp.where(lane == routes_ref[:, k : k + 1], probs, 0.0), axis=1, keepdims=True)
        for k in range(2)
    ]
    tall[...] = resid[...] + gates[0] * jnp.dot(
        first[...], returned[...], preferred_element_type=jnp.float32
    )
    output_ref[...] = (
        tall[...]
        + gates[1] * jnp.dot(second[...], returned[...], preferred_element_type=jnp.float32)
    ).astype(jnp.bfloat16)

    forwards = []
    pending = [None, None]

    def convert(owner, first_wait):
        for kind in range(2):
            staged, full = ((cast_back, full_back), (cast_in, full_in))[kind]
            size = staged.shape[0]
            whole = (piece, D)[kind]
            for block in range(whole // size):
                span = pl.ds(block * size, size)
                load = pltpu.make_async_copy(
                    arrays[kind][2].at[owner, span, :], staged, cast_sem.at[kind]
                )
                load.start()
                load.wait()
                if pending[kind] is not None:
                    pending[kind].wait()

                def one(step, carry):
                    here = pl.ds(pl.multiple_of(step * 48, 16), 48)
                    full[here, :] = staged[here, :].astype(jnp.float32)
                    return carry

                lax.fori_loop(0, size // 48, one, 0)
                if kind == 0:
                    target = total_back_ref.at[
                        pl.ds(pl.multiple_of(owner * piece + block * size, 16), size), :
                    ]
                else:
                    target = total_in_ref.at[span, pl.ds(pl.multiple_of(owner * piece, LANES), piece)]
                store = pltpu.make_async_copy(full, target, cast_sem.at[2 + kind])
                store.start()
                pending[kind] = store

    for local, _ in finals:
        local.wait()
    convert(rep, True)
    partner = flip(rep, 0)
    for kind in range(2):
        spread(kind, arrays[kind][2].at[partner], partner, (mine, partner), 0).wait_recv()
    convert(partner, True)
    for step in range(1, half):
        came = lax.rem(along + half - step, half)
        owner = 2 * came + core
        for kind in range(2):
            spread(kind, arrays[kind][2].at[owner], owner, (mine, owner), step).wait_recv()
            forward = spread(
                kind, arrays[kind][2].at[owner], owner, (mine, partner), half + step - 1
            )
            forward.start()
            forwards.append(forward)
        convert(owner, True)
    for step in range(1, half):
        came = lax.rem(along + half - step, half)
        owner = 2 * came + 1 - core
        for kind in range(2):
            spread(
                kind, arrays[kind][2].at[owner], owner, (mine, partner), half + step - 1
            ).wait_recv()
        convert(owner, True)
    for copy in pending:
        copy.wait()
    for copy in forwards:
        copy.wait_send()
    for _, moves in finals:
        for move in moves:
            move.wait_send()
    for moves in half_moves:
        for move in moves:
            move.wait_send()

    def dense_sent(c):
        def one(expert, carry):
            first_copy(c, expert).wait_send()
            return carry

        lax.fori_loop(0, experts, one, 0)
        for phase in range(1, bits):
            later_copy(c, phase).wait_send()

    for c in range(count):
        dense_sent(c)


def run_backward(operands, experts, reps, rows):
    devices = experts * reps
    bits = bit_count(devices)
    half = reps // 2
    (
        back,
        result,
        first,
        second,
        terms,
        probs,
        routes,
        cotangent,
        resid,
        tokens,
        normed,
        routed,
        qkv,
        mixed,
        weights,
        vectors,
        segment_col,
        segment_row,
        live_col,
        half_back,
        half_in,
    ) = operands
    low = jnp.bfloat16
    full = jnp.float32
    piece = half_in.shape[2]
    tail_rows = half_back.shape[1]
    chunks = [(0, k * D, D) for k in range(3)] + [(1, 0, D), (2, 0, LANES)]
    anywhere = pl.BlockSpec(memory_space=pl.ANY)
    inside = pl.BlockSpec(memory_space=pltpu.VMEM)
    slots = result.shape[0]
    scratch = [
        pltpu.VMEM((slots, D), low),
        pltpu.VMEM((SLOTS, slots), low),
        pltpu.VMEM((SLOTS, slots), low),
        pltpu.VMEM((SLOTS, D), low),
        pltpu.VMEM((SLOTS, D), full),
        pltpu.VMEM((SLOTS, D), low),
        pltpu.VMEM((SLOTS, D), low),
        pltpu.VMEM((SLOTS, D), low),
        pltpu.VMEM((SLOTS, 3 * D), low),
        pltpu.VMEM((SLOTS, D), low),
        pltpu.VMEM(weights.shape, low),
        pltpu.VMEM((slots, D), low),
        pltpu.VMEM((SLOTS, SLOTS), full),
        pltpu.VMEM((D, D), full),
        pltpu.VMEM((SLOTS, D), full),
        pltpu.VMEM((SLOTS, D), full),
        pltpu.VMEM((SLOTS, D), low),
        pltpu.VMEM((SLOTS, D), low),
        pltpu.VMEM((SLOTS, 3 * D), low),
        pltpu.VMEM((SLOTS, LANES), low),
        pltpu.VMEM((tail_rows, D), low),
        pltpu.VMEM((D, piece), low),
        pltpu.VMEM((half - 1, tail_rows, D), low),
        pltpu.VMEM((half - 1, D, piece), low),
        pltpu.VMEM((piece // 2, D), low),
        pltpu.VMEM((D // 2, piece), low),
        pltpu.VMEM((piece // 2, D), full),
        pltpu.VMEM((D // 2, piece), full),
    ]
    summed = rows % 8 == 0
    for _, _, width in chunks if summed else ():
        scratch.append(pltpu.VMEM((experts, half, 2, rows, width), low))
    for _, _, width in chunks if summed else ():
        for phase in range(bits):
            scratch.append(pltpu.VMEM((devices >> (phase + 1), rows, width), low))
    dense = len(chunks) * (experts + bits - 1)
    scratch = scratch + [
        pltpu.SemaphoreType.DMA((13,)),
        pltpu.SemaphoreType.DMA((experts,)),
        pltpu.SemaphoreType.DMA((experts,)),
        pltpu.SemaphoreType.DMA((dense,)),
        pltpu.SemaphoreType.DMA((dense,)),
        pltpu.SemaphoreType.DMA((2, half - 1)),
        pltpu.SemaphoreType.DMA((2, half - 1)),
        pltpu.SemaphoreType.DMA((2, reps)),
        pltpu.SemaphoreType.DMA((2, reps)),
        pltpu.SemaphoreType.DMA((6,)),
    ]
    hidden = piece * reps
    call = pl.pallas_call(
        functools.partial(backward_kernel, experts, reps, chunks, summed),
        out_shape=[
            jax.ShapeDtypeStruct((SLOTS, D), low),
            jax.ShapeDtypeStruct((SLOTS, D), full),
            jax.ShapeDtypeStruct((rows if summed else D, 3 * D), full),
            jax.ShapeDtypeStruct((rows if summed else D, D), full),
            jax.ShapeDtypeStruct((rows if summed else D, LANES), full),
            jax.ShapeDtypeStruct((hidden, D), full),
            jax.ShapeDtypeStruct((D, hidden), full),
            jax.ShapeDtypeStruct((reps, tail_rows, D), low),
            jax.ShapeDtypeStruct((reps, D, piece), low),
        ],
        in_specs=[anywhere] * 4
        + [inside] * 3
        + [anywhere] * 8
        + [inside] * 4
        + [anywhere] * 2,
        out_specs=[inside] * 2 + [inside if summed else anywhere] * 3 + [anywhere] * 4,
        scratch_shapes=scratch,
        compiler_params=pltpu.CompilerParams(
            collective_id=1, has_side_effects=True, vmem_limit_bytes=63 * 1024 * 1024
        ),
        name="backward",
    )
    gradients = list(call(*operands))
    if not summed:
        for index in (2, 3, 4):
            gradients[index] = lax.psum_scatter(
                gradients[index], ("exp", "rep"), scatter_dimension=0, tiled=True
            )
    return gradients


def exchange(blocks):
    return lax.all_to_all(blocks, "exp", split_axis=0, concat_axis=0, tiled=True)


def on_device(
    tokens,
    ln1_gain,
    ln1_bias,
    w_qkv,
    w_out,
    ln2_gain,
    ln2_bias,
    w_router,
    w_in,
    b_in,
    w_back,
    b_back,
    lengths,
    routes,
    priority,
    padding,
    cotangent,
):
    experts = lax.axis_size("exp")
    reps = lax.axis_size("rep")
    devices = experts * reps
    capacity = (TOK_DEV * 210 + experts * 100 - 1) // (experts * 100)
    padded = -(-(capacity + 3) // 16) * 16
    rows = w_qkv.shape[0]
    small = jnp.concatenate(
        [w_router, jnp.stack([ln1_gain, ln1_bias, ln2_gain, ln2_bias], axis=1)], axis=1
    )
    small = jnp.pad(small, ((0, 0), (0, LANES - small.shape[1])))
    packed = jnp.concatenate([w_qkv, w_out, small], axis=1)
    gathered = gather_blocks(packed, devices, reps).reshape(D, packed.shape[1])
    qkv_weight = gathered[:, : 3 * D]
    out_weight = gathered[:, 3 * D : 4 * D]
    router_weight = gathered[:, 4 * D : 4 * D + experts]
    vectors = gathered[:, 4 * D + experts : 4 * D + experts + 4].T
    gain_one, bias_one, gain_two, bias_two = (vectors[0], vectors[1], vectors[2], vectors[3])

    first_hot, second_hot, pick_first, pick_second = dispatch_tables(
        routes, priority, padding, experts, capacity, padded
    )
    picks = pick_first + pick_second
    grad_blocks = lax.dot_general(picks, cotangent, contract_first, preferred_element_type=jnp.float32)
    grad_blocks = grad_blocks.astype(jnp.bfloat16).reshape(experts, padded, D)
    grad_blocks, gathered_done = lax.optimization_barrier((grad_blocks, qkv_weight))
    qkv_weight = gathered_done
    grad_arrived = exchange(grad_blocks)

    inputs = tokens.astype(jnp.float32)
    normed, normal_one, inverse_one = norm_forward(inputs, gain_one, bias_one)
    normed_low = normed.astype(jnp.bfloat16)
    qkv = (
        jnp.dot(normed_low, qkv_weight, preferred_element_type=jnp.float32)
        .astype(jnp.bfloat16)
        .reshape(ROWS_DEV, SLOTS, 3 * D)
    )
    bounds = jnp.cumsum(lengths[0])
    segments = jnp.sum(
        (jnp.arange(SLOTS, dtype=jnp.int32)[:, None] >= bounds[None, :]).astype(jnp.int32), axis=1
    )
    mixed_low = attend(qkv[0], segments, padding)
    resid = inputs + jnp.dot(mixed_low, out_weight, preferred_element_type=jnp.float32)
    routed_float, normal_two, inverse_two = norm_forward(resid, gain_two, bias_two)
    routed = routed_float.astype(jnp.bfloat16)
    logits = jnp.dot(routed, router_weight, preferred_element_type=jnp.float32)
    probs = jax.nn.softmax(logits, axis=-1)
    gate_first = jnp.sum(probs * first_hot, axis=1)
    gate_second = jnp.sum(probs * second_hot, axis=1)
    buffer = lax.dot_general(picks, routed, contract_first, preferred_element_type=jnp.float32)
    buffer = buffer.astype(jnp.bfloat16).reshape(experts, padded, D)
    slot_gates = jnp.sum(
        pick_first.astype(jnp.float32) * gate_first[:, None]
        + pick_second.astype(jnp.float32) * gate_second[:, None],
        axis=0,
    ).reshape(experts, padded)[:, :capacity]
    high = lax.reduce_precision(slot_gates, 8, 7)
    middle = lax.reduce_precision(slot_gates - high, 8, 7)
    terms = jnp.stack([high, middle, slot_gates - high - middle], axis=1).astype(jnp.bfloat16)
    terms = jnp.pad(terms, ((0, 0), (0, padded - capacity - 3), (0, D - capacity)))
    buffer = lax.dynamic_update_slice(buffer, terms, (0, capacity, 0))
    grad_buffer, result, half_back, half_in = run_experts(
        buffer, grad_arrived, w_in[0], w_back[0], b_in, b_back, capacity, reps
    )
    terms = grad_buffer[:, capacity : capacity + 3, :padded].transpose(1, 0, 2)
    terms = jnp.pad(terms.reshape(3, experts * padded), ((0, 13), (0, 0)))
    (
        output,
        grad_tokens,
        sum_qkv,
        sum_out,
        sum_small,
        back_total,
        in_total,
        all_back,
        all_in,
    ) = run_backward(
        (
            grad_buffer.reshape(experts * padded, D),
            result,
            pick_first,
            pick_second,
            terms,
            jnp.pad(probs, ((0, 0), (0, LANES - experts))),
            routes,
            cotangent,
            resid,
            tokens,
            normed_low,
            routed,
            qkv[0],
            mixed_low,
            gathered,
            vectors.astype(jnp.float32),
            segments.reshape(SLOTS, 1),
            segments.reshape(1, SLOTS),
            padding.reshape(SLOTS, 1),
            half_back,
            half_in,
        ),
        experts,
        reps,
        rows,
    )
    vector_sums = sum_small[:, experts : experts + 4]
    hidden = b_in.shape[1]
    piece = hidden // reps
    return (
        output,
        grad_tokens,
        vector_sums[:, 0],
        vector_sums[:, 1],
        sum_qkv,
        sum_out,
        vector_sums[:, 2],
        vector_sums[:, 3],
        sum_small[:, :experts],
        in_total[None],
        all_back[:, piece, :piece].astype(jnp.float32).reshape(1, hidden),
        back_total[None],
        all_back[:1, piece + 1, :].astype(jnp.float32),
    )


def solution(mesh):
    return jax.shard_map(
        on_device,
        mesh=mesh,
        in_specs=(
            P(("exp", "rep"), None),
            P(("exp", "rep")),
            P(("exp", "rep")),
            P(("exp", "rep"), None),
            P(("exp", "rep"), None),
            P(("exp", "rep")),
            P(("exp", "rep")),
            P(("exp", "rep"), None),
            P("exp", None, None),
            P("exp", None),
            P("exp", None, None),
            P("exp", None),
            P(("exp", "rep"), None),
            P(("exp", "rep"), None),
            P(("exp", "rep")),
            P(("exp", "rep")),
            P(("exp", "rep"), None),
        ),
        out_specs=(
            P(("exp", "rep"), None),
            P(("exp", "rep"), None),
            P(("exp", "rep")),
            P(("exp", "rep")),
            P(("exp", "rep"), None),
            P(("exp", "rep"), None),
            P(("exp", "rep")),
            P(("exp", "rep")),
            P(("exp", "rep"), None),
            P("exp", None, None),
            P("exp", None),
            P("exp", None, None),
            P("exp", None),
        ),
        check_vma=False,
    )
```

```python
import functools

import jax
import jax.numpy as jnp
from jax import lax
from jax.experimental import pallas as pl
from jax.experimental.pallas import tpu as pltpu
from jax.sharding import PartitionSpec as P

D = 768
HEADS = 12
HEAD = 64
SLOTS = 576
ROWS_DEV = 1
TOK_DEV = 576


root_half = 0.7071067811865476
inverse_root_tau = 0.3989422804014327
contract_first = (((0,), (0,)), ((), ()))
contract_last = (((1,), (1,)), ((), ()))


def norm_forward(inputs, gain, offset):
    center = inputs - jnp.mean(inputs, axis=-1, keepdims=True)
    inverse = lax.rsqrt(jnp.mean(center * center, axis=-1, keepdims=True) + 1e-06)
    normal = center * inverse
    return (normal * gain.astype(jnp.float32) + offset.astype(jnp.float32), normal, inverse)


def dispatch_tables(routes, priority, padding, experts, capacity, padded):
    labels = jnp.arange(experts, dtype=jnp.int32)
    first_hot = (routes[:, 0:1] == labels[None, :]).astype(jnp.bfloat16)
    second_hot = (routes[:, 1:2] == labels[None, :]).astype(jnp.bfloat16)
    live = padding[:, None].astype(jnp.bfloat16)
    earlier = (priority[None, :] < priority[:, None]).astype(jnp.bfloat16)
    before_first = jnp.dot(earlier, first_hot * live, preferred_element_type=jnp.float32)
    first_counts = jnp.sum((first_hot * live).astype(jnp.float32), axis=0)
    before_second = (
        jnp.dot(earlier, second_hot * live, preferred_element_type=jnp.float32)
        + first_counts[None, :]
    )
    place_first = jnp.sum(before_first * first_hot, axis=1).astype(jnp.int32)
    place_second = jnp.sum(before_second * second_hot, axis=1).astype(jnp.int32)
    kept_first = (padding == 1) & (place_first < capacity)
    kept_second = (padding == 1) & (place_second < capacity)
    slot_labels = jnp.arange(experts * padded, dtype=jnp.int32)
    slot_first = routes[:, 0] * padded + place_first
    slot_second = routes[:, 1] * padded + place_second
    pick_first = ((slot_first[:, None] == slot_labels[None, :]) & kept_first[:, None]).astype(
        jnp.bfloat16
    )
    pick_second = ((slot_second[:, None] == slot_labels[None, :]) & kept_second[:, None]).astype(
        jnp.bfloat16
    )
    return (first_hot.astype(jnp.float32), second_hot.astype(jnp.float32), pick_first, pick_second)


LANES = 128
MESH_ID = pl.DeviceIdType.MESH


def bit_count(number):
    return number.bit_length() - 1


def flip(position, bit):
    step = 1 << bit
    return position + (1 - 2 * lax.rem(lax.div(position, step), 2)) * step


def coordinates(position, reps):
    return (lax.div(position, reps), lax.rem(position, reps))


def greet(bits, me, reps):
    barrier = pltpu.get_barrier_semaphore()
    for bit in range(bits):
        pl.semaphore_signal(
            barrier, inc=1, device_id=coordinates(flip(me, bit), reps), device_id_type=MESH_ID
        )
    pl.semaphore_wait(barrier, bits)


def lowest_bit(number):
    return (number & -number).bit_length() - 1


def gather_kernel(devices, reps, own_ref, all_ref, send_sem, recv_sem, local_sem):
    bits = bit_count(devices)
    me = lax.axis_index("exp") * reps + lax.axis_index("rep")
    greet(bits, me, reps)
    local = pltpu.make_async_copy(own_ref, all_ref.at[me], local_sem)
    local.start()

    def owner_of(distance):
        found = me
        for bit in range(bits):
            if distance >> bit & 1:
                found = flip(found, bit)
        return found

    def transfer(source_ref, distance, bit):
        owner = owner_of(distance)
        index = distance + (1 << bit)
        return pltpu.make_async_remote_copy(
            src_ref=source_ref,
            dst_ref=all_ref.at[owner],
            send_sem=send_sem.at[index],
            recv_sem=recv_sem.at[index],
            device_id=coordinates(flip(me, bit), reps),
            device_id_type=MESH_ID,
        )

    def arrival(distance):
        owner = owner_of(distance)
        return pltpu.make_async_remote_copy(
            src_ref=all_ref.at[owner],
            dst_ref=all_ref.at[owner],
            send_sem=send_sem.at[distance],
            recv_sem=recv_sem.at[distance],
            device_id=coordinates(flip(me, lowest_bit(distance)), reps),
            device_id_type=MESH_ID,
        )

    sent = []
    for bit in range(bits):
        copy = transfer(own_ref, 0, bit)
        copy.start()
        sent.append(copy)
    order = sorted(range(1, devices), key=lambda d: (bin(d).count("1"), -d))
    last = []
    for distance in order:
        low = lowest_bit(distance)
        if low == 0:
            last.append(distance)
            continue
        arrival(distance).wait_recv()
        for bit in range(low):
            copy = transfer(all_ref.at[owner_of(distance)], distance, bit)
            copy.start()
            sent.append(copy)
    for distance in last:
        arrival(distance).wait_recv()
    for copy in sent:
        copy.wait_send()
    local.wait()


def gather_blocks(block, devices, reps):
    return pl.pallas_call(
        functools.partial(gather_kernel, devices, reps),
        out_shape=jax.ShapeDtypeStruct((devices,) + block.shape, block.dtype),
        in_specs=[pl.BlockSpec(memory_space=pl.ANY)],
        out_specs=pl.BlockSpec(memory_space=pl.ANY),
        scratch_shapes=[
            pltpu.SemaphoreType.DMA((devices,)),
            pltpu.SemaphoreType.DMA((devices,)),
            pltpu.SemaphoreType.DMA,
        ],
        compiler_params=pltpu.CompilerParams(collective_id=0, has_side_effects=True),
        name="gather_dense",
    )(block)


def row_of(column, width):
    count = column.shape[0]
    down = lax.broadcasted_iota(jnp.int32, (count, width), 0)
    across = lax.broadcasted_iota(jnp.int32, (count, width), 1)
    return jnp.sum(jnp.where(down == across, column, 0.0), axis=0, keepdims=True)


def column_of(row, count):
    width = row.shape[1]
    down = lax.broadcasted_iota(jnp.int32, (count, width), 0)
    across = lax.broadcasted_iota(jnp.int32, (count, width), 1)
    return jnp.sum(jnp.where(down == across, row, 0.0), axis=1, keepdims=True)


def three_terms(value):
    high = value.astype(jnp.bfloat16).astype(jnp.float32)
    rest = value - high
    middle = rest.astype(jnp.bfloat16).astype(jnp.float32)
    return (high, middle, rest - middle)


def expert_kernel(
    experts,
    capacity,
    padded,
    block,
    send_ref,
    grad_ref,
    w_in_ref,
    w_back_ref,
    b_in_ref,
    b_back_ref,
    return_ref,
    result_ref,
    half_back_ref,
    half_in_ref,
    slots,
    grads,
    gated,
    weight_in,
    weight_back,
    active,
    grad_pre,
    back_rows,
    result_rows,
    result_total,
    back_total,
    away_back,
    away_in,
    other_back,
    other_in,
    load_sem,
    send_sem,
    recv_sem,
    return_send_sem,
    return_recv_sem,
    result_sem,
    core_send,
    core_recv,
    stage_sem,
):
    mine = lax.axis_index("exp")
    rep = lax.axis_index("rep")
    bits = bit_count(experts)
    groups = experts // 2
    hidden = weight_in.shape[1]
    steps = hidden // block
    lanes = 256 if capacity <= 256 else D
    gate_row = capacity - (padded - 16)

    barrier = pltpu.get_barrier_semaphore()

    def greet_one(step, carry):
        other = lax.rem(mine + step, experts)
        pl.semaphore_signal(barrier, inc=1, device_id=(other, rep), device_id_type=MESH_ID)
        return carry

    lax.fori_loop(1, experts, greet_one, 0)
    core = lax.rem(rep, 2)
    partner = (mine, flip(rep, 0))
    pl.semaphore_signal(barrier, inc=1, device_id=partner, device_id_type=MESH_ID)

    def group_of(index):
        half = lax.div(mine, 2)
        found = half
        for bit in range(bits - 1):
            found = found + lax.rem(lax.div(index, 1 << bit), 2) * (
                (1 - 2 * lax.rem(lax.div(half, 1 << bit), 2)) * (1 << bit)
            )
        return found

    def place(expert):
        return pl.ds(pl.multiple_of(expert * padded, 16), padded)

    def outgoing(expert):
        return pltpu.make_async_remote_copy(
            src_ref=send_ref.at[expert],
            dst_ref=slots.at[place(mine)],
            send_sem=send_sem.at[expert],
            recv_sem=recv_sem.at[mine],
            device_id=(expert, rep),
            device_id_type=MESH_ID,
        )

    def incoming(expert):
        return pltpu.make_async_remote_copy(
            src_ref=send_ref.at[mine],
            dst_ref=slots.at[place(expert)],
            send_sem=send_sem.at[expert],
            recv_sem=recv_sem.at[expert],
            device_id=(expert, rep),
            device_id_type=MESH_ID,
        )

    def going_back(expert):
        return pltpu.make_async_remote_copy(
            src_ref=back_rows.at[place(expert)],
            dst_ref=return_ref.at[mine],
            send_sem=return_send_sem.at[expert],
            recv_sem=return_recv_sem.at[mine],
            device_id=(expert, rep),
            device_id_type=MESH_ID,
        )

    def coming_back(expert):
        return pltpu.make_async_remote_copy(
            src_ref=back_rows.at[place(expert)],
            dst_ref=return_ref.at[expert],
            send_sem=return_send_sem.at[expert],
            recv_sem=return_recv_sem.at[expert],
            device_id=(expert, rep),
            device_id_type=MESH_ID,
        )

    neighbour = flip(mine, 0)
    loads = [
        pltpu.make_async_copy(send_ref.at[mine], slots.at[place(mine)], load_sem.at[0]),
        pltpu.make_async_copy(grad_ref, grads, load_sem.at[1]),
        pltpu.make_async_copy(w_in_ref, weight_in, load_sem.at[2]),
        pltpu.make_async_copy(w_back_ref, weight_back, load_sem.at[3]),
    ]
    for copy in loads:
        copy.start()
    pl.semaphore_wait(barrier, experts)

    def send_group(index):
        pair = group_of(index)
        outgoing(2 * pair).start()
        outgoing(2 * pair + 1).start()

    outgoing(neighbour).start()
    if groups > 2:
        send_group(2)
    if groups > 1:
        send_group(1)
    for copy in loads:
        copy.wait()

    def send_back_group(index):
        pair = group_of(index)
        going_back(2 * pair).start()
        going_back(2 * pair + 1).start()

    def gate_columns(expert):
        tail = slots[pl.ds(pl.multiple_of(expert * padded + padded - 16, 16), 16), :].astype(jnp.float32)
        row = jnp.sum(tail[gate_row : gate_row + 3, :lanes], axis=0, keepdims=True)
        return column_of(row, padded)

    def group_step(index, carry):
        pair = group_of(index)

        @pl.when(index == 0)
        def _():
            incoming(neighbour).wait_recv()

        @pl.when(index > 0)
        def _():
            incoming(2 * pair).wait_recv()
            incoming(2 * pair + 1).wait_recv()

        @pl.when(jnp.logical_and(index >= 1, index + 2 < groups))
        def _():
            send_group(index + 2)

        @pl.when(index == 1)
        def _():
            going_back(neighbour).start()

        @pl.when(index > 1)
        def _():
            send_back_group(index - 1)

        here = pl.ds(pl.multiple_of(pair * 2 * padded, 16), 2 * padded)
        for side in range(2):
            spot = place(2 * pair + side)
            gate = gate_columns(2 * pair + side)
            gated[spot, :] = (gate * grads[spot, :].astype(jnp.float32)).astype(jnp.bfloat16)

        def hidden_step(step, inner):
            columns = pl.ds(pl.multiple_of(step * block, block), block)
            pre = (
                jnp.dot(slots[here, :], weight_in[:, columns], preferred_element_type=jnp.float32)
                + b_in_ref[:, columns]
            )
            grad_active = lax.dot_general(
                gated[here, :],
                weight_back[columns, :],
                contract_last,
                preferred_element_type=jnp.float32,
            )
            cumulative = 0.5 * (1.0 + lax.erf(pre * root_half))
            slope = cumulative + pre * inverse_root_tau * jnp.exp(-0.5 * pre * pre)
            active_low = (pre * cumulative).astype(jnp.bfloat16)
            grad_low = (grad_active * slope).astype(jnp.bfloat16)
            active[here, columns] = active_low
            grad_pre[here, columns] = grad_low
            result_part = jnp.dot(
                active_low, weight_back[columns, :], preferred_element_type=jnp.float32
            )
            back_part = lax.dot_general(
                grad_low, weight_in[:, columns], contract_last, preferred_element_type=jnp.float32
            )

            @pl.when(step == 0)
            def _():
                result_total[...] = result_part
                back_total[...] = back_part

            @pl.when(step > 0)
            def _():
                result_total[...] += result_part
                back_total[...] += back_part

            return inner

        lax.fori_loop(0, steps, hidden_step, 0)
        for side in range(2):
            expert = 2 * pair + side
            span = slice(side * padded, (side + 1) * padded)
            spot = place(expert)
            result_low = (result_total[span, :] + b_back_ref[...]).astype(jnp.bfloat16)
            result_rows[spot, :] = result_low
            grad_gate = jnp.sum(
                grads[spot, :].astype(jnp.float32) * result_low.astype(jnp.float32),
                axis=1,
                keepdims=True,
            )
            gate_line = row_of(
                jnp.where(
                    lax.broadcasted_iota(jnp.int32, (padded, 1), 0) < capacity, grad_gate, 0.0
                ),
                lanes,
            )
            if lanes < D:
                gate_line = jnp.concatenate(
                    [gate_line, jnp.zeros((1, D - lanes), jnp.float32)], axis=1
                )
            high, middle, lowest = three_terms(gate_line)
            row = lax.broadcasted_iota(jnp.int32, (padded, D), 0)
            value = back_total[span, :]
            value = jnp.where(row == capacity, high, value)
            value = jnp.where(row == capacity + 1, middle, value)
            value = jnp.where(row == capacity + 2, lowest, value)
            back_rows[spot, :] = value.astype(jnp.bfloat16)
        return carry

    lax.fori_loop(0, groups, group_step, 0)
    if groups > 1:
        send_back_group(groups - 1)
    else:
        going_back(neighbour).start()
    own_back = pltpu.make_async_copy(back_rows.at[place(mine)], return_ref.at[mine], load_sem.at[0])
    own_back.start()
    results = pltpu.make_async_copy(result_rows, result_ref, result_sem)
    results.start()

    piece = away_in.shape[2]
    half = away_in.shape[0]
    bias_back = jnp.sum(gated[...].astype(jnp.float32), axis=0, keepdims=True)

    def sums_of(number):
        columns = pl.ds(pl.multiple_of(number * piece, LANES), piece)
        back = lax.dot_general(
            active[:, columns], gated[...], contract_first, preferred_element_type=jnp.float32
        )
        inward = lax.dot_general(
            slots[...], grad_pre[:, columns], contract_first, preferred_element_type=jnp.float32
        )
        bias_in = jnp.sum(grad_pre[:, columns].astype(jnp.float32), axis=0, keepdims=True)
        if piece < D:
            bias_in = jnp.concatenate([bias_in, jnp.zeros((1, D - piece), jnp.float32)], axis=1)
        row = lax.broadcasted_iota(jnp.int32, (16, D), 0)
        extra = jnp.where(row == 0, bias_in, jnp.where(row == 1, bias_back, 0.0))
        return (back, inward, extra)

    def core_copies(index):
        return [
            pltpu.make_async_remote_copy(
                src_ref=source.at[index],
                dst_ref=target.at[index],
                send_sem=core_send.at[kind, index],
                recv_sem=core_recv.at[kind, index],
                device_id=partner,
                device_id_type=MESH_ID,
            )
            for kind, (source, target) in enumerate(
                ((away_back, other_back), (away_in, other_in))
            )
        ]

    def away_step(index, carry):
        back, inward, extra = sums_of(2 * index + 1 - core)
        away_back[index, :piece, :] = back.astype(jnp.bfloat16)
        away_back[index, piece:, :] = extra.astype(jnp.bfloat16)
        away_in[index] = inward.astype(jnp.bfloat16)
        for copy in core_copies(index):
            copy.start()
        return carry

    def kept_copies(index):
        return (
            pltpu.make_async_copy(other_back.at[index], half_back_ref.at[index], stage_sem.at[0, index]),
            pltpu.make_async_copy(other_in.at[index], half_in_ref.at[index], stage_sem.at[1, index]),
        )

    def kept_step(index, carry):
        back, inward, extra = sums_of(2 * index + core)
        for copy in core_copies(index):
            copy.wait_recv()
        other_back[index, :piece, :] = (
            back + other_back[index, :piece, :].astype(jnp.float32)
        ).astype(jnp.bfloat16)
        other_back[index, piece:, :] = (
            extra + other_back[index, piece:, :].astype(jnp.float32)
        ).astype(jnp.bfloat16)
        other_in[index] = (inward + other_in[index].astype(jnp.float32)).astype(jnp.bfloat16)
        for copy in kept_copies(index):
            copy.start()
        return carry

    lax.fori_loop(0, half, away_step, 0)
    lax.fori_loop(0, half, kept_step, 0)
    for index in range(half):
        for copy in kept_copies(index):
            copy.wait()
        for copy in core_copies(index):
            copy.wait_send()
    own_back.wait()
    results.wait()

    def finish(step, carry):
        other = lax.rem(mine + step, experts)
        outgoing(other).wait_send()
        going_back(other).wait_send()
        coming_back(other).wait_recv()
        return carry

    lax.fori_loop(1, experts, finish, 0)


def run_experts(buffer, grads, w_in, w_back, b_in, b_back, capacity, reps):
    experts, padded = (buffer.shape[0], buffer.shape[1])
    hidden = w_in.shape[1]
    block = 512
    rows = experts * padded
    half = reps // 2
    piece = hidden // reps
    low = jnp.bfloat16
    anywhere = pl.BlockSpec(memory_space=pl.ANY)
    inside = pl.BlockSpec(memory_space=pltpu.VMEM)
    return pl.pallas_call(
        functools.partial(expert_kernel, experts, capacity, padded, block),
        out_shape=[
            jax.ShapeDtypeStruct((experts, padded, D), low),
            jax.ShapeDtypeStruct((rows, D), low),
            jax.ShapeDtypeStruct((half, piece + 16, D), low),
            jax.ShapeDtypeStruct((half, D, piece), low),
        ],
        in_specs=[anywhere, anywhere, anywhere, anywhere, inside, inside],
        out_specs=[anywhere, anywhere, anywhere, anywhere],
        scratch_shapes=[
            pltpu.VMEM((rows, D), low),
            pltpu.VMEM((rows, D), low),
            pltpu.VMEM((rows, D), low),
            pltpu.VMEM((D, hidden), low),
            pltpu.VMEM((hidden, D), low),
            pltpu.VMEM((rows, hidden), low),
            pltpu.VMEM((rows, hidden), low),
            pltpu.VMEM((rows, D), low),
            pltpu.VMEM((rows, D), low),
            pltpu.VMEM((2 * padded, D), jnp.float32),
            pltpu.VMEM((2 * padded, D), jnp.float32),
            pltpu.VMEM((half, piece + 16, D), low),
            pltpu.VMEM((half, D, piece), low),
            pltpu.VMEM((half, piece + 16, D), low),
            pltpu.VMEM((half, D, piece), low),
            pltpu.SemaphoreType.DMA((4,)),
            pltpu.SemaphoreType.DMA((experts,)),
            pltpu.SemaphoreType.DMA((experts,)),
            pltpu.SemaphoreType.DMA((experts,)),
            pltpu.SemaphoreType.DMA((experts,)),
            pltpu.SemaphoreType.DMA,
            pltpu.SemaphoreType.DMA((2, half)),
            pltpu.SemaphoreType.DMA((2, half)),
            pltpu.SemaphoreType.DMA((2, half)),
        ],
        compiler_params=pltpu.CompilerParams(
            collective_id=2, has_side_effects=True, vmem_limit_bytes=60 * 1024 * 1024
        ),
        cost_estimate=pl.CostEstimate(
            flops=12 * rows * D * hidden, bytes_accessed=40 << 20, transcendentals=2 * rows * hidden
        ),
        name="experts",
    )(buffer, grads.reshape(rows, D), w_in, w_back, b_in.astype(jnp.float32), b_back.astype(jnp.float32))


def attend_kernel(segment_col, segment_row, live_row, query_ref, keys_ref, values_ref, mixed_ref, bias):
    @pl.when(pl.program_id(0) == 0)
    def _():
        row = lax.broadcasted_iota(jnp.int32, (SLOTS, SLOTS), 0)
        column = lax.broadcasted_iota(jnp.int32, (SLOTS, SLOTS), 1)
        seen = (segment_col[...] == segment_row[...]) & ((live_row[...] == 1) | (row == column))
        bias[...] = jnp.where(seen, 0.0, -1e30)

    for side in range(2):
        lanes = slice(side * HEAD, (side + 1) * HEAD)
        scores = lax.dot_general(
            query_ref[:, lanes], keys_ref[:, lanes], contract_last, preferred_element_type=jnp.float32
        )
        scores = scores * HEAD ** (-0.5) + bias[...]
        expo = jnp.exp(scores - jnp.max(scores, axis=1, keepdims=True))
        total = jnp.sum(expo, axis=1, keepdims=True)
        probs = (expo * (1.0 / total)).astype(jnp.bfloat16)
        mixed = jnp.dot(probs, values_ref[:, lanes], preferred_element_type=jnp.float32)
        mixed_ref[:, lanes] = mixed.astype(jnp.bfloat16)


def attend(qkv, segments, live):
    pairs = HEADS // 2
    return pl.pallas_call(
        attend_kernel,
        grid=(pairs,),
        out_shape=jax.ShapeDtypeStruct((SLOTS, D), jnp.bfloat16),
        in_specs=[
            pl.BlockSpec((SLOTS, 1), lambda i: (0, 0)),
            pl.BlockSpec((1, SLOTS), lambda i: (0, 0)),
            pl.BlockSpec((1, SLOTS), lambda i: (0, 0)),
            pl.BlockSpec((SLOTS, 2 * HEAD), lambda i: (0, i)),
            pl.BlockSpec((SLOTS, 2 * HEAD), lambda i: (0, pairs + i)),
            pl.BlockSpec((SLOTS, 2 * HEAD), lambda i: (0, 2 * pairs + i)),
        ],
        out_specs=pl.BlockSpec((SLOTS, 2 * HEAD), lambda i: (0, i)),
        scratch_shapes=[pltpu.VMEM((SLOTS, SLOTS), jnp.float32)],
        cost_estimate=pl.CostEstimate(
            flops=16 * HEADS * SLOTS * SLOTS * HEAD, bytes_accessed=4 << 20, transcendentals=HEADS * SLOTS * SLOTS
        ),
        name="attend",
    )(segments.reshape(SLOTS, 1), segments.reshape(1, SLOTS), live.reshape(1, SLOTS), qkv, qkv, qkv)


BAND = 48


def fold_rows(values):
    return jnp.sum(values.reshape(BAND // 8, 8, values.shape[1]), axis=0)


def backward_kernel(
    experts,
    reps,
    chunks,
    summed,
    back_ref,
    result_ref,
    first_ref,
    second_ref,
    terms_ref,
    probs_ref,
    routes_ref,
    cotangent_ref,
    resid_ref,
    tokens_ref,
    normed_ref,
    routed_ref,
    qkv_ref,
    mixed_ref,
    weights_ref,
    vectors_ref,
    segment_col,
    segment_row,
    live_col,
    half_back_ref,
    half_in_ref,
    output_ref,
    grad_tokens_ref,
    sum_qkv_ref,
    sum_out_ref,
    sum_small_ref,
    all_back_ref,
    all_in_ref,
    all_tail_ref,
    *refs,
):
    devices = experts * reps
    bits = bit_count(devices)
    half = reps // 2
    mine = lax.axis_index("exp")
    rep = lax.axis_index("rep")
    me = mine * reps + rep
    core = lax.rem(rep, 2)
    along = lax.div(rep, 2)
    (
        back,
        first,
        second,
        cotangent,
        resid,
        tokens,
        normed,
        routed,
        qkv,
        mixed,
        weights,
        returned,
        bias,
        wide,
        tall,
        grad_resid,
        grad_attn,
        grad_mixed,
        grad_qkv,
        grad_logits,
        own_back,
        own_in,
        other_back,
        other_in,
    ) = refs[:24]
    refs = refs[24:]
    count = len(chunks) if summed else 0
    parts, refs = (refs[:count], refs[count:])
    recvs, refs = ([refs[c * bits : (c + 1) * bits] for c in range(count)], refs[count * bits :])
    (
        load_sem,
        result_send,
        result_recv,
        dense_send,
        dense_recv,
        half_send,
        half_recv,
        all_send,
        all_recv,
        own_sem,
    ) = refs
    padded = result_ref.shape[0] // experts
    piece = half_in_ref.shape[2]

    barrier = pltpu.get_barrier_semaphore()

    def greet_expert(step, carry):
        other = lax.rem(mine + step, experts)
        pl.semaphore_signal(barrier, inc=1, device_id=(other, rep), device_id_type=MESH_ID)
        return carry

    def greet_rep(step, carry):
        other = lax.rem(rep + step, reps)
        pl.semaphore_signal(barrier, inc=1, device_id=(mine, other), device_id_type=MESH_ID)
        return carry

    lax.fori_loop(1, experts, greet_expert, 0)
    lax.fori_loop(1, reps, greet_rep, 0)

    sources = [
        (back_ref, back),
        (first_ref, first),
        (second_ref, second),
        (routed_ref, routed),
        (weights_ref, weights),
        (resid_ref, resid),
        (cotangent_ref, cotangent),
        (mixed_ref, mixed),
        (qkv_ref, qkv),
        (normed_ref, normed),
        (tokens_ref, tokens),
        (half_back_ref.at[along], own_back),
        (half_in_ref.at[along], own_in),
    ]
    loads = [
        pltpu.make_async_copy(source, target, load_sem.at[i])
        for i, (source, target) in enumerate(sources)
    ]
    for copy in loads:
        copy.start()
    pl.semaphore_wait(barrier, experts - 1 + reps - 1)

    def half_copies(step):
        other = lax.rem(along + step, half)
        came = lax.rem(along + half - step, half)
        device = (mine, 2 * other + core)
        return [
            pltpu.make_async_remote_copy(
                src_ref=source.at[other],
                dst_ref=target.at[step - 1],
                send_sem=half_send.at[kind, step - 1],
                recv_sem=half_recv.at[kind, step - 1],
                device_id=device,
                device_id_type=MESH_ID,
            )
            for kind, (source, target) in enumerate(
                ((half_back_ref, other_back), (half_in_ref, other_in))
            )
        ]

    half_moves = [half_copies(step) for step in range(1, half)]
    for kind in range(2):
        for moves in half_moves:
            moves[kind].start()

    def place(expert):
        return pl.ds(pl.multiple_of(expert * padded, 16), padded)

    def result_copy(step):
        other = lax.rem(mine + step, experts)
        came = lax.rem(mine + experts - step, experts)
        return pltpu.make_async_remote_copy(
            src_ref=result_ref.at[place(other)],
            dst_ref=returned.at[place(mine)],
            send_sem=result_send.at[step],
            recv_sem=result_recv.at[step],
            device_id=(other, rep),
            device_id_type=MESH_ID,
        )

    def start_result(step, carry):
        result_copy(step).start()
        return carry

    own_result = pltpu.make_async_copy(
        result_ref.at[place(mine)], returned.at[place(mine)], result_send.at[0]
    )
    own_result.start()
    lax.fori_loop(1, experts, start_result, 0)

    row = lax.broadcasted_iota(jnp.int32, (SLOTS, SLOTS), 0)
    column = lax.broadcasted_iota(jnp.int32, (SLOTS, SLOTS), 1)
    seen = (segment_col[...] == segment_row[...]) & ((live_col[...] == 1) | (row == column))
    bias[...] = jnp.where(seen, 0.0, -1e30)

    for copy in loads[:5]:
        copy.wait()
    tall[...] = jnp.dot(first[...] + second[...], back[...], preferred_element_type=jnp.float32)
    gates_back = [
        jnp.sum(
            lax.dot_general(
                pick[...], terms_ref[...], contract_last, preferred_element_type=jnp.float32
            ),
            axis=1,
            keepdims=True,
        )
        for pick in (first, second)
    ]
    lane = lax.broadcasted_iota(jnp.int32, (SLOTS, LANES), 1)
    hots = [(lane == routes_ref[:, k : k + 1]).astype(jnp.float32) for k in range(2)]
    grad_probs = gates_back[0] * hots[0] + gates_back[1] * hots[1]
    probs = probs_ref[...]
    grad_logits[...] = (
        probs * (grad_probs - jnp.sum(probs * grad_probs, axis=1, keepdims=True))
    ).astype(jnp.bfloat16)
    tall[...] += lax.dot_general(
        grad_logits[...], weights[:, 4 * D :], contract_last, preferred_element_type=jnp.float32
    )
    for copy in loads[5:]:
        copy.wait()

    def band(step):
        return pl.ds(pl.multiple_of(step * BAND, 16), BAND)

    def norm_back(inputs, grad, gain):
        center = inputs - jnp.mean(inputs, axis=1, keepdims=True)
        inverse = lax.rsqrt(jnp.mean(center * center, axis=1, keepdims=True) + 1e-06)
        normal = center * inverse
        scaled = grad * gain
        grad_in = inverse * (
            scaled
            - jnp.mean(scaled, axis=1, keepdims=True)
            - normal * jnp.mean(scaled * normal, axis=1, keepdims=True)
        )
        return (grad_in, fold_rows(grad * normal), fold_rows(grad))

    zero = jnp.zeros((8, D), jnp.float32)

    def second_norm(step, carry):
        here = band(step)
        grad_in, grad_gain, grad_bias = norm_back(
            resid[here, :], tall[here, :], vectors_ref[2:3, :]
        )
        total = cotangent[here, :].astype(jnp.float32) + grad_in
        grad_resid[here, :] = total
        grad_attn[here, :] = total.astype(jnp.bfloat16)
        return (carry[0] + grad_gain, carry[1] + grad_bias)

    gain_two, bias_two = lax.fori_loop(0, SLOTS // BAND, second_norm, (zero, zero))

    plan = [0] + [bit_count(reps)] + list(range(bits - 1, bit_count(reps), -1))
    plan = plan + list(range(bit_count(reps) - 1, 0, -1))
    my_bit = [lax.rem(lax.div(me, 1 << bit), 2) for bit in range(bits)]
    rows = parts[0].shape[3] if summed else 0
    stride = experts + bits - 1
    outs = (sum_qkv_ref, sum_out_ref, sum_small_ref)

    def fill(c):
        width = chunks[c][2]

        def one(block, carry):
            owner = lax.div(block, reps)
            inner = lax.rem(block, reps)
            parts[c][owner, lax.div(inner, 2), lax.rem(inner, 2)] = wide[
                pl.ds(pl.multiple_of(block * rows, rows), rows), :width
            ].astype(jnp.bfloat16)
            return carry

        lax.fori_loop(0, devices, one, 0)

    def first_copy(c, expert):
        spot = lax.rem(expert, 2) * (devices // 4) + lax.div(expert, 2) * half
        return pltpu.make_async_remote_copy(
            src_ref=parts[c].at[expert, :, 1 - core],
            dst_ref=recvs[c][0].at[pl.ds(spot, half)],
            send_sem=dense_send.at[c * stride + expert],
            recv_sem=dense_recv.at[c * stride + expert],
            device_id=(mine, flip(rep, 0)),
            device_id_type=MESH_ID,
        )

    def later_copy(c, phase):
        size = devices >> (phase + 1)
        index = c * stride + experts + phase - 1
        return pltpu.make_async_remote_copy(
            src_ref=recvs[c][phase - 1].at[pl.ds((1 - my_bit[plan[phase]]) * size, size)],
            dst_ref=recvs[c][phase],
            send_sem=dense_send.at[index],
            recv_sem=dense_recv.at[index],
            device_id=coordinates(flip(me, plan[phase]), reps),
            device_id_type=MESH_ID,
        )

    def send_chunk(c):
        if not summed:
            array, start, width = chunks[c]
            pltpu.sync_copy(wide.at[:, :width], outs[array].at[:, pl.ds(start, width)])
            return
        fill(c)

        def one(expert, carry):
            first_copy(c, expert).start()
            return carry

        lax.fori_loop(0, experts, one, 0)

    def absorb(c, phase):
        if not summed:
            return
        size = devices >> (phase + 1)
        into = recvs[c][phase]
        if phase == 0:

            def arrived(expert, carry):
                first_copy(c, expert).wait_recv()
                return carry

            lax.fori_loop(0, experts, arrived, 0)

            def held(i):
                side = lax.div(i, devices // 4)
                rest = lax.rem(i, devices // 4)
                return parts[c][2 * lax.div(rest, half) + side, lax.rem(rest, half), core]
        else:
            later_copy(c, phase).wait_recv()
            base = my_bit[plan[phase]] * size

            def held(i):
                return recvs[c][phase - 1][base + i]

        if phase == bits - 1:
            array, start, width = chunks[c]
            outs[array][:, pl.ds(start, width)] = into[0].astype(jnp.float32) + held(0).astype(
                jnp.float32
            )
            return

        def one(i, carry):
            into[i] = (into[i].astype(jnp.float32) + held(i).astype(jnp.float32)).astype(
                jnp.bfloat16
            )
            return carry

        lax.fori_loop(0, size, one, 0)
        later_copy(c, phase + 1).start()

    out_chunk = [c for c in range(len(chunks)) if chunks[c][0] == 1][0]
    small_chunk = [c for c in range(len(chunks)) if chunks[c][0] == 2][0]
    qkv_chunks = [c for c in range(len(chunks)) if chunks[c][0] == 0]
    wide[...] = lax.dot_general(
        mixed[...], grad_attn[...], contract_first, preferred_element_type=jnp.float32
    )
    send_chunk(out_chunk)
    grad_mixed[...] = lax.dot_general(
        grad_attn[...], weights[:, 3 * D : 4 * D], contract_last, preferred_element_type=jnp.float32
    ).astype(jnp.bfloat16)

    sums = ((own_back, other_back), (own_in, other_in))
    kinds = ((0, 2), (1,))

    def own_part(kind):
        return (own_back.at[pl.ds(0, piece), :], own_in, own_back.at[pl.ds(piece, 16), :])[kind]

    def landing(kind, owner):
        if kind == 0:
            return all_back_ref.at[pl.ds(pl.multiple_of(owner * piece, 16), piece), :]
        if kind == 1:
            return all_in_ref.at[:, pl.ds(pl.multiple_of(owner * piece, LANES), piece)]
        return all_tail_ref.at[owner]

    def spread(kind, source, owner, device, step):
        return pltpu.make_async_remote_copy(
            src_ref=source,
            dst_ref=landing(kind, owner),
            send_sem=all_send.at[kind, step],
            recv_sem=all_recv.at[kind, step],
            device_id=device,
            device_id_type=MESH_ID,
        )

    def own_moves(kind):
        moves = [pltpu.make_async_copy(own_part(kind), landing(kind, rep), own_sem.at[kind])]
        for step in range(1, half):
            other = lax.rem(along + step, half)
            moves.append(spread(kind, own_part(kind), rep, (mine, 2 * other + core), step))
        moves.append(spread(kind, own_part(kind), rep, (mine, flip(rep, 0)), 0))
        return moves

    def complete(number):
        own, others = sums[number]
        for step in range(1, half):
            half_moves[step - 1][number].wait_recv()
        size = 16
        steps = own.shape[0] // size

        def one(step, carry):
            here = pl.ds(pl.multiple_of(step * size, 16), size)
            total = own[here, :].astype(jnp.float32)
            for step in range(1, half):
                total = total + others[step - 1, here, :].astype(jnp.float32)
            own[here, :] = total.astype(jnp.bfloat16)
            return carry

        lax.fori_loop(0, steps, one, 0)
        for kind in kinds[number]:
            for move in own_moves(kind):
                move.start()

    complete(0)
    absorb(out_chunk, 0)

    def attend_back(pair, carry):
        @pl.when(pair == 1)
        def _():
            absorb(out_chunk, 1)

        @pl.when(pair == 3)
        def _():
            complete(1)

        base = pl.multiple_of(pair * 2 * HEAD, 2 * HEAD)
        queries = qkv[:, pl.ds(base, 2 * HEAD)]
        keys = qkv[:, pl.ds(base + D, 2 * HEAD)]
        values = qkv[:, pl.ds(base + 2 * D, 2 * HEAD)]
        grads = grad_mixed[:, pl.ds(base, 2 * HEAD)]
        done = []
        for side in range(2):
            lanes = slice(side * HEAD, (side + 1) * HEAD)
            query, key, value, grad = (
                queries[:, lanes],
                keys[:, lanes],
                values[:, lanes],
                grads[:, lanes],
            )
            scores = lax.dot_general(key, query, contract_last, preferred_element_type=jnp.float32)
            scores = scores * HEAD ** (-0.5) + bias[...]
            expo = jnp.exp(scores - jnp.max(scores, axis=0, keepdims=True))
            weight = expo * (1.0 / jnp.sum(expo, axis=0, keepdims=True))
            grad_weight = lax.dot_general(
                value, grad, contract_last, preferred_element_type=jnp.float32
            )
            product = weight * grad_weight
            delta = jnp.sum(product, axis=0, keepdims=True)
            grad_scores = (product - weight * delta).astype(jnp.bfloat16)
            grad_value = jnp.dot(
                weight.astype(jnp.bfloat16), grad, preferred_element_type=jnp.float32
            )
            grad_key = jnp.dot(grad_scores, query, preferred_element_type=jnp.float32)
            grad_query = lax.dot_general(
                grad_scores, key, contract_first, preferred_element_type=jnp.float32
            )
            done.append(
                (grad_query * HEAD ** (-0.5), grad_key * HEAD ** (-0.5), grad_value)
            )
        for kind in range(3):
            grad_qkv[:, pl.ds(base + kind * D, 2 * HEAD)] = jnp.concatenate(
                [done[0][kind], done[1][kind]], axis=1
            ).astype(jnp.bfloat16)
        return carry

    lax.fori_loop(0, HEADS // 2, attend_back, 0)

    for position, c in enumerate(qkv_chunks):
        start = chunks[c][1]
        wide[...] = lax.dot_general(
            normed[...], grad_qkv[:, start : start + D], contract_first, preferred_element_type=jnp.float32
        )
        send_chunk(c)
        if position > 0:
            absorb(qkv_chunks[position - 1], 0)
    absorb(out_chunk, 2)
    tall[...] = lax.dot_general(
        grad_qkv[...], weights[:, : 3 * D], contract_last, preferred_element_type=jnp.float32
    )
    absorb(qkv_chunks[2], 0)
    absorb(qkv_chunks[0], 1)

    def first_norm(step, carry):
        here = band(step)
        grad_in, grad_gain, grad_bias = norm_back(
            tokens[here, :].astype(jnp.float32), tall[here, :], vectors_ref[0:1, :]
        )
        grad_tokens_ref[here, :] = grad_resid[here, :] + grad_in
        return (carry[0] + grad_gain, carry[1] + grad_bias)

    gain_one, bias_one = lax.fori_loop(0, SLOTS // BAND, first_norm, (zero, zero))
    wide[:, :LANES] = lax.dot_general(
        routed[...], grad_logits[...], contract_first, preferred_element_type=jnp.float32
    )
    lines = [jnp.sum(v, axis=0, keepdims=True) for v in (gain_one, bias_one, gain_two, bias_two)]
    lane = lax.broadcasted_iota(jnp.int32, (LANES, LANES), 1)
    for part in range(D // LANES):
        span = slice(part * LANES, (part + 1) * LANES)
        block = wide[span, :LANES]
        for k in range(4):
            block = jnp.where(lane == experts + k, column_of(lines[k][:, span], LANES), block)
        wide[span, :LANES] = block
    send_chunk(small_chunk)

    absorb(qkv_chunks[1], 1)
    absorb(out_chunk, 3)

    own_result.wait()

    def result_arrived(step, carry):
        result_copy(step).wait_recv()
        result_copy(step).wait_send()
        return carry

    lax.fori_loop(1, experts, result_arrived, 0)
    lane = lax.broadcasted_iota(jnp.int32, (SLOTS, LANES), 1)
    probs = probs_ref[...]
    gates = [
        jnp.sum(jnp.where(lane == routes_ref[:, k : k + 1], probs, 0.0), axis=1, keepdims=True)
        for k in range(2)
    ]
    tall[...] = resid[...] + gates[0] * jnp.dot(
        first[...], returned[...], preferred_element_type=jnp.float32
    )
    output_ref[...] = (
        tall[...]
        + gates[1] * jnp.dot(second[...], returned[...], preferred_element_type=jnp.float32)
    ).astype(jnp.bfloat16)

    order = [out_chunk] + qkv_chunks + [small_chunk]
    done = {out_chunk: 4, qkv_chunks[0]: 2, qkv_chunks[1]: 2, qkv_chunks[2]: 1, small_chunk: 0}
    for step in range(bits + len(order) - 1):
        for position, c in enumerate(order):
            phase = step - position
            if done[c] <= phase < bits:
                absorb(c, phase)

    partner = flip(rep, 0)

    def passed_on(kind, step):
        owner = 2 * lax.rem(along + half - step, half) + core
        return spread(kind, landing(kind, owner), owner, (mine, partner), half + step - 1)

    for kind in (0, 2, 1):
        for step in range(1, half):
            owner = 2 * lax.rem(along + half - step, half) + core
            spread(kind, landing(kind, owner), owner, (mine, owner), step).wait_recv()
            passed_on(kind, step).start()
    for kind in (0, 2, 1):
        spread(kind, landing(kind, partner), partner, (mine, partner), 0).wait_recv()
        for step in range(1, half):
            owner = 2 * lax.rem(along + half - step, half) + 1 - core
            spread(
                kind, landing(kind, owner), owner, (mine, partner), half + step - 1
            ).wait_recv()
        moves = own_moves(kind)
        moves[0].wait()
        for move in moves[1:]:
            move.wait_send()
        for step in range(1, half):
            passed_on(kind, step).wait_send()
    for moves in half_moves:
        for move in moves:
            move.wait_send()

    def dense_sent(c):
        def one(expert, carry):
            first_copy(c, expert).wait_send()
            return carry

        lax.fori_loop(0, experts, one, 0)
        for phase in range(1, bits):
            later_copy(c, phase).wait_send()

    for c in range(count):
        dense_sent(c)


def run_backward(operands, experts, reps, rows):
    devices = experts * reps
    bits = bit_count(devices)
    half = reps // 2
    (
        back,
        result,
        first,
        second,
        terms,
        probs,
        routes,
        cotangent,
        resid,
        tokens,
        normed,
        routed,
        qkv,
        mixed,
        weights,
        vectors,
        segment_col,
        segment_row,
        live_col,
        half_back,
        half_in,
    ) = operands
    low = jnp.bfloat16
    full = jnp.float32
    piece = half_in.shape[2]
    tail_rows = half_back.shape[1]
    chunks = [(0, k * D, D) for k in range(3)] + [(1, 0, D), (2, 0, LANES)]
    anywhere = pl.BlockSpec(memory_space=pl.ANY)
    inside = pl.BlockSpec(memory_space=pltpu.VMEM)
    slots = result.shape[0]
    scratch = [
        pltpu.VMEM((slots, D), low),
        pltpu.VMEM((SLOTS, slots), low),
        pltpu.VMEM((SLOTS, slots), low),
        pltpu.VMEM((SLOTS, D), low),
        pltpu.VMEM((SLOTS, D), full),
        pltpu.VMEM((SLOTS, D), low),
        pltpu.VMEM((SLOTS, D), low),
        pltpu.VMEM((SLOTS, D), low),
        pltpu.VMEM((SLOTS, 3 * D), low),
        pltpu.VMEM((SLOTS, D), low),
        pltpu.VMEM(weights.shape, low),
        pltpu.VMEM((slots, D), low),
        pltpu.VMEM((SLOTS, SLOTS), full),
        pltpu.VMEM((D, D), full),
        pltpu.VMEM((SLOTS, D), full),
        pltpu.VMEM((SLOTS, D), full),
        pltpu.VMEM((SLOTS, D), low),
        pltpu.VMEM((SLOTS, D), low),
        pltpu.VMEM((SLOTS, 3 * D), low),
        pltpu.VMEM((SLOTS, LANES), low),
        pltpu.VMEM((tail_rows, D), low),
        pltpu.VMEM((D, piece), low),
        pltpu.VMEM((half - 1, tail_rows, D), low),
        pltpu.VMEM((half - 1, D, piece), low),
    ]
    summed = rows % 8 == 0
    for _, _, width in chunks if summed else ():
        scratch.append(pltpu.VMEM((experts, half, 2, rows, width), low))
    for _, _, width in chunks if summed else ():
        for phase in range(bits):
            scratch.append(pltpu.VMEM((devices >> (phase + 1), rows, width), low))
    dense = len(chunks) * (experts + bits - 1)
    scratch = scratch + [
        pltpu.SemaphoreType.DMA((13,)),
        pltpu.SemaphoreType.DMA((experts,)),
        pltpu.SemaphoreType.DMA((experts,)),
        pltpu.SemaphoreType.DMA((dense,)),
        pltpu.SemaphoreType.DMA((dense,)),
        pltpu.SemaphoreType.DMA((2, half - 1)),
        pltpu.SemaphoreType.DMA((2, half - 1)),
        pltpu.SemaphoreType.DMA((3, reps)),
        pltpu.SemaphoreType.DMA((3, reps)),
        pltpu.SemaphoreType.DMA((3,)),
    ]
    call = pl.pallas_call(
        functools.partial(backward_kernel, experts, reps, chunks, summed),
        out_shape=[
            jax.ShapeDtypeStruct((SLOTS, D), low),
            jax.ShapeDtypeStruct((SLOTS, D), full),
            jax.ShapeDtypeStruct((rows if summed else D, 3 * D), full),
            jax.ShapeDtypeStruct((rows if summed else D, D), full),
            jax.ShapeDtypeStruct((rows if summed else D, LANES), full),
            jax.ShapeDtypeStruct((reps * piece, D), low),
            jax.ShapeDtypeStruct((D, reps * piece), low),
            jax.ShapeDtypeStruct((reps, tail_rows - piece, D), low),
        ],
        in_specs=[anywhere] * 4
        + [inside] * 3
        + [anywhere] * 8
        + [inside] * 4
        + [anywhere] * 2,
        out_specs=[inside] * 2 + [inside if summed else anywhere] * 3 + [anywhere] * 3,
        scratch_shapes=scratch,
        compiler_params=pltpu.CompilerParams(
            collective_id=1, has_side_effects=True, vmem_limit_bytes=63 * 1024 * 1024
        ),
        name="backward",
    )
    gradients = list(call(*operands))
    if not summed:
        for index in (2, 3, 4):
            gradients[index] = lax.psum_scatter(
                gradients[index], ("exp", "rep"), scatter_dimension=0, tiled=True
            )
    return gradients


def exchange(blocks):
    return lax.all_to_all(blocks, "exp", split_axis=0, concat_axis=0, tiled=True)


def on_device(
    tokens,
    ln1_gain,
    ln1_bias,
    w_qkv,
    w_out,
    ln2_gain,
    ln2_bias,
    w_router,
    w_in,
    b_in,
    w_back,
    b_back,
    lengths,
    routes,
    priority,
    padding,
    cotangent,
):
    experts = lax.axis_size("exp")
    reps = lax.axis_size("rep")
    devices = experts * reps
    capacity = (TOK_DEV * 210 + experts * 100 - 1) // (experts * 100)
    padded = -(-(capacity + 3) // 16) * 16
    rows = w_qkv.shape[0]
    small = jnp.concatenate(
        [w_router, jnp.stack([ln1_gain, ln1_bias, ln2_gain, ln2_bias], axis=1)], axis=1
    )
    small = jnp.pad(small, ((0, 0), (0, LANES - small.shape[1])))
    packed = jnp.concatenate([w_qkv, w_out, small], axis=1)
    gathered = gather_blocks(packed, devices, reps).reshape(D, packed.shape[1])
    qkv_weight = gathered[:, : 3 * D]
    out_weight = gathered[:, 3 * D : 4 * D]
    router_weight = gathered[:, 4 * D : 4 * D + experts]
    vectors = gathered[:, 4 * D + experts : 4 * D + experts + 4].T
    gain_one, bias_one, gain_two, bias_two = (vectors[0], vectors[1], vectors[2], vectors[3])

    first_hot, second_hot, pick_first, pick_second = dispatch_tables(
        routes, priority, padding, experts, capacity, padded
    )
    picks = pick_first + pick_second
    grad_blocks = lax.dot_general(picks, cotangent, contract_first, preferred_element_type=jnp.float32)
    grad_blocks = grad_blocks.astype(jnp.bfloat16).reshape(experts, padded, D)
    grad_blocks, gathered_done = lax.optimization_barrier((grad_blocks, qkv_weight))
    qkv_weight = gathered_done
    grad_arrived = exchange(grad_blocks)

    inputs = tokens.astype(jnp.float32)
    normed, normal_one, inverse_one = norm_forward(inputs, gain_one, bias_one)
    normed_low = normed.astype(jnp.bfloat16)
    qkv = (
        jnp.dot(normed_low, qkv_weight, preferred_element_type=jnp.float32)
        .astype(jnp.bfloat16)
        .reshape(ROWS_DEV, SLOTS, 3 * D)
    )
    bounds = jnp.cumsum(lengths[0])
    segments = jnp.sum(
        (jnp.arange(SLOTS, dtype=jnp.int32)[:, None] >= bounds[None, :]).astype(jnp.int32), axis=1
    )
    mixed_low = attend(qkv[0], segments, padding)
    resid = inputs + jnp.dot(mixed_low, out_weight, preferred_element_type=jnp.float32)
    routed_float, normal_two, inverse_two = norm_forward(resid, gain_two, bias_two)
    routed = routed_float.astype(jnp.bfloat16)
    logits = jnp.dot(routed, router_weight, preferred_element_type=jnp.float32)
    probs = jax.nn.softmax(logits, axis=-1)
    gate_first = jnp.sum(probs * first_hot, axis=1)
    gate_second = jnp.sum(probs * second_hot, axis=1)
    buffer = lax.dot_general(picks, routed, contract_first, preferred_element_type=jnp.float32)
    buffer = buffer.astype(jnp.bfloat16).reshape(experts, padded, D)
    slot_gates = jnp.sum(
        pick_first.astype(jnp.float32) * gate_first[:, None]
        + pick_second.astype(jnp.float32) * gate_second[:, None],
        axis=0,
    ).reshape(experts, padded)[:, :capacity]
    high = lax.reduce_precision(slot_gates, 8, 7)
    middle = lax.reduce_precision(slot_gates - high, 8, 7)
    terms = jnp.stack([high, middle, slot_gates - high - middle], axis=1).astype(jnp.bfloat16)
    terms = jnp.pad(terms, ((0, 0), (0, padded - capacity - 3), (0, D - capacity)))
    buffer = lax.dynamic_update_slice(buffer, terms, (0, capacity, 0))
    grad_buffer, result, half_back, half_in = run_experts(
        buffer, grad_arrived, w_in[0], w_back[0], b_in, b_back, capacity, reps
    )
    terms = grad_buffer[:, capacity : capacity + 3, :padded].transpose(1, 0, 2)
    terms = jnp.pad(terms.reshape(3, experts * padded), ((0, 13), (0, 0)))
    (
        output,
        grad_tokens,
        sum_qkv,
        sum_out,
        sum_small,
        all_back,
        all_in,
        all_tail,
    ) = run_backward(
        (
            grad_buffer.reshape(experts * padded, D),
            result,
            pick_first,
            pick_second,
            terms,
            jnp.pad(probs, ((0, 0), (0, LANES - experts))),
            routes,
            cotangent,
            resid,
            tokens,
            normed_low,
            routed,
            qkv[0],
            mixed_low,
            gathered,
            vectors.astype(jnp.float32),
            segments.reshape(SLOTS, 1),
            segments.reshape(1, SLOTS),
            padding.reshape(SLOTS, 1),
            half_back,
            half_in,
        ),
        experts,
        reps,
        rows,
    )
    vector_sums = sum_small[:, experts : experts + 4]
    hidden = b_in.shape[1]
    piece = hidden // reps
    return (
        output,
        grad_tokens,
        vector_sums[:, 0],
        vector_sums[:, 1],
        sum_qkv,
        sum_out,
        vector_sums[:, 2],
        vector_sums[:, 3],
        sum_small[:, :experts],
        all_in[None].astype(jnp.float32),
        all_tail[:, 0, :piece].astype(jnp.float32).reshape(1, hidden),
        all_back[None].astype(jnp.float32),
        all_tail[:1, 1, :].astype(jnp.float32),
    )


def solution(mesh):
    return jax.shard_map(
        on_device,
        mesh=mesh,
        in_specs=(
            P(("exp", "rep"), None),
            P(("exp", "rep")),
            P(("exp", "rep")),
            P(("exp", "rep"), None),
            P(("exp", "rep"), None),
            P(("exp", "rep")),
            P(("exp", "rep")),
            P(("exp", "rep"), None),
            P("exp", None, None),
            P("exp", None),
            P("exp", None, None),
            P("exp", None),
            P(("exp", "rep"), None),
            P(("exp", "rep"), None),
            P(("exp", "rep")),
            P(("exp", "rep")),
            P(("exp", "rep"), None),
        ),
        out_specs=(
            P(("exp", "rep"), None),
            P(("exp", "rep"), None),
            P(("exp", "rep")),
            P(("exp", "rep")),
            P(("exp", "rep"), None),
            P(("exp", "rep"), None),
            P(("exp", "rep")),
            P(("exp", "rep")),
            P(("exp", "rep"), None),
            P("exp", None, None),
            P("exp", None),
            P("exp", None, None),
            P("exp", None),
        ),
        check_vma=False,
    )
```

```python
import functools

import jax
import jax.numpy as jnp
from jax import lax
from jax.experimental import pallas as pl
from jax.experimental.pallas import tpu as pltpu
from jax.sharding import PartitionSpec as P

D = 768
HEADS = 12
HEAD = 64
SLOTS = 576
ROWS_DEV = 1
TOK_DEV = 576


root_half = 0.7071067811865476
inverse_root_tau = 0.3989422804014327
contract_first = (((0,), (0,)), ((), ()))
contract_last = (((1,), (1,)), ((), ()))


def norm_forward(inputs, gain, offset):
    center = inputs - jnp.mean(inputs, axis=-1, keepdims=True)
    inverse = lax.rsqrt(jnp.mean(center * center, axis=-1, keepdims=True) + 1e-06)
    normal = center * inverse
    return (normal * gain.astype(jnp.float32) + offset.astype(jnp.float32), normal, inverse)


def dispatch_tables(routes, priority, padding, experts, capacity, padded):
    labels = jnp.arange(experts, dtype=jnp.int32)
    first_hot = (routes[:, 0:1] == labels[None, :]).astype(jnp.bfloat16)
    second_hot = (routes[:, 1:2] == labels[None, :]).astype(jnp.bfloat16)
    live = padding[:, None].astype(jnp.bfloat16)
    earlier = (priority[None, :] < priority[:, None]).astype(jnp.bfloat16)
    before_first = jnp.dot(earlier, first_hot * live, preferred_element_type=jnp.float32)
    first_counts = jnp.sum((first_hot * live).astype(jnp.float32), axis=0)
    before_second = (
        jnp.dot(earlier, second_hot * live, preferred_element_type=jnp.float32)
        + first_counts[None, :]
    )
    place_first = jnp.sum(before_first * first_hot, axis=1).astype(jnp.int32)
    place_second = jnp.sum(before_second * second_hot, axis=1).astype(jnp.int32)
    kept_first = (padding == 1) & (place_first < capacity)
    kept_second = (padding == 1) & (place_second < capacity)
    slot_labels = jnp.arange(experts * padded, dtype=jnp.int32)
    slot_first = routes[:, 0] * padded + place_first
    slot_second = routes[:, 1] * padded + place_second
    pick_first = ((slot_first[:, None] == slot_labels[None, :]) & kept_first[:, None]).astype(
        jnp.bfloat16
    )
    pick_second = ((slot_second[:, None] == slot_labels[None, :]) & kept_second[:, None]).astype(
        jnp.bfloat16
    )
    return (first_hot.astype(jnp.float32), second_hot.astype(jnp.float32), pick_first, pick_second)


LANES = 128
MESH_ID = pl.DeviceIdType.MESH


def bit_count(number):
    return number.bit_length() - 1


def flip(position, bit):
    step = 1 << bit
    return position + (1 - 2 * lax.rem(lax.div(position, step), 2)) * step


def coordinates(position, reps):
    return (lax.div(position, reps), lax.rem(position, reps))


def greet(bits, me, reps):
    barrier = pltpu.get_barrier_semaphore()
    for bit in range(bits):
        pl.semaphore_signal(
            barrier, inc=1, device_id=coordinates(flip(me, bit), reps), device_id_type=MESH_ID
        )
    pl.semaphore_wait(barrier, bits)


def lowest_bit(number):
    return (number & -number).bit_length() - 1


def gather_kernel(devices, reps, own_ref, all_ref, send_sem, recv_sem, local_sem):
    bits = bit_count(devices)
    me = lax.axis_index("exp") * reps + lax.axis_index("rep")
    greet(bits, me, reps)
    local = pltpu.make_async_copy(own_ref, all_ref.at[me], local_sem)
    local.start()

    def owner_of(distance):
        found = me
        for bit in range(bits):
            if distance >> bit & 1:
                found = flip(found, bit)
        return found

    def transfer(source_ref, distance, bit):
        owner = owner_of(distance)
        index = distance + (1 << bit)
        return pltpu.make_async_remote_copy(
            src_ref=source_ref,
            dst_ref=all_ref.at[owner],
            send_sem=send_sem.at[index],
            recv_sem=recv_sem.at[index],
            device_id=coordinates(flip(me, bit), reps),
            device_id_type=MESH_ID,
        )

    def arrival(distance):
        owner = owner_of(distance)
        return pltpu.make_async_remote_copy(
            src_ref=all_ref.at[owner],
            dst_ref=all_ref.at[owner],
            send_sem=send_sem.at[distance],
            recv_sem=recv_sem.at[distance],
            device_id=coordinates(flip(me, lowest_bit(distance)), reps),
            device_id_type=MESH_ID,
        )

    sent = []
    for bit in range(bits):
        copy = transfer(own_ref, 0, bit)
        copy.start()
        sent.append(copy)
    order = sorted(range(1, devices), key=lambda d: (bin(d).count("1"), -d))
    last = []
    for distance in order:
        low = lowest_bit(distance)
        if low == 0:
            last.append(distance)
            continue
        arrival(distance).wait_recv()
        for bit in range(low):
            copy = transfer(all_ref.at[owner_of(distance)], distance, bit)
            copy.start()
            sent.append(copy)
    for distance in last:
        arrival(distance).wait_recv()
    for copy in sent:
        copy.wait_send()
    local.wait()


def gather_blocks(block, devices, reps):
    return pl.pallas_call(
        functools.partial(gather_kernel, devices, reps),
        out_shape=jax.ShapeDtypeStruct((devices,) + block.shape, block.dtype),
        in_specs=[pl.BlockSpec(memory_space=pl.ANY)],
        out_specs=pl.BlockSpec(memory_space=pl.ANY),
        scratch_shapes=[
            pltpu.SemaphoreType.DMA((devices,)),
            pltpu.SemaphoreType.DMA((devices,)),
            pltpu.SemaphoreType.DMA,
        ],
        compiler_params=pltpu.CompilerParams(collective_id=0, has_side_effects=True),
        name="gather_dense",
    )(block)


def row_of(column, width):
    count = column.shape[0]
    down = lax.broadcasted_iota(jnp.int32, (count, width), 0)
    across = lax.broadcasted_iota(jnp.int32, (count, width), 1)
    return jnp.sum(jnp.where(down == across, column, 0.0), axis=0, keepdims=True)


def column_of(row, count):
    width = row.shape[1]
    down = lax.broadcasted_iota(jnp.int32, (count, width), 0)
    across = lax.broadcasted_iota(jnp.int32, (count, width), 1)
    return jnp.sum(jnp.where(down == across, row, 0.0), axis=1, keepdims=True)


def three_terms(value):
    high = value.astype(jnp.bfloat16).astype(jnp.float32)
    rest = value - high
    middle = rest.astype(jnp.bfloat16).astype(jnp.float32)
    return (high, middle, rest - middle)


def expert_kernel(
    experts,
    capacity,
    padded,
    block,
    send_ref,
    grad_ref,
    w_in_ref,
    w_back_ref,
    b_in_ref,
    b_back_ref,
    return_ref,
    result_ref,
    half_back_ref,
    half_in_ref,
    slots,
    grads,
    gated,
    weight_in,
    weight_back,
    active,
    grad_pre,
    back_rows,
    result_rows,
    result_total,
    back_total,
    away_back,
    away_in,
    other_back,
    other_in,
    came_back,
    load_sem,
    send_sem,
    recv_sem,
    return_send_sem,
    return_recv_sem,
    result_sem,
    core_send,
    core_recv,
    along_send,
    along_recv,
    stage_sem,
):
    mine = lax.axis_index("exp")
    rep = lax.axis_index("rep")
    bits = bit_count(experts)
    groups = experts // 2
    hidden = weight_in.shape[1]
    steps = hidden // block
    lanes = 256 if capacity <= 256 else D
    gate_row = capacity - (padded - 16)

    barrier = pltpu.get_barrier_semaphore()

    def greet_one(step, carry):
        other = lax.rem(mine + step, experts)
        pl.semaphore_signal(barrier, inc=1, device_id=(other, rep), device_id_type=MESH_ID)
        return carry

    lax.fori_loop(1, experts, greet_one, 0)
    core = lax.rem(rep, 2)
    partner = (mine, flip(rep, 0))
    pl.semaphore_signal(barrier, inc=1, device_id=partner, device_id_type=MESH_ID)
    half = away_in.shape[0]
    along = lax.div(rep, 2)

    def greet_along(step, carry):
        other = 2 * lax.rem(along + step, half) + core
        pl.semaphore_signal(barrier, inc=1, device_id=(mine, other), device_id_type=MESH_ID)
        return carry

    lax.fori_loop(1, half, greet_along, 0)

    def group_of(index):
        half = lax.div(mine, 2)
        found = half
        for bit in range(bits - 1):
            found = found + lax.rem(lax.div(index, 1 << bit), 2) * (
                (1 - 2 * lax.rem(lax.div(half, 1 << bit), 2)) * (1 << bit)
            )
        return found

    def place(expert):
        return pl.ds(pl.multiple_of(expert * padded, 16), padded)

    def outgoing(expert):
        return pltpu.make_async_remote_copy(
            src_ref=send_ref.at[expert],
            dst_ref=slots.at[place(mine)],
            send_sem=send_sem.at[expert],
            recv_sem=recv_sem.at[mine],
            device_id=(expert, rep),
            device_id_type=MESH_ID,
        )

    def incoming(expert):
        return pltpu.make_async_remote_copy(
            src_ref=send_ref.at[mine],
            dst_ref=slots.at[place(expert)],
            send_sem=send_sem.at[expert],
            recv_sem=recv_sem.at[expert],
            device_id=(expert, rep),
            device_id_type=MESH_ID,
        )

    def going_back(expert):
        return pltpu.make_async_remote_copy(
            src_ref=back_rows.at[place(expert)],
            dst_ref=return_ref.at[mine],
            send_sem=return_send_sem.at[expert],
            recv_sem=return_recv_sem.at[mine],
            device_id=(expert, rep),
            device_id_type=MESH_ID,
        )

    def coming_back(expert):
        return pltpu.make_async_remote_copy(
            src_ref=back_rows.at[place(expert)],
            dst_ref=return_ref.at[expert],
            send_sem=return_send_sem.at[expert],
            recv_sem=return_recv_sem.at[expert],
            device_id=(expert, rep),
            device_id_type=MESH_ID,
        )

    neighbour = flip(mine, 0)
    side = lax.rem(mine, 2)
    loads = [
        pltpu.make_async_copy(send_ref.at[mine], slots.at[place(mine)], load_sem.at[0]),
        pltpu.make_async_copy(grad_ref, grads, load_sem.at[1]),
        pltpu.make_async_copy(w_in_ref, weight_in, load_sem.at[2]),
        pltpu.make_async_copy(w_back_ref, weight_back, load_sem.at[3]),
    ]
    for copy in loads:
        copy.start()
    pl.semaphore_wait(barrier, experts + half - 1)

    def send_group(index):
        pair = group_of(index)
        outgoing(2 * pair + side).start()
        outgoing(2 * pair + 1 - side).start()

    half_pair = lax.div(mine, 2)
    inner = lax.rem(lax.rem(half_pair, 2) + lax.div(half_pair, 2), 2)

    def turn(index):
        if groups != 4:
            return index
        high, low = (lax.div(index, 2), lax.rem(index, 2))
        return inner * (2 * high + lax.rem(low + high, 2)) + (1 - inner) * (2 * low + high)

    outgoing(neighbour).start()

    def send_step(step, carry):
        if groups == 4:
            send_group(inner * (lax.rem(step + 1, 3) + 1) + (1 - inner) * (step + 1))
        else:
            send_group(step + 1)
        return carry

    lax.fori_loop(0, groups - 1, send_step, 0)
    for copy in loads:
        copy.wait()

    def send_back_group(index):
        pair = group_of(index)
        going_back(2 * pair + side).start()
        going_back(2 * pair + 1 - side).start()

    def gate_columns(expert):
        tail = slots[pl.ds(pl.multiple_of(expert * padded + padded - 16, 16), 16), :].astype(jnp.float32)
        row = jnp.sum(tail[gate_row : gate_row + 3, :lanes], axis=0, keepdims=True)
        return column_of(row, padded)

    def group_step(index, carry):
        pair = group_of(turn(index))

        @pl.when(index == 0)
        def _():
            incoming(neighbour).wait_recv()

        @pl.when(index > 0)
        def _():
            incoming(2 * pair).wait_recv()
            incoming(2 * pair + 1).wait_recv()

        @pl.when(index == 1)
        def _():
            going_back(neighbour).start()

        @pl.when(index > 1)
        def _():
            send_back_group(turn(index - 1))

        here = pl.ds(pl.multiple_of(pair * 2 * padded, 16), 2 * padded)
        for member in range(2):
            spot = place(2 * pair + member)
            gate = gate_columns(2 * pair + member)
            gated[spot, :] = (gate * grads[spot, :].astype(jnp.float32)).astype(jnp.bfloat16)

        def hidden_step(step, inner):
            columns = pl.ds(pl.multiple_of(step * block, block), block)
            pre = (
                jnp.dot(slots[here, :], weight_in[:, columns], preferred_element_type=jnp.float32)
                + b_in_ref[:, columns]
            )
            grad_active = lax.dot_general(
                gated[here, :],
                weight_back[columns, :],
                contract_last,
                preferred_element_type=jnp.float32,
            )
            cumulative = 0.5 * (1.0 + lax.erf(pre * root_half))
            slope = cumulative + pre * inverse_root_tau * jnp.exp(-0.5 * pre * pre)
            active_low = (pre * cumulative).astype(jnp.bfloat16)
            grad_low = (grad_active * slope).astype(jnp.bfloat16)
            active[here, columns] = active_low
            grad_pre[here, columns] = grad_low
            result_part = jnp.dot(
                active_low, weight_back[columns, :], preferred_element_type=jnp.float32
            )
            back_part = lax.dot_general(
                grad_low, weight_in[:, columns], contract_last, preferred_element_type=jnp.float32
            )

            @pl.when(step == 0)
            def _():
                result_total[...] = result_part
                back_total[...] = back_part

            @pl.when(step > 0)
            def _():
                result_total[...] += result_part
                back_total[...] += back_part

            return inner

        lax.fori_loop(0, steps, hidden_step, 0)
        for member in range(2):
            expert = 2 * pair + member
            span = slice(member * padded, (member + 1) * padded)
            spot = place(expert)
            result_low = (result_total[span, :] + b_back_ref[...]).astype(jnp.bfloat16)
            result_rows[spot, :] = result_low
            grad_gate = jnp.sum(
                grads[spot, :].astype(jnp.float32) * result_low.astype(jnp.float32),
                axis=1,
                keepdims=True,
            )
            gate_line = row_of(
                jnp.where(
                    lax.broadcasted_iota(jnp.int32, (padded, 1), 0) < capacity, grad_gate, 0.0
                ),
                lanes,
            )
            if lanes < D:
                gate_line = jnp.concatenate(
                    [gate_line, jnp.zeros((1, D - lanes), jnp.float32)], axis=1
                )
            high, middle, lowest = three_terms(gate_line)
            row = lax.broadcasted_iota(jnp.int32, (padded, D), 0)
            value = back_total[span, :]
            value = jnp.where(row == capacity, high, value)
            value = jnp.where(row == capacity + 1, middle, value)
            value = jnp.where(row == capacity + 2, lowest, value)
            back_rows[spot, :] = value.astype(jnp.bfloat16)
        return carry

    lax.fori_loop(0, groups, group_step, 0)
    own_back = pltpu.make_async_copy(back_rows.at[place(mine)], return_ref.at[mine], load_sem.at[0])
    own_back.start()
    results = pltpu.make_async_copy(result_rows, result_ref, result_sem)
    results.start()

    piece = away_in.shape[2]
    bias_back = jnp.sum(gated[...].astype(jnp.float32), axis=0, keepdims=True)

    def columns_of(number):
        return pl.ds(pl.multiple_of(number * piece, LANES), piece)

    def back_sums(number):
        columns = columns_of(number)
        back = lax.dot_general(
            active[:, columns], gated[...], contract_first, preferred_element_type=jnp.float32
        )
        bias_in = jnp.sum(grad_pre[:, columns].astype(jnp.float32), axis=0, keepdims=True)
        if piece < D:
            bias_in = jnp.concatenate([bias_in, jnp.zeros((1, D - piece), jnp.float32)], axis=1)
        row = lax.broadcasted_iota(jnp.int32, (16, D), 0)
        extra = jnp.where(row == 0, bias_in, jnp.where(row == 1, bias_back, 0.0))
        return (back, extra)

    def in_sums(number):
        return lax.dot_general(
            slots[...],
            grad_pre[:, columns_of(number)],
            contract_first,
            preferred_element_type=jnp.float32,
        )

    def core_copy(kind, index):
        source, target = ((away_back, other_back), (away_in, other_in))[kind]
        return pltpu.make_async_remote_copy(
            src_ref=source.at[index],
            dst_ref=target.at[index],
            send_sem=core_send.at[kind, index],
            recv_sem=core_recv.at[kind, index],
            device_id=partner,
            device_id_type=MESH_ID,
        )

    def along_copy(step):
        other = lax.rem(along + step, half)
        return pltpu.make_async_remote_copy(
            src_ref=other_back.at[other],
            dst_ref=came_back.at[step - 1],
            send_sem=along_send.at[step - 1],
            recv_sem=along_recv.at[step - 1],
            device_id=(mine, 2 * other + core),
            device_id_type=MESH_ID,
        )

    def away_back_step(step, carry):
        index = lax.rem(along + step, half)
        back, extra = back_sums(2 * index + 1 - core)
        away_back[index, :piece, :] = back.astype(jnp.bfloat16)
        away_back[index, piece:, :] = extra.astype(jnp.bfloat16)
        core_copy(0, index).start()
        return carry

    def kept_back_step(step, carry):
        index = lax.rem(along + step, half)
        back, extra = back_sums(2 * index + core)
        core_copy(0, index).wait_recv()
        other_back[index, :piece, :] = (
            back + other_back[index, :piece, :].astype(jnp.float32)
        ).astype(jnp.bfloat16)
        other_back[index, piece:, :] = (
            extra + other_back[index, piece:, :].astype(jnp.float32)
        ).astype(jnp.bfloat16)

        @pl.when(step < half)
        def _():
            along_copy(step).start()

        return carry

    def away_in_step(index, carry):
        away_in[index] = in_sums(2 * index + 1 - core).astype(jnp.bfloat16)
        core_copy(1, index).start()
        return carry

    def kept_in_copy(index):
        return pltpu.make_async_copy(other_in.at[index], half_in_ref.at[index], stage_sem.at[index])

    def kept_in_step(index, carry):
        inward = in_sums(2 * index + core)
        core_copy(1, index).wait_recv()
        other_in[index] = (inward + other_in[index].astype(jnp.float32)).astype(jnp.bfloat16)
        kept_in_copy(index).start()
        return carry

    lax.fori_loop(1, half + 1, away_back_step, 0)
    if groups > 1:
        send_back_group(turn(groups - 1))
    else:
        going_back(neighbour).start()
    lax.fori_loop(1, half + 1, kept_back_step, 0)
    lax.fori_loop(0, half, away_in_step, 0)
    lax.fori_loop(0, half, kept_in_step, 0)
    for step in range(1, half):
        along_copy(step).wait_recv()

    def along_sum(step, carry):
        here = pl.ds(pl.multiple_of(step * 16, 16), 16)
        total = other_back[along, here, :].astype(jnp.float32)
        for came in range(half - 1):
            total = total + came_back[came, here, :].astype(jnp.float32)
        other_back[along, here, :] = total.astype(jnp.bfloat16)
        return carry

    lax.fori_loop(0, (piece + 16) // 16, along_sum, 0)
    sum_back = pltpu.make_async_copy(other_back.at[along], half_back_ref, stage_sem.at[half])
    sum_back.start()
    sum_back.wait()
    for step in range(1, half):
        along_copy(step).wait_send()
    for index in range(half):
        kept_in_copy(index).wait()
        for kind in range(2):
            core_copy(kind, index).wait_send()
    own_back.wait()
    results.wait()

    def finish(step, carry):
        other = lax.rem(mine + step, experts)
        outgoing(other).wait_send()
        going_back(other).wait_send()
        coming_back(other).wait_recv()
        return carry

    lax.fori_loop(1, experts, finish, 0)


def run_experts(buffer, grads, w_in, w_back, b_in, b_back, capacity, reps):
    experts, padded = (buffer.shape[0], buffer.shape[1])
    hidden = w_in.shape[1]
    block = 512
    rows = experts * padded
    half = reps // 2
    piece = hidden // reps
    low = jnp.bfloat16
    anywhere = pl.BlockSpec(memory_space=pl.ANY)
    inside = pl.BlockSpec(memory_space=pltpu.VMEM)
    return pl.pallas_call(
        functools.partial(expert_kernel, experts, capacity, padded, block),
        out_shape=[
            jax.ShapeDtypeStruct((experts, padded, D), low),
            jax.ShapeDtypeStruct((rows, D), low),
            jax.ShapeDtypeStruct((piece + 16, D), low),
            jax.ShapeDtypeStruct((half, D, piece), low),
        ],
        in_specs=[anywhere, anywhere, anywhere, anywhere, inside, inside],
        out_specs=[anywhere, anywhere, anywhere, anywhere],
        scratch_shapes=[
            pltpu.VMEM((rows, D), low),
            pltpu.VMEM((rows, D), low),
            pltpu.VMEM((rows, D), low),
            pltpu.VMEM((D, hidden), low),
            pltpu.VMEM((hidden, D), low),
            pltpu.VMEM((rows, hidden), low),
            pltpu.VMEM((rows, hidden), low),
            pltpu.VMEM((rows, D), low),
            pltpu.VMEM((rows, D), low),
            pltpu.VMEM((2 * padded, D), jnp.float32),
            pltpu.VMEM((2 * padded, D), jnp.float32),
            pltpu.VMEM((half, piece + 16, D), low),
            pltpu.VMEM((half, D, piece), low),
            pltpu.VMEM((half, piece + 16, D), low),
            pltpu.VMEM((half, D, piece), low),
            pltpu.VMEM((half - 1, piece + 16, D), low),
            pltpu.SemaphoreType.DMA((4,)),
            pltpu.SemaphoreType.DMA((experts,)),
            pltpu.SemaphoreType.DMA((experts,)),
            pltpu.SemaphoreType.DMA((experts,)),
            pltpu.SemaphoreType.DMA((experts,)),
            pltpu.SemaphoreType.DMA,
            pltpu.SemaphoreType.DMA((2, half)),
            pltpu.SemaphoreType.DMA((2, half)),
            pltpu.SemaphoreType.DMA((half - 1,)),
            pltpu.SemaphoreType.DMA((half - 1,)),
            pltpu.SemaphoreType.DMA((half + 1,)),
        ],
        compiler_params=pltpu.CompilerParams(
            collective_id=2, has_side_effects=True, vmem_limit_bytes=63 * 1024 * 1024
        ),
        cost_estimate=pl.CostEstimate(
            flops=12 * rows * D * hidden, bytes_accessed=40 << 20, transcendentals=2 * rows * hidden
        ),
        name="experts",
    )(buffer, grads.reshape(rows, D), w_in, w_back, b_in.astype(jnp.float32), b_back.astype(jnp.float32))


def attend_kernel(segment_col, segment_row, live_row, query_ref, keys_ref, values_ref, mixed_ref, bias):
    @pl.when(pl.program_id(0) == 0)
    def _():
        row = lax.broadcasted_iota(jnp.int32, (SLOTS, SLOTS), 0)
        column = lax.broadcasted_iota(jnp.int32, (SLOTS, SLOTS), 1)
        seen = (segment_col[...] == segment_row[...]) & ((live_row[...] == 1) | (row == column))
        bias[...] = jnp.where(seen, 0.0, -1e30)

    for side in range(2):
        lanes = slice(side * HEAD, (side + 1) * HEAD)
        scores = lax.dot_general(
            query_ref[:, lanes], keys_ref[:, lanes], contract_last, preferred_element_type=jnp.float32
        )
        scores = scores * HEAD ** (-0.5) + bias[...]
        expo = jnp.exp(scores - jnp.max(scores, axis=1, keepdims=True))
        total = jnp.sum(expo, axis=1, keepdims=True)
        probs = (expo * (1.0 / total)).astype(jnp.bfloat16)
        mixed = jnp.dot(probs, values_ref[:, lanes], preferred_element_type=jnp.float32)
        mixed_ref[:, lanes] = mixed.astype(jnp.bfloat16)


def attend(qkv, segments, live):
    pairs = HEADS // 2
    return pl.pallas_call(
        attend_kernel,
        grid=(pairs,),
        out_shape=jax.ShapeDtypeStruct((SLOTS, D), jnp.bfloat16),
        in_specs=[
            pl.BlockSpec((SLOTS, 1), lambda i: (0, 0)),
            pl.BlockSpec((1, SLOTS), lambda i: (0, 0)),
            pl.BlockSpec((1, SLOTS), lambda i: (0, 0)),
            pl.BlockSpec((SLOTS, 2 * HEAD), lambda i: (0, i)),
            pl.BlockSpec((SLOTS, 2 * HEAD), lambda i: (0, pairs + i)),
            pl.BlockSpec((SLOTS, 2 * HEAD), lambda i: (0, 2 * pairs + i)),
        ],
        out_specs=pl.BlockSpec((SLOTS, 2 * HEAD), lambda i: (0, i)),
        scratch_shapes=[pltpu.VMEM((SLOTS, SLOTS), jnp.float32)],
        cost_estimate=pl.CostEstimate(
            flops=16 * HEADS * SLOTS * SLOTS * HEAD, bytes_accessed=4 << 20, transcendentals=HEADS * SLOTS * SLOTS
        ),
        name="attend",
    )(segments.reshape(SLOTS, 1), segments.reshape(1, SLOTS), live.reshape(1, SLOTS), qkv, qkv, qkv)


BAND = 48


def fold_rows(values):
    return jnp.sum(values.reshape(BAND // 8, 8, values.shape[1]), axis=0)


def backward_kernel(
    experts,
    reps,
    chunks,
    summed,
    back_ref,
    result_ref,
    first_ref,
    second_ref,
    terms_ref,
    probs_ref,
    routes_ref,
    cotangent_ref,
    resid_ref,
    tokens_ref,
    normed_ref,
    routed_ref,
    qkv_ref,
    mixed_ref,
    weights_ref,
    vectors_ref,
    segment_col,
    segment_row,
    live_col,
    half_back_ref,
    half_in_ref,
    output_ref,
    grad_tokens_ref,
    sum_qkv_ref,
    sum_out_ref,
    sum_small_ref,
    all_back_ref,
    all_in_ref,
    all_tail_ref,
    *refs,
):
    devices = experts * reps
    bits = bit_count(devices)
    half = reps // 2
    mine = lax.axis_index("exp")
    rep = lax.axis_index("rep")
    me = mine * reps + rep
    core = lax.rem(rep, 2)
    along = lax.div(rep, 2)
    (
        back,
        first,
        second,
        cotangent,
        resid,
        tokens,
        normed,
        routed,
        qkv,
        mixed,
        weights,
        returned,
        bias,
        wide,
        tall,
        grad_resid,
        grad_attn,
        grad_mixed,
        grad_qkv,
        grad_logits,
        own_in,
        other_in,
    ) = refs[:22]
    refs = refs[22:]
    lines, refs = (refs[0], refs[1:])
    count = len(chunks) if summed else 0
    parts, refs = (refs[:count], refs[count:])
    recvs, refs = ([refs[c * bits : (c + 1) * bits] for c in range(count)], refs[count * bits :])
    (
        load_sem,
        result_send,
        result_recv,
        dense_send,
        dense_recv,
        half_send,
        half_recv,
        all_send,
        all_recv,
        own_sem,
    ) = refs
    padded = result_ref.shape[0] // experts
    piece = half_in_ref.shape[2]

    barrier = pltpu.get_barrier_semaphore()

    def greet_expert(step, carry):
        other = lax.rem(mine + step, experts)
        pl.semaphore_signal(barrier, inc=1, device_id=(other, rep), device_id_type=MESH_ID)
        return carry

    def greet_rep(step, carry):
        other = lax.rem(rep + step, reps)
        pl.semaphore_signal(barrier, inc=1, device_id=(mine, other), device_id_type=MESH_ID)
        return carry

    lax.fori_loop(1, experts, greet_expert, 0)
    lax.fori_loop(1, reps, greet_rep, 0)

    sources = [
        (back_ref, back),
        (first_ref, first),
        (second_ref, second),
        (routed_ref, routed),
        (weights_ref, weights),
        (resid_ref, resid),
        (cotangent_ref, cotangent),
        (mixed_ref, mixed),
        (qkv_ref, qkv),
        (normed_ref, normed),
        (tokens_ref, tokens),
        (half_in_ref.at[along], own_in),
    ]
    loads = [
        pltpu.make_async_copy(source, target, load_sem.at[i])
        for i, (source, target) in enumerate(sources)
    ]
    for copy in loads:
        copy.start()
    pl.semaphore_wait(barrier, experts - 1 + reps - 1)

    def half_copy(step):
        other = lax.rem(along + step, half)
        return pltpu.make_async_remote_copy(
            src_ref=half_in_ref.at[other],
            dst_ref=other_in.at[step - 1],
            send_sem=half_send.at[step - 1],
            recv_sem=half_recv.at[step - 1],
            device_id=(mine, 2 * other + core),
            device_id_type=MESH_ID,
        )

    half_moves = [half_copy(step) for step in range(1, half)]
    for move in half_moves:
        move.start()

    def own_part(kind):
        return (half_back_ref.at[pl.ds(0, piece), :], own_in, half_back_ref.at[pl.ds(piece, 16), :])[kind]

    def landing(kind, owner):
        if kind == 0:
            return all_back_ref.at[pl.ds(pl.multiple_of(owner * piece, 16), piece), :]
        if kind == 1:
            return all_in_ref.at[:, pl.ds(pl.multiple_of(owner * piece, LANES), piece)]
        return all_tail_ref.at[owner]

    def spread(kind, source, owner, device, step):
        return pltpu.make_async_remote_copy(
            src_ref=source,
            dst_ref=landing(kind, owner),
            send_sem=all_send.at[kind, step],
            recv_sem=all_recv.at[kind, step],
            device_id=device,
            device_id_type=MESH_ID,
        )

    def own_moves(kind):
        moves = [pltpu.make_async_copy(own_part(kind), landing(kind, rep), own_sem.at[kind])]
        for step in range(1, half):
            other = lax.rem(along + step, half)
            moves.append(spread(kind, own_part(kind), rep, (mine, 2 * other + core), step))
        moves.append(spread(kind, own_part(kind), rep, (mine, flip(rep, 0)), 0))
        return moves

    for kind in (0, 2):
        for move in own_moves(kind):
            move.start()

    def place(expert):
        return pl.ds(pl.multiple_of(expert * padded, 16), padded)

    def result_copy(step):
        other = lax.rem(mine + step, experts)
        came = lax.rem(mine + experts - step, experts)
        return pltpu.make_async_remote_copy(
            src_ref=result_ref.at[place(other)],
            dst_ref=returned.at[place(mine)],
            send_sem=result_send.at[step],
            recv_sem=result_recv.at[step],
            device_id=(other, rep),
            device_id_type=MESH_ID,
        )

    def start_result(step, carry):
        result_copy(step).start()
        return carry

    own_result = pltpu.make_async_copy(
        result_ref.at[place(mine)], returned.at[place(mine)], result_send.at[0]
    )
    own_result.start()
    lax.fori_loop(1, experts, start_result, 0)

    row = lax.broadcasted_iota(jnp.int32, (SLOTS, SLOTS), 0)
    column = lax.broadcasted_iota(jnp.int32, (SLOTS, SLOTS), 1)
    seen = (segment_col[...] == segment_row[...]) & ((live_col[...] == 1) | (row == column))
    bias[...] = jnp.where(seen, 0.0, -1e30)

    for copy in loads[:5]:
        copy.wait()
    tall[...] = jnp.dot(first[...] + second[...], back[...], preferred_element_type=jnp.float32)
    gates_back = [
        jnp.sum(
            lax.dot_general(
                pick[...], terms_ref[...], contract_last, preferred_element_type=jnp.float32
            ),
            axis=1,
            keepdims=True,
        )
        for pick in (first, second)
    ]
    lane = lax.broadcasted_iota(jnp.int32, (SLOTS, LANES), 1)
    hots = [(lane == routes_ref[:, k : k + 1]).astype(jnp.float32) for k in range(2)]
    grad_probs = gates_back[0] * hots[0] + gates_back[1] * hots[1]
    probs = probs_ref[...]
    grad_logits[...] = (
        probs * (grad_probs - jnp.sum(probs * grad_probs, axis=1, keepdims=True))
    ).astype(jnp.bfloat16)
    tall[...] += lax.dot_general(
        grad_logits[...], weights[:, 4 * D :], contract_last, preferred_element_type=jnp.float32
    )
    for copy in loads[5:]:
        copy.wait()

    def band(step):
        return pl.ds(pl.multiple_of(step * BAND, 16), BAND)

    def norm_back(inputs, grad, gain):
        center = inputs - jnp.mean(inputs, axis=1, keepdims=True)
        inverse = lax.rsqrt(jnp.mean(center * center, axis=1, keepdims=True) + 1e-06)
        normal = center * inverse
        scaled = grad * gain
        grad_in = inverse * (
            scaled
            - jnp.mean(scaled, axis=1, keepdims=True)
            - normal * jnp.mean(scaled * normal, axis=1, keepdims=True)
        )
        return (grad_in, fold_rows(grad * normal), fold_rows(grad))

    zero = jnp.zeros((8, D), jnp.float32)

    def second_norm(step, carry):
        here = band(step)
        grad_in, grad_gain, grad_bias = norm_back(
            resid[here, :], tall[here, :], vectors_ref[2:3, :]
        )
        total = cotangent[here, :].astype(jnp.float32) + grad_in
        grad_resid[here, :] = total
        grad_attn[here, :] = total.astype(jnp.bfloat16)
        return (carry[0] + grad_gain, carry[1] + grad_bias)

    gain_two, bias_two = lax.fori_loop(0, SLOTS // BAND, second_norm, (zero, zero))

    lines[16:24, :] = gain_two
    lines[24:32, :] = bias_two

    own_bits = bit_count(reps)
    plan = [0] + list(range(own_bits, bits)) + list(range(own_bits - 1, 0, -1))
    my_bit = [lax.rem(lax.div(me, 1 << bit), 2) for bit in range(bits)]
    rows = parts[0].shape[4] if summed else 0
    stride = experts + bits - 1
    first_of = [sum(number for number, _ in chunks[:family]) for family in range(len(chunks))]

    def turned(number):
        length = bits - own_bits - 1
        found = 0
        for bit in range(length):
            found = found + lax.rem(lax.div(number, 1 << bit), 2) * (1 << (length - 1 - bit))
        return found

    def fill(family, c):
        width = chunks[family][1]

        def one(block, carry):
            owner = lax.div(block, reps)
            inner = lax.rem(block, reps)
            parts[family][c, owner, lax.div(inner, 2), lax.rem(inner, 2)] = wide[
                pl.ds(pl.multiple_of(block * rows, rows), rows), :width
            ].astype(jnp.bfloat16)
            return carry

        lax.fori_loop(0, devices, one, 0)

    def first_copy(family, c, expert):
        spot = lax.rem(expert, 2) * (devices // 4) + turned(lax.div(expert, 2)) * half
        index = (first_of[family] + c) * stride + expert
        return pltpu.make_async_remote_copy(
            src_ref=parts[family].at[c, expert, :, 1 - core],
            dst_ref=recvs[family][0].at[c, pl.ds(spot, half)],
            send_sem=dense_send.at[index],
            recv_sem=dense_recv.at[index],
            device_id=(mine, flip(rep, 0)),
            device_id_type=MESH_ID,
        )

    def later_copy(family, c, phase):
        size = devices >> (phase + 1)
        index = (first_of[family] + c) * stride + experts + phase - 1
        return pltpu.make_async_remote_copy(
            src_ref=recvs[family][phase - 1].at[c, pl.ds((1 - my_bit[plan[phase]]) * size, size)],
            dst_ref=recvs[family][phase].at[c],
            send_sem=dense_send.at[index],
            recv_sem=dense_recv.at[index],
            device_id=coordinates(flip(me, plan[phase]), reps),
            device_id_type=MESH_ID,
        )

    def columns_of(c, kind):
        return pl.ds(pl.multiple_of(c * LANES + kind * D, LANES), LANES)

    def send_chunk(family, c):
        if not summed:
            if family == 1:
                for kind in range(3):
                    span = slice(kind * LANES, (kind + 1) * LANES)
                    pltpu.sync_copy(wide.at[:, span], sum_qkv_ref.at[:, columns_of(c, kind)])
            else:
                out = sum_out_ref if family == 0 else sum_small_ref
                pltpu.sync_copy(wide.at[:, : chunks[family][1]], out)
            return
        fill(family, c)

        def one(expert, carry):
            first_copy(family, c, expert).start()
            return carry

        lax.fori_loop(0, experts, one, 0)

    def absorb(family, c, phase):
        if not summed:
            return
        size = devices >> (phase + 1)
        into = recvs[family][phase]
        if phase == 0:

            def arrived(expert, carry):
                first_copy(family, c, expert).wait_recv()
                return carry

            lax.fori_loop(0, experts, arrived, 0)

            def held(i):
                side = lax.div(i, devices // 4)
                rest = lax.rem(i, devices // 4)
                expert = 2 * turned(lax.div(rest, half)) + side
                return parts[family][c, expert, lax.rem(rest, half), core]
        else:
            later_copy(family, c, phase).wait_recv()
            base = my_bit[plan[phase]] * size

            def held(i):
                return recvs[family][phase - 1][c, base + i]

        if phase == bits - 1:
            total = into[c, 0].astype(jnp.float32) + held(0).astype(jnp.float32)
            if family == 1:
                for kind in range(3):
                    sum_qkv_ref[:, columns_of(c, kind)] = total[:, kind * LANES : (kind + 1) * LANES]
            elif family == 0:
                sum_out_ref[...] = total
            else:
                sum_small_ref[...] = total
            return

        def one(i, carry):
            into[c, i] = (into[c, i].astype(jnp.float32) + held(i).astype(jnp.float32)).astype(
                jnp.bfloat16
            )
            return carry

        lax.fori_loop(0, size, one, 0)
        later_copy(family, c, phase + 1).start()

    wide[...] = lax.dot_general(
        mixed[...], grad_attn[...], contract_first, preferred_element_type=jnp.float32
    )
    send_chunk(0, 0)
    grad_mixed[...] = lax.dot_general(
        grad_attn[...], weights[:, 3 * D : 4 * D], contract_last, preferred_element_type=jnp.float32
    ).astype(jnp.bfloat16)

    def complete():
        for move in half_moves:
            move.wait_recv()
        size = 16

        def one(step, carry):
            here = pl.ds(pl.multiple_of(step * size, 16), size)
            total = own_in[here, :].astype(jnp.float32)
            for came in range(half - 1):
                total = total + other_in[came, here, :].astype(jnp.float32)
            own_in[here, :] = total.astype(jnp.bfloat16)
            return carry

        lax.fori_loop(0, own_in.shape[0] // size, one, 0)
        for move in own_moves(1):
            move.start()

    partner = flip(rep, 0)

    def passed_on(kind, step):
        owner = 2 * lax.rem(along + half - step, half) + core
        return spread(kind, landing(kind, owner), owner, (mine, partner), half + step - 1)

    def pass_on(kind):
        for step in range(1, half):
            owner = 2 * lax.rem(along + half - step, half) + core
            spread(kind, landing(kind, owner), owner, (mine, owner), step).wait_recv()
            passed_on(kind, step).start()

    pairs = HEADS // 2

    def attend_back(pair):
        base = pl.multiple_of(pair * 2 * HEAD, 2 * HEAD)
        queries = qkv[:, pl.ds(base, 2 * HEAD)]
        keys = qkv[:, pl.ds(base + D, 2 * HEAD)]
        values = qkv[:, pl.ds(base + 2 * D, 2 * HEAD)]
        grads = grad_mixed[:, pl.ds(base, 2 * HEAD)]
        done = []
        for side in range(2):
            lanes = slice(side * HEAD, (side + 1) * HEAD)
            query, key, value, grad = (
                queries[:, lanes],
                keys[:, lanes],
                values[:, lanes],
                grads[:, lanes],
            )
            scores = lax.dot_general(key, query, contract_last, preferred_element_type=jnp.float32)
            scores = scores * HEAD ** (-0.5) + bias[...]
            expo = jnp.exp(scores - jnp.max(scores, axis=0, keepdims=True))
            weight = expo * (1.0 / jnp.sum(expo, axis=0, keepdims=True))
            grad_weight = lax.dot_general(
                value, grad, contract_last, preferred_element_type=jnp.float32
            )
            product = weight * grad_weight
            delta = jnp.sum(product, axis=0, keepdims=True)
            grad_scores = (product - weight * delta).astype(jnp.bfloat16)
            grad_value = jnp.dot(
                weight.astype(jnp.bfloat16), grad, preferred_element_type=jnp.float32
            )
            grad_key = jnp.dot(grad_scores, query, preferred_element_type=jnp.float32)
            grad_query = lax.dot_general(
                grad_scores, key, contract_first, preferred_element_type=jnp.float32
            )
            done.append(
                (grad_query * HEAD ** (-0.5), grad_key * HEAD ** (-0.5), grad_value)
            )
        block = jnp.concatenate(
            [jnp.concatenate([done[0][kind], done[1][kind]], axis=1) for kind in range(3)], axis=1
        ).astype(jnp.bfloat16)
        for kind in range(3):
            grad_qkv[:, pl.ds(base + kind * D, 2 * HEAD)] = block[:, kind * LANES : (kind + 1) * LANES]
        wide[:, : 3 * LANES] = lax.dot_general(
            normed[...], block, contract_first, preferred_element_type=jnp.float32
        )
        send_chunk(1, pair)

    def finish_tokens():
        tall[...] = lax.dot_general(
            grad_qkv[...], weights[:, : 3 * D], contract_last, preferred_element_type=jnp.float32
        )

        def first_norm(step, carry):
            here = band(step)
            grad_in, grad_gain, grad_bias = norm_back(
                tokens[here, :].astype(jnp.float32), tall[here, :], vectors_ref[0:1, :]
            )
            grad_tokens_ref[here, :] = grad_resid[here, :] + grad_in
            return (carry[0] + grad_gain, carry[1] + grad_bias)

        gain_one, bias_one = lax.fori_loop(0, SLOTS // BAND, first_norm, (zero, zero))
        lines[0:8, :] = gain_one
        lines[8:16, :] = bias_one
        wide[:, :LANES] = lax.dot_general(
            routed[...], grad_logits[...], contract_first, preferred_element_type=jnp.float32
        )
        sums = [jnp.sum(lines[8 * k : 8 * k + 8, :], axis=0, keepdims=True) for k in range(4)]
        lane = lax.broadcasted_iota(jnp.int32, (LANES, LANES), 1)
        for part in range(D // LANES):
            span = slice(part * LANES, (part + 1) * LANES)
            block = wide[span, :LANES]
            for k in range(4):
                block = jnp.where(lane == experts + k, column_of(sums[k][:, span], LANES), block)
            wide[span, :LANES] = block
        send_chunk(2, 0)

    def finish_output():
        own_result.wait()

        def result_arrived(step, carry):
            result_copy(step).wait_recv()
            result_copy(step).wait_send()
            return carry

        lax.fori_loop(1, experts, result_arrived, 0)
        lane = lax.broadcasted_iota(jnp.int32, (SLOTS, LANES), 1)
        probs = probs_ref[...]
        gates = [
            jnp.sum(jnp.where(lane == routes_ref[:, k : k + 1], probs, 0.0), axis=1, keepdims=True)
            for k in range(2)
        ]
        tall[...] = resid[...] + gates[0] * jnp.dot(
            first[...], returned[...], preferred_element_type=jnp.float32
        )
        output_ref[...] = (
            tall[...]
            + gates[1] * jnp.dot(second[...], returned[...], preferred_element_type=jnp.float32)
        ).astype(jnp.bfloat16)

    slack = (0, 1, 4, 5, 8)

    def work(step, carry):
        @pl.when(step == 2)
        def _():
            complete()

        @pl.when(step < pairs)
        def _():
            attend_back(step)

        @pl.when(step == pairs)
        def _():
            finish_tokens()

        @pl.when(step == pairs + 1)
        def _():
            finish_output()

        @pl.when(step == pairs + 4)
        def _():
            pass_on(0)
            pass_on(2)

        for phase in range(bits):
            later = phase + slack[min(phase, 4)]

            @pl.when(step == later)
            def _():
                absorb(0, 0, phase)

            @pl.when(jnp.logical_and(step > later, step <= later + pairs))
            def _():
                absorb(1, step - 1 - later, phase)

            @pl.when(step == pairs + max(1, slack[-1] - 1) + phase)
            def _():
                absorb(2, 0, phase)

        return carry

    lax.fori_loop(0, pairs + bits + max(1, slack[-1]), work, 0)
    pass_on(1)
    for kind in (0, 2, 1):
        spread(kind, landing(kind, partner), partner, (mine, partner), 0).wait_recv()
        for step in range(1, half):
            owner = 2 * lax.rem(along + half - step, half) + 1 - core
            spread(
                kind, landing(kind, owner), owner, (mine, partner), half + step - 1
            ).wait_recv()
        moves = own_moves(kind)
        moves[0].wait()
        for move in moves[1:]:
            move.wait_send()
        for step in range(1, half):
            passed_on(kind, step).wait_send()
    for move in half_moves:
        move.wait_send()

    def dense_sent(family, c):
        def one(expert, carry):
            first_copy(family, c, expert).wait_send()
            return carry

        lax.fori_loop(0, experts, one, 0)
        for phase in range(1, bits):
            later_copy(family, c, phase).wait_send()

    def pair_sent(c, carry):
        dense_sent(1, c)
        return carry

    if summed:
        dense_sent(0, 0)
        lax.fori_loop(0, pairs, pair_sent, 0)
        dense_sent(2, 0)


def run_backward(operands, experts, reps, rows):
    devices = experts * reps
    bits = bit_count(devices)
    half = reps // 2
    (
        back,
        result,
        first,
        second,
        terms,
        probs,
        routes,
        cotangent,
        resid,
        tokens,
        normed,
        routed,
        qkv,
        mixed,
        weights,
        vectors,
        segment_col,
        segment_row,
        live_col,
        half_back,
        half_in,
    ) = operands
    low = jnp.bfloat16
    full = jnp.float32
    piece = half_in.shape[2]
    tail_rows = half_back.shape[0]
    chunks = [(1, D), (HEADS // 2, 3 * LANES), (1, LANES)]
    anywhere = pl.BlockSpec(memory_space=pl.ANY)
    inside = pl.BlockSpec(memory_space=pltpu.VMEM)
    slots = result.shape[0]
    scratch = [
        pltpu.VMEM((slots, D), low),
        pltpu.VMEM((SLOTS, slots), low),
        pltpu.VMEM((SLOTS, slots), low),
        pltpu.VMEM((SLOTS, D), low),
        pltpu.VMEM((SLOTS, D), full),
        pltpu.VMEM((SLOTS, D), low),
        pltpu.VMEM((SLOTS, D), low),
        pltpu.VMEM((SLOTS, D), low),
        pltpu.VMEM((SLOTS, 3 * D), low),
        pltpu.VMEM((SLOTS, D), low),
        pltpu.VMEM(weights.shape, low),
        pltpu.VMEM((slots, D), low),
        pltpu.VMEM((SLOTS, SLOTS), full),
        pltpu.VMEM((D, D), full),
        pltpu.VMEM((SLOTS, D), full),
        pltpu.VMEM((SLOTS, D), full),
        pltpu.VMEM((SLOTS, D), low),
        pltpu.VMEM((SLOTS, D), low),
        pltpu.VMEM((SLOTS, 3 * D), low),
        pltpu.VMEM((SLOTS, LANES), low),
        pltpu.VMEM((D, piece), low),
        pltpu.VMEM((half - 1, D, piece), low),
    ]
    summed = rows % 8 == 0
    scratch.append(pltpu.VMEM((32, D), full))
    for number, width in chunks if summed else ():
        scratch.append(pltpu.VMEM((number, experts, half, 2, rows, width), low))
    for number, width in chunks if summed else ():
        for phase in range(bits):
            scratch.append(pltpu.VMEM((number, devices >> (phase + 1), rows, width), low))
    dense = sum(number for number, _ in chunks) * (experts + bits - 1)
    scratch = scratch + [
        pltpu.SemaphoreType.DMA((12,)),
        pltpu.SemaphoreType.DMA((experts,)),
        pltpu.SemaphoreType.DMA((experts,)),
        pltpu.SemaphoreType.DMA((dense,)),
        pltpu.SemaphoreType.DMA((dense,)),
        pltpu.SemaphoreType.DMA((half - 1,)),
        pltpu.SemaphoreType.DMA((half - 1,)),
        pltpu.SemaphoreType.DMA((3, reps)),
        pltpu.SemaphoreType.DMA((3, reps)),
        pltpu.SemaphoreType.DMA((3,)),
    ]
    call = pl.pallas_call(
        functools.partial(backward_kernel, experts, reps, chunks, summed),
        out_shape=[
            jax.ShapeDtypeStruct((SLOTS, D), low),
            jax.ShapeDtypeStruct((SLOTS, D), full),
            jax.ShapeDtypeStruct((rows if summed else D, 3 * D), full),
            jax.ShapeDtypeStruct((rows if summed else D, D), full),
            jax.ShapeDtypeStruct((rows if summed else D, LANES), full),
            jax.ShapeDtypeStruct((reps * piece, D), low),
            jax.ShapeDtypeStruct((D, reps * piece), low),
            jax.ShapeDtypeStruct((reps, tail_rows - piece, D), low),
        ],
        in_specs=[anywhere] * 4
        + [inside] * 3
        + [anywhere] * 8
        + [inside] * 4
        + [anywhere] * 2,
        out_specs=[inside] * 2 + [inside if summed else anywhere] * 3 + [anywhere] * 3,
        scratch_shapes=scratch,
        compiler_params=pltpu.CompilerParams(
            collective_id=1, has_side_effects=True, vmem_limit_bytes=63 * 1024 * 1024
        ),
        name="backward",
    )
    gradients = list(call(*operands))
    if not summed:
        for index in (2, 3, 4):
            gradients[index] = lax.psum_scatter(
                gradients[index], ("exp", "rep"), scatter_dimension=0, tiled=True
            )
    return gradients


def exchange(blocks):
    return lax.all_to_all(blocks, "exp", split_axis=0, concat_axis=0, tiled=True)


def on_device(
    tokens,
    ln1_gain,
    ln1_bias,
    w_qkv,
    w_out,
    ln2_gain,
    ln2_bias,
    w_router,
    w_in,
    b_in,
    w_back,
    b_back,
    lengths,
    routes,
    priority,
    padding,
    cotangent,
):
    experts = lax.axis_size("exp")
    reps = lax.axis_size("rep")
    devices = experts * reps
    capacity = (TOK_DEV * 210 + experts * 100 - 1) // (experts * 100)
    padded = -(-(capacity + 3) // 16) * 16
    rows = w_qkv.shape[0]
    small = jnp.concatenate(
        [w_router, jnp.stack([ln1_gain, ln1_bias, ln2_gain, ln2_bias], axis=1)], axis=1
    )
    small = jnp.pad(small, ((0, 0), (0, LANES - small.shape[1])))
    packed = jnp.concatenate([w_qkv, w_out, small], axis=1)
    gathered = gather_blocks(packed, devices, reps).reshape(D, packed.shape[1])
    qkv_weight = gathered[:, : 3 * D]
    out_weight = gathered[:, 3 * D : 4 * D]
    router_weight = gathered[:, 4 * D : 4 * D + experts]
    vectors = gathered[:, 4 * D + experts : 4 * D + experts + 4].T
    gain_one, bias_one, gain_two, bias_two = (vectors[0], vectors[1], vectors[2], vectors[3])

    first_hot, second_hot, pick_first, pick_second = dispatch_tables(
        routes, priority, padding, experts, capacity, padded
    )
    picks = pick_first + pick_second
    grad_blocks = lax.dot_general(picks, cotangent, contract_first, preferred_element_type=jnp.float32)
    grad_blocks = grad_blocks.astype(jnp.bfloat16).reshape(experts, padded, D)
    grad_blocks, gathered_done = lax.optimization_barrier((grad_blocks, qkv_weight))
    qkv_weight = gathered_done
    grad_arrived = exchange(grad_blocks)

    inputs = tokens.astype(jnp.float32)
    normed, normal_one, inverse_one = norm_forward(inputs, gain_one, bias_one)
    normed_low = normed.astype(jnp.bfloat16)
    qkv = (
        jnp.dot(normed_low, qkv_weight, preferred_element_type=jnp.float32)
        .astype(jnp.bfloat16)
        .reshape(ROWS_DEV, SLOTS, 3 * D)
    )
    bounds = jnp.cumsum(lengths[0])
    segments = jnp.sum(
        (jnp.arange(SLOTS, dtype=jnp.int32)[:, None] >= bounds[None, :]).astype(jnp.int32), axis=1
    )
    mixed_low = attend(qkv[0], segments, padding)
    resid = inputs + jnp.dot(mixed_low, out_weight, preferred_element_type=jnp.float32)
    routed_float, normal_two, inverse_two = norm_forward(resid, gain_two, bias_two)
    routed = routed_float.astype(jnp.bfloat16)
    logits = jnp.dot(routed, router_weight, preferred_element_type=jnp.float32)
    probs = jax.nn.softmax(logits, axis=-1)
    gate_first = jnp.sum(probs * first_hot, axis=1)
    gate_second = jnp.sum(probs * second_hot, axis=1)
    buffer = lax.dot_general(picks, routed, contract_first, preferred_element_type=jnp.float32)
    buffer = buffer.astype(jnp.bfloat16).reshape(experts, padded, D)
    slot_gates = jnp.sum(
        pick_first.astype(jnp.float32) * gate_first[:, None]
        + pick_second.astype(jnp.float32) * gate_second[:, None],
        axis=0,
    ).reshape(experts, padded)[:, :capacity]
    high = lax.reduce_precision(slot_gates, 8, 7)
    middle = lax.reduce_precision(slot_gates - high, 8, 7)
    terms = jnp.stack([high, middle, slot_gates - high - middle], axis=1).astype(jnp.bfloat16)
    terms = jnp.pad(terms, ((0, 0), (0, padded - capacity - 3), (0, D - capacity)))
    buffer = lax.dynamic_update_slice(buffer, terms, (0, capacity, 0))
    grad_buffer, result, half_back, half_in = run_experts(
        buffer, grad_arrived, w_in[0], w_back[0], b_in, b_back, capacity, reps
    )
    terms = grad_buffer[:, capacity : capacity + 3, :padded].transpose(1, 0, 2)
    terms = jnp.pad(terms.reshape(3, experts * padded), ((0, 13), (0, 0)))
    (
        output,
        grad_tokens,
        sum_qkv,
        sum_out,
        sum_small,
        all_back,
        all_in,
        all_tail,
    ) = run_backward(
        (
            grad_buffer.reshape(experts * padded, D),
            result,
            pick_first,
            pick_second,
            terms,
            jnp.pad(probs, ((0, 0), (0, LANES - experts))),
            routes,
            cotangent,
            resid,
            tokens,
            normed_low,
            routed,
            qkv[0],
            mixed_low,
            gathered,
            vectors.astype(jnp.float32),
            segments.reshape(SLOTS, 1),
            segments.reshape(1, SLOTS),
            padding.reshape(SLOTS, 1),
            half_back,
            half_in,
        ),
        experts,
        reps,
        rows,
    )
    vector_sums = sum_small[:, experts : experts + 4]
    hidden = b_in.shape[1]
    piece = hidden // reps
    return (
        output,
        grad_tokens,
        vector_sums[:, 0],
        vector_sums[:, 1],
        sum_qkv,
        sum_out,
        vector_sums[:, 2],
        vector_sums[:, 3],
        sum_small[:, :experts],
        all_in[None].astype(jnp.float32),
        all_tail[:, 0, :piece].astype(jnp.float32).reshape(1, hidden),
        all_back[None].astype(jnp.float32),
        all_tail[:1, 1, :].astype(jnp.float32),
    )


def solution(mesh):
    return jax.shard_map(
        on_device,
        mesh=mesh,
        in_specs=(
            P(("exp", "rep"), None),
            P(("exp", "rep")),
            P(("exp", "rep")),
            P(("exp", "rep"), None),
            P(("exp", "rep"), None),
            P(("exp", "rep")),
            P(("exp", "rep")),
            P(("exp", "rep"), None),
            P("exp", None, None),
            P("exp", None),
            P("exp", None, None),
            P("exp", None),
            P(("exp", "rep"), None),
            P(("exp", "rep"), None),
            P(("exp", "rep")),
            P(("exp", "rep")),
            P(("exp", "rep"), None),
        ),
        out_specs=(
            P(("exp", "rep"), None),
            P(("exp", "rep"), None),
            P(("exp", "rep")),
            P(("exp", "rep")),
            P(("exp", "rep"), None),
            P(("exp", "rep"), None),
            P(("exp", "rep")),
            P(("exp", "rep")),
            P(("exp", "rep"), None),
            P("exp", None, None),
            P("exp", None),
            P("exp", None, None),
            P("exp", None),
        ),
        check_vma=False,
    )
```

```python
import functools

import jax
import jax.numpy as jnp
from jax import lax
from jax.experimental import pallas as pl
from jax.experimental.pallas import tpu as pltpu
from jax.sharding import PartitionSpec as P

D = 768
HEADS = 12
HEAD = 64
SLOTS = 576
ROWS_DEV = 1
TOK_DEV = 576


root_half = 0.7071067811865476
inverse_root_tau = 0.3989422804014327
contract_first = (((0,), (0,)), ((), ()))
contract_last = (((1,), (1,)), ((), ()))


def norm_forward(inputs, gain, offset):
    center = inputs - jnp.mean(inputs, axis=-1, keepdims=True)
    inverse = lax.rsqrt(jnp.mean(center * center, axis=-1, keepdims=True) + 1e-06)
    normal = center * inverse
    return (normal * gain.astype(jnp.float32) + offset.astype(jnp.float32), normal, inverse)


def dispatch_tables(routes, priority, padding, experts, capacity, padded):
    labels = jnp.arange(experts, dtype=jnp.int32)
    first_hot = (routes[:, 0:1] == labels[None, :]).astype(jnp.bfloat16)
    second_hot = (routes[:, 1:2] == labels[None, :]).astype(jnp.bfloat16)
    live = padding[:, None].astype(jnp.bfloat16)
    earlier = (priority[None, :] < priority[:, None]).astype(jnp.bfloat16)
    before_first = jnp.dot(earlier, first_hot * live, preferred_element_type=jnp.float32)
    first_counts = jnp.sum((first_hot * live).astype(jnp.float32), axis=0)
    before_second = (
        jnp.dot(earlier, second_hot * live, preferred_element_type=jnp.float32)
        + first_counts[None, :]
    )
    place_first = jnp.sum(before_first * first_hot, axis=1).astype(jnp.int32)
    place_second = jnp.sum(before_second * second_hot, axis=1).astype(jnp.int32)
    kept_first = (padding == 1) & (place_first < capacity)
    kept_second = (padding == 1) & (place_second < capacity)
    slot_labels = jnp.arange(experts * padded, dtype=jnp.int32)
    slot_first = routes[:, 0] * padded + place_first
    slot_second = routes[:, 1] * padded + place_second
    pick_first = ((slot_first[:, None] == slot_labels[None, :]) & kept_first[:, None]).astype(
        jnp.bfloat16
    )
    pick_second = ((slot_second[:, None] == slot_labels[None, :]) & kept_second[:, None]).astype(
        jnp.bfloat16
    )
    return (first_hot.astype(jnp.float32), second_hot.astype(jnp.float32), pick_first, pick_second)


LANES = 128
MESH_ID = pl.DeviceIdType.MESH


def bit_count(number):
    return number.bit_length() - 1


def flip(position, bit):
    step = 1 << bit
    return position + (1 - 2 * lax.rem(lax.div(position, step), 2)) * step


def coordinates(position, reps):
    return (lax.div(position, reps), lax.rem(position, reps))


def greet(bits, me, reps):
    barrier = pltpu.get_barrier_semaphore()
    for bit in range(bits):
        pl.semaphore_signal(
            barrier, inc=1, device_id=coordinates(flip(me, bit), reps), device_id_type=MESH_ID
        )
    pl.semaphore_wait(barrier, bits)


def lowest_bit(number):
    return (number & -number).bit_length() - 1


def gather_kernel(devices, reps, pieces, qkv_ref, rest_ref, all_qkv_ref, all_rest_ref, send_sem, recv_sem, local_sem):
    bits = bit_count(devices)
    me = lax.axis_index("exp") * reps + lax.axis_index("rep")
    greet(bits, me, reps)
    own = (qkv_ref, rest_ref)
    everywhere = (all_qkv_ref, all_rest_ref)
    locals_ = [
        pltpu.make_async_copy(own[k], everywhere[k].at[me], local_sem.at[k]) for k in range(2)
    ]
    for copy in locals_:
        copy.start()

    def owner_of(distance, order):
        found = me
        for bit in range(bits):
            if distance >> bit & 1:
                found = flip(found, order[bit])
        return found

    def block(number, owner):
        array, start, width, _ = pieces[number]
        return everywhere[array].at[owner, :, pl.ds(start, width)]

    def transfer(number, distance, bit):
        array, start, width, order = pieces[number]
        owner = owner_of(distance, order)
        index = distance + (1 << bit)
        source = own[array].at[:, pl.ds(start, width)] if distance == 0 else block(number, owner)
        return pltpu.make_async_remote_copy(
            src_ref=source,
            dst_ref=block(number, owner),
            send_sem=send_sem.at[number, index],
            recv_sem=recv_sem.at[number, index],
            device_id=coordinates(flip(me, order[bit]), reps),
            device_id_type=MESH_ID,
        )

    def arrival(number, distance):
        order = pieces[number][3]
        owner = owner_of(distance, order)
        return pltpu.make_async_remote_copy(
            src_ref=block(number, owner),
            dst_ref=block(number, owner),
            send_sem=send_sem.at[number, distance],
            recv_sem=recv_sem.at[number, distance],
            device_id=coordinates(flip(me, order[lowest_bit(distance)]), reps),
            device_id_type=MESH_ID,
        )

    sent = []
    for bit in range(bits):
        for number in range(len(pieces)):
            copy = transfer(number, 0, bit)
            copy.start()
            sent.append(copy)
    sequence = sorted(range(1, devices), key=lambda d: (bin(d).count("1"), -d))
    last = []
    for distance in sequence:
        low = lowest_bit(distance)
        for number in range(len(pieces)):
            if low == 0:
                last.append((number, distance))
                continue
            arrival(number, distance).wait_recv()
            for bit in range(low):
                copy = transfer(number, distance, bit)
                copy.start()
                sent.append(copy)
    for number, distance in last:
        arrival(number, distance).wait_recv()
    for copy in sent:
        copy.wait_send()
    for copy in locals_:
        copy.wait()


def gather_blocks(qkv, rest, devices, reps):
    bits = bit_count(devices)
    plain = list(range(bits))
    low = bit_count(reps)
    turned = list(plain)
    turned[low - 1], turned[low] = (plain[low], plain[low - 1])
    pieces = [(0, 0, 2 * D, plain), (0, 2 * D, D, turned), (1, 0, rest.shape[1], turned)]
    anywhere = pl.BlockSpec(memory_space=pl.ANY)
    return pl.pallas_call(
        functools.partial(gather_kernel, devices, reps, pieces),
        out_shape=[
            jax.ShapeDtypeStruct((devices,) + qkv.shape, qkv.dtype),
            jax.ShapeDtypeStruct((devices,) + rest.shape, rest.dtype),
        ],
        in_specs=[anywhere] * 2,
        out_specs=[anywhere] * 2,
        scratch_shapes=[
            pltpu.SemaphoreType.DMA((len(pieces), devices)),
            pltpu.SemaphoreType.DMA((len(pieces), devices)),
            pltpu.SemaphoreType.DMA((2,)),
        ],
        compiler_params=pltpu.CompilerParams(collective_id=0, has_side_effects=True),
        name="gather_dense",
    )(qkv, rest)


def row_of(column, width):
    count = column.shape[0]
    down = lax.broadcasted_iota(jnp.int32, (count, width), 0)
    across = lax.broadcasted_iota(jnp.int32, (count, width), 1)
    return jnp.sum(jnp.where(down == across, column, 0.0), axis=0, keepdims=True)


def column_of(row, count):
    width = row.shape[1]
    down = lax.broadcasted_iota(jnp.int32, (count, width), 0)
    across = lax.broadcasted_iota(jnp.int32, (count, width), 1)
    return jnp.sum(jnp.where(down == across, row, 0.0), axis=1, keepdims=True)


def three_terms(value):
    high = value.astype(jnp.bfloat16).astype(jnp.float32)
    rest = value - high
    middle = rest.astype(jnp.bfloat16).astype(jnp.float32)
    return (high, middle, rest - middle)


def expert_kernel(
    experts,
    capacity,
    padded,
    block,
    send_ref,
    grad_ref,
    w_in_ref,
    w_back_ref,
    b_in_ref,
    b_back_ref,
    return_ref,
    result_ref,
    half_back_ref,
    half_in_ref,
    slots,
    grads,
    gated,
    weight_in,
    weight_back,
    active,
    grad_pre,
    back_rows,
    result_rows,
    result_total,
    back_total,
    away_back,
    away_in,
    other_back,
    other_in,
    came_back,
    load_sem,
    send_sem,
    recv_sem,
    return_send_sem,
    return_recv_sem,
    result_sem,
    core_send,
    core_recv,
    along_send,
    along_recv,
    stage_sem,
):
    mine = lax.axis_index("exp")
    rep = lax.axis_index("rep")
    bits = bit_count(experts)
    groups = experts // 2
    hidden = weight_in.shape[1]
    steps = hidden // block
    lanes = 256 if capacity <= 256 else D
    gate_row = capacity - (padded - 16)

    barrier = pltpu.get_barrier_semaphore()

    def greet_one(step, carry):
        other = lax.rem(mine + step, experts)
        pl.semaphore_signal(barrier, inc=1, device_id=(other, rep), device_id_type=MESH_ID)
        return carry

    lax.fori_loop(1, experts, greet_one, 0)
    core = lax.rem(rep, 2)
    partner = (mine, flip(rep, 0))
    pl.semaphore_signal(barrier, inc=1, device_id=partner, device_id_type=MESH_ID)
    half = away_in.shape[0]
    along = lax.div(rep, 2)

    def greet_along(step, carry):
        other = 2 * lax.rem(along + step, half) + core
        pl.semaphore_signal(barrier, inc=1, device_id=(mine, other), device_id_type=MESH_ID)
        return carry

    lax.fori_loop(1, half, greet_along, 0)

    def group_of(index):
        half = lax.div(mine, 2)
        found = half
        for bit in range(bits - 1):
            found = found + lax.rem(lax.div(index, 1 << bit), 2) * (
                (1 - 2 * lax.rem(lax.div(half, 1 << bit), 2)) * (1 << bit)
            )
        return found

    def place(expert):
        return pl.ds(pl.multiple_of(expert * padded, 16), padded)

    def outgoing(expert):
        return pltpu.make_async_remote_copy(
            src_ref=send_ref.at[expert],
            dst_ref=slots.at[place(mine)],
            send_sem=send_sem.at[expert],
            recv_sem=recv_sem.at[mine],
            device_id=(expert, rep),
            device_id_type=MESH_ID,
        )

    def incoming(expert):
        return pltpu.make_async_remote_copy(
            src_ref=send_ref.at[mine],
            dst_ref=slots.at[place(expert)],
            send_sem=send_sem.at[expert],
            recv_sem=recv_sem.at[expert],
            device_id=(expert, rep),
            device_id_type=MESH_ID,
        )

    def going_back(expert):
        return pltpu.make_async_remote_copy(
            src_ref=back_rows.at[place(expert)],
            dst_ref=return_ref.at[mine],
            send_sem=return_send_sem.at[expert],
            recv_sem=return_recv_sem.at[mine],
            device_id=(expert, rep),
            device_id_type=MESH_ID,
        )

    def coming_back(expert):
        return pltpu.make_async_remote_copy(
            src_ref=back_rows.at[place(expert)],
            dst_ref=return_ref.at[expert],
            send_sem=return_send_sem.at[expert],
            recv_sem=return_recv_sem.at[expert],
            device_id=(expert, rep),
            device_id_type=MESH_ID,
        )

    neighbour = flip(mine, 0)
    side = lax.rem(mine, 2)
    loads = [
        pltpu.make_async_copy(send_ref.at[mine], slots.at[place(mine)], load_sem.at[0]),
        pltpu.make_async_copy(grad_ref, grads, load_sem.at[1]),
        pltpu.make_async_copy(w_in_ref, weight_in, load_sem.at[2]),
        pltpu.make_async_copy(w_back_ref, weight_back, load_sem.at[3]),
    ]
    for copy in loads:
        copy.start()
    pl.semaphore_wait(barrier, experts + half - 1)

    def send_group(index):
        pair = group_of(index)
        outgoing(2 * pair + side).start()
        outgoing(2 * pair + 1 - side).start()

    half_pair = lax.div(mine, 2)
    inner = lax.rem(lax.rem(half_pair, 2) + lax.div(half_pair, 2), 2)

    def turn(index):
        if groups != 4:
            return index
        high, low = (lax.div(index, 2), lax.rem(index, 2))
        return inner * (2 * high + lax.rem(low + high, 2)) + (1 - inner) * (2 * low + high)

    outgoing(neighbour).start()

    def send_step(step, carry):
        if groups == 4:
            send_group(inner * (lax.rem(step + 1, 3) + 1) + (1 - inner) * (step + 1))
        else:
            send_group(step + 1)
        return carry

    lax.fori_loop(0, groups - 1, send_step, 0)
    for copy in loads:
        copy.wait()

    def send_back_group(index):
        pair = group_of(index)
        going_back(2 * pair + side).start()
        going_back(2 * pair + 1 - side).start()

    def gate_columns(expert):
        tail = slots[pl.ds(pl.multiple_of(expert * padded + padded - 16, 16), 16), :].astype(jnp.float32)
        row = jnp.sum(tail[gate_row : gate_row + 3, :lanes], axis=0, keepdims=True)
        return column_of(row, padded)

    def group_step(index, carry):
        pair = group_of(turn(index))

        @pl.when(index == 0)
        def _():
            incoming(neighbour).wait_recv()

        @pl.when(index > 0)
        def _():
            incoming(2 * pair).wait_recv()
            incoming(2 * pair + 1).wait_recv()

        @pl.when(index == 1)
        def _():
            going_back(neighbour).start()

        @pl.when(index > 1)
        def _():
            send_back_group(turn(index - 1))

        here = pl.ds(pl.multiple_of(pair * 2 * padded, 16), 2 * padded)
        for member in range(2):
            spot = place(2 * pair + member)
            gate = gate_columns(2 * pair + member)
            gated[spot, :] = (gate * grads[spot, :].astype(jnp.float32)).astype(jnp.bfloat16)

        def hidden_step(step, inner):
            columns = pl.ds(pl.multiple_of(step * block, block), block)
            pre = (
                jnp.dot(slots[here, :], weight_in[:, columns], preferred_element_type=jnp.float32)
                + b_in_ref[:, columns]
            )
            grad_active = lax.dot_general(
                gated[here, :],
                weight_back[columns, :],
                contract_last,
                preferred_element_type=jnp.float32,
            )
            cumulative = 0.5 * (1.0 + lax.erf(pre * root_half))
            slope = cumulative + pre * inverse_root_tau * jnp.exp(-0.5 * pre * pre)
            active_low = (pre * cumulative).astype(jnp.bfloat16)
            grad_low = (grad_active * slope).astype(jnp.bfloat16)
            active[here, columns] = active_low
            grad_pre[here, columns] = grad_low
            result_part = jnp.dot(
                active_low, weight_back[columns, :], preferred_element_type=jnp.float32
            )
            back_part = lax.dot_general(
                grad_low, weight_in[:, columns], contract_last, preferred_element_type=jnp.float32
            )

            @pl.when(step == 0)
            def _():
                result_total[...] = result_part
                back_total[...] = back_part

            @pl.when(step > 0)
            def _():
                result_total[...] += result_part
                back_total[...] += back_part

            return inner

        lax.fori_loop(0, steps, hidden_step, 0)
        for member in range(2):
            expert = 2 * pair + member
            span = slice(member * padded, (member + 1) * padded)
            spot = place(expert)
            result_low = (result_total[span, :] + b_back_ref[...]).astype(jnp.bfloat16)
            result_rows[spot, :] = result_low
            grad_gate = jnp.sum(
                grads[spot, :].astype(jnp.float32) * result_low.astype(jnp.float32),
                axis=1,
                keepdims=True,
            )
            gate_line = row_of(
                jnp.where(
                    lax.broadcasted_iota(jnp.int32, (padded, 1), 0) < capacity, grad_gate, 0.0
                ),
                lanes,
            )
            if lanes < D:
                gate_line = jnp.concatenate(
                    [gate_line, jnp.zeros((1, D - lanes), jnp.float32)], axis=1
                )
            high, middle, lowest = three_terms(gate_line)
            row = lax.broadcasted_iota(jnp.int32, (padded, D), 0)
            value = back_total[span, :]
            value = jnp.where(row == capacity, high, value)
            value = jnp.where(row == capacity + 1, middle, value)
            value = jnp.where(row == capacity + 2, lowest, value)
            back_rows[spot, :] = value.astype(jnp.bfloat16)
        return carry

    lax.fori_loop(0, groups, group_step, 0)
    own_back = pltpu.make_async_copy(back_rows.at[place(mine)], return_ref.at[mine], load_sem.at[0])
    own_back.start()
    results = pltpu.make_async_copy(result_rows, result_ref, result_sem)
    results.start()

    piece = away_in.shape[2]
    bias_back = jnp.sum(gated[...].astype(jnp.float32), axis=0, keepdims=True)

    def columns_of(number):
        return pl.ds(pl.multiple_of(number * piece, LANES), piece)

    def back_sums(number):
        columns = columns_of(number)
        back = lax.dot_general(
            active[:, columns], gated[...], contract_first, preferred_element_type=jnp.float32
        )
        bias_in = jnp.sum(grad_pre[:, columns].astype(jnp.float32), axis=0, keepdims=True)
        if piece < D:
            bias_in = jnp.concatenate([bias_in, jnp.zeros((1, D - piece), jnp.float32)], axis=1)
        row = lax.broadcasted_iota(jnp.int32, (16, D), 0)
        extra = jnp.where(row == 0, bias_in, jnp.where(row == 1, bias_back, 0.0))
        return (back, extra)

    def in_sums(number):
        return lax.dot_general(
            slots[...],
            grad_pre[:, columns_of(number)],
            contract_first,
            preferred_element_type=jnp.float32,
        )

    def core_copy(kind, index):
        source, target = ((away_back, other_back), (away_in, other_in))[kind]
        return pltpu.make_async_remote_copy(
            src_ref=source.at[index],
            dst_ref=target.at[index],
            send_sem=core_send.at[kind, index],
            recv_sem=core_recv.at[kind, index],
            device_id=partner,
            device_id_type=MESH_ID,
        )

    def along_copy(step):
        other = lax.rem(along + step, half)
        return pltpu.make_async_remote_copy(
            src_ref=other_back.at[other],
            dst_ref=came_back.at[step - 1],
            send_sem=along_send.at[step - 1],
            recv_sem=along_recv.at[step - 1],
            device_id=(mine, 2 * other + core),
            device_id_type=MESH_ID,
        )

    def away_back_step(step, carry):
        index = lax.rem(along + step, half)
        back, extra = back_sums(2 * index + 1 - core)
        away_back[index, :piece, :] = back.astype(jnp.bfloat16)
        away_back[index, piece:, :] = extra.astype(jnp.bfloat16)
        core_copy(0, index).start()
        return carry

    def kept_back_step(step, carry):
        index = lax.rem(along + step, half)
        back, extra = back_sums(2 * index + core)
        core_copy(0, index).wait_recv()
        other_back[index, :piece, :] = (
            back + other_back[index, :piece, :].astype(jnp.float32)
        ).astype(jnp.bfloat16)
        other_back[index, piece:, :] = (
            extra + other_back[index, piece:, :].astype(jnp.float32)
        ).astype(jnp.bfloat16)

        @pl.when(step < half)
        def _():
            along_copy(step).start()

        return carry

    def away_in_step(index, carry):
        away_in[index] = in_sums(2 * index + 1 - core).astype(jnp.bfloat16)
        core_copy(1, index).start()
        return carry

    def kept_in_copy(index):
        return pltpu.make_async_copy(other_in.at[index], half_in_ref.at[index], stage_sem.at[index])

    def kept_in_step(index, carry):
        inward = in_sums(2 * index + core)
        core_copy(1, index).wait_recv()
        other_in[index] = (inward + other_in[index].astype(jnp.float32)).astype(jnp.bfloat16)
        kept_in_copy(index).start()
        return carry

    lax.fori_loop(1, half + 1, away_back_step, 0)
    if groups > 1:
        send_back_group(turn(groups - 1))
    else:
        going_back(neighbour).start()
    lax.fori_loop(1, half + 1, kept_back_step, 0)
    lax.fori_loop(0, half, away_in_step, 0)
    lax.fori_loop(0, half, kept_in_step, 0)
    for step in range(1, half):
        along_copy(step).wait_recv()

    def along_sum(step, carry):
        here = pl.ds(pl.multiple_of(step * 16, 16), 16)
        total = other_back[along, here, :].astype(jnp.float32)
        for came in range(half - 1):
            total = total + came_back[came, here, :].astype(jnp.float32)
        other_back[along, here, :] = total.astype(jnp.bfloat16)
        return carry

    lax.fori_loop(0, (piece + 16) // 16, along_sum, 0)
    sum_back = pltpu.make_async_copy(other_back.at[along], half_back_ref, stage_sem.at[half])
    sum_back.start()
    sum_back.wait()
    for step in range(1, half):
        along_copy(step).wait_send()
    for index in range(half):
        kept_in_copy(index).wait()
        for kind in range(2):
            core_copy(kind, index).wait_send()
    own_back.wait()
    results.wait()

    def finish(step, carry):
        other = lax.rem(mine + step, experts)
        outgoing(other).wait_send()
        going_back(other).wait_send()
        coming_back(other).wait_recv()
        return carry

    lax.fori_loop(1, experts, finish, 0)


def run_experts(buffer, grads, w_in, w_back, b_in, b_back, capacity, reps):
    experts, padded = (buffer.shape[0], buffer.shape[1])
    hidden = w_in.shape[1]
    block = 512
    rows = experts * padded
    half = reps // 2
    piece = hidden // reps
    low = jnp.bfloat16
    anywhere = pl.BlockSpec(memory_space=pl.ANY)
    inside = pl.BlockSpec(memory_space=pltpu.VMEM)
    return pl.pallas_call(
        functools.partial(expert_kernel, experts, capacity, padded, block),
        out_shape=[
            jax.ShapeDtypeStruct((experts, padded, D), low),
            jax.ShapeDtypeStruct((rows, D), low),
            jax.ShapeDtypeStruct((piece + 16, D), low),
            jax.ShapeDtypeStruct((half, D, piece), low),
        ],
        in_specs=[anywhere, anywhere, anywhere, anywhere, inside, inside],
        out_specs=[anywhere, anywhere, anywhere, anywhere],
        scratch_shapes=[
            pltpu.VMEM((rows, D), low),
            pltpu.VMEM((rows, D), low),
            pltpu.VMEM((rows, D), low),
            pltpu.VMEM((D, hidden), low),
            pltpu.VMEM((hidden, D), low),
            pltpu.VMEM((rows, hidden), low),
            pltpu.VMEM((rows, hidden), low),
            pltpu.VMEM((rows, D), low),
            pltpu.VMEM((rows, D), low),
            pltpu.VMEM((2 * padded, D), jnp.float32),
            pltpu.VMEM((2 * padded, D), jnp.float32),
            pltpu.VMEM((half, piece + 16, D), low),
            pltpu.VMEM((half, D, piece), low),
            pltpu.VMEM((half, piece + 16, D), low),
            pltpu.VMEM((half, D, piece), low),
            pltpu.VMEM((half - 1, piece + 16, D), low),
            pltpu.SemaphoreType.DMA((4,)),
            pltpu.SemaphoreType.DMA((experts,)),
            pltpu.SemaphoreType.DMA((experts,)),
            pltpu.SemaphoreType.DMA((experts,)),
            pltpu.SemaphoreType.DMA((experts,)),
            pltpu.SemaphoreType.DMA,
            pltpu.SemaphoreType.DMA((2, half)),
            pltpu.SemaphoreType.DMA((2, half)),
            pltpu.SemaphoreType.DMA((half - 1,)),
            pltpu.SemaphoreType.DMA((half - 1,)),
            pltpu.SemaphoreType.DMA((half + 1,)),
        ],
        compiler_params=pltpu.CompilerParams(
            collective_id=2, has_side_effects=True, vmem_limit_bytes=63 * 1024 * 1024
        ),
        cost_estimate=pl.CostEstimate(
            flops=12 * rows * D * hidden, bytes_accessed=40 << 20, transcendentals=2 * rows * hidden
        ),
        name="experts",
    )(buffer, grads.reshape(rows, D), w_in, w_back, b_in.astype(jnp.float32), b_back.astype(jnp.float32))


def attend_kernel(segment_col, segment_row, live_row, query_ref, keys_ref, values_ref, mixed_ref, bias):
    @pl.when(pl.program_id(0) == 0)
    def _():
        row = lax.broadcasted_iota(jnp.int32, (SLOTS, SLOTS), 0)
        column = lax.broadcasted_iota(jnp.int32, (SLOTS, SLOTS), 1)
        seen = (segment_col[...] == segment_row[...]) & ((live_row[...] == 1) | (row == column))
        bias[...] = jnp.where(seen, 0.0, -1e30)

    for side in range(2):
        lanes = slice(side * HEAD, (side + 1) * HEAD)
        scores = lax.dot_general(
            query_ref[:, lanes], keys_ref[:, lanes], contract_last, preferred_element_type=jnp.float32
        )
        scores = scores * HEAD ** (-0.5) + bias[...]
        expo = jnp.exp(scores - jnp.max(scores, axis=1, keepdims=True))
        total = jnp.sum(expo, axis=1, keepdims=True)
        probs = (expo * (1.0 / total)).astype(jnp.bfloat16)
        mixed = jnp.dot(probs, values_ref[:, lanes], preferred_element_type=jnp.float32)
        mixed_ref[:, lanes] = mixed.astype(jnp.bfloat16)


def attend(qkv, segments, live):
    pairs = HEADS // 2
    return pl.pallas_call(
        attend_kernel,
        grid=(pairs,),
        out_shape=jax.ShapeDtypeStruct((SLOTS, D), jnp.bfloat16),
        in_specs=[
            pl.BlockSpec((SLOTS, 1), lambda i: (0, 0)),
            pl.BlockSpec((1, SLOTS), lambda i: (0, 0)),
            pl.BlockSpec((1, SLOTS), lambda i: (0, 0)),
            pl.BlockSpec((SLOTS, 2 * HEAD), lambda i: (0, i)),
            pl.BlockSpec((SLOTS, 2 * HEAD), lambda i: (0, pairs + i)),
            pl.BlockSpec((SLOTS, 2 * HEAD), lambda i: (0, 2 * pairs + i)),
        ],
        out_specs=pl.BlockSpec((SLOTS, 2 * HEAD), lambda i: (0, i)),
        scratch_shapes=[pltpu.VMEM((SLOTS, SLOTS), jnp.float32)],
        cost_estimate=pl.CostEstimate(
            flops=16 * HEADS * SLOTS * SLOTS * HEAD, bytes_accessed=4 << 20, transcendentals=HEADS * SLOTS * SLOTS
        ),
        name="attend",
    )(segments.reshape(SLOTS, 1), segments.reshape(1, SLOTS), live.reshape(1, SLOTS), qkv, qkv, qkv)


BAND = 48


def fold_rows(values):
    return jnp.sum(values.reshape(BAND // 8, 8, values.shape[1]), axis=0)


def backward_kernel(
    experts,
    reps,
    chunks,
    summed,
    back_ref,
    result_ref,
    first_ref,
    second_ref,
    terms_ref,
    probs_ref,
    routes_ref,
    cotangent_ref,
    resid_ref,
    tokens_ref,
    normed_ref,
    routed_ref,
    qkv_ref,
    mixed_ref,
    qkv_weight_ref,
    rest_weight_ref,
    vectors_ref,
    segment_col,
    segment_row,
    live_col,
    half_back_ref,
    half_in_ref,
    output_ref,
    grad_tokens_ref,
    sum_qkv_ref,
    sum_out_ref,
    sum_small_ref,
    all_back_ref,
    all_in_ref,
    all_tail_ref,
    *refs,
):
    devices = experts * reps
    bits = bit_count(devices)
    half = reps // 2
    mine = lax.axis_index("exp")
    rep = lax.axis_index("rep")
    me = mine * reps + rep
    core = lax.rem(rep, 2)
    along = lax.div(rep, 2)
    (
        back,
        first,
        second,
        cotangent,
        resid,
        tokens,
        normed,
        routed,
        qkv,
        mixed,
        qkv_weight,
        rest_weight,
        returned,
        bias,
        wide,
        tall,
        grad_resid,
        grad_attn,
        grad_mixed,
        grad_qkv,
        grad_logits,
        own_in,
        other_in,
    ) = refs[:23]
    refs = refs[23:]
    lines, refs = (refs[0], refs[1:])
    count = len(chunks) if summed else 0
    parts, refs = (refs[:count], refs[count:])
    recvs, refs = ([refs[c * bits : (c + 1) * bits] for c in range(count)], refs[count * bits :])
    (
        load_sem,
        result_send,
        result_recv,
        dense_send,
        dense_recv,
        half_send,
        half_recv,
        all_send,
        all_recv,
        own_sem,
    ) = refs
    padded = result_ref.shape[0] // experts
    piece = half_in_ref.shape[2]

    barrier = pltpu.get_barrier_semaphore()

    def greet_expert(step, carry):
        other = lax.rem(mine + step, experts)
        pl.semaphore_signal(barrier, inc=1, device_id=(other, rep), device_id_type=MESH_ID)
        return carry

    def greet_rep(step, carry):
        other = lax.rem(rep + step, reps)
        pl.semaphore_signal(barrier, inc=1, device_id=(mine, other), device_id_type=MESH_ID)
        return carry

    lax.fori_loop(1, experts, greet_expert, 0)
    lax.fori_loop(1, reps, greet_rep, 0)

    sources = [
        (back_ref, back),
        (first_ref, first),
        (second_ref, second),
        (routed_ref, routed),
        (rest_weight_ref, rest_weight),
        (resid_ref, resid),
        (cotangent_ref, cotangent),
        (mixed_ref, mixed),
        (qkv_ref, qkv),
        (normed_ref, normed),
        (tokens_ref, tokens),
        (qkv_weight_ref, qkv_weight),
        (half_in_ref.at[along], own_in),
    ]
    loads = [
        pltpu.make_async_copy(source, target, load_sem.at[i])
        for i, (source, target) in enumerate(sources)
    ]
    for copy in loads:
        copy.start()
    pl.semaphore_wait(barrier, experts - 1 + reps - 1)

    def half_copy(step):
        other = lax.rem(along + step, half)
        return pltpu.make_async_remote_copy(
            src_ref=half_in_ref.at[other],
            dst_ref=other_in.at[step - 1],
            send_sem=half_send.at[step - 1],
            recv_sem=half_recv.at[step - 1],
            device_id=(mine, 2 * other + core),
            device_id_type=MESH_ID,
        )

    half_moves = [half_copy(step) for step in range(1, half)]
    for move in half_moves:
        move.start()

    def own_part(kind):
        return (half_back_ref.at[pl.ds(0, piece), :], own_in, half_back_ref.at[pl.ds(piece, 16), :])[kind]

    def landing(kind, owner):
        if kind == 0:
            return all_back_ref.at[pl.ds(pl.multiple_of(owner * piece, 16), piece), :]
        if kind == 1:
            return all_in_ref.at[:, pl.ds(pl.multiple_of(owner * piece, LANES), piece)]
        return all_tail_ref.at[owner]

    def spread(kind, source, owner, device, step):
        return pltpu.make_async_remote_copy(
            src_ref=source,
            dst_ref=landing(kind, owner),
            send_sem=all_send.at[kind, step],
            recv_sem=all_recv.at[kind, step],
            device_id=device,
            device_id_type=MESH_ID,
        )

    def own_moves(kind):
        moves = [pltpu.make_async_copy(own_part(kind), landing(kind, rep), own_sem.at[kind])]
        for step in range(1, half):
            other = lax.rem(along + step, half)
            moves.append(spread(kind, own_part(kind), rep, (mine, 2 * other + core), step))
        moves.append(spread(kind, own_part(kind), rep, (mine, flip(rep, 0)), 0))
        return moves

    for kind in (0, 2):
        for move in own_moves(kind):
            move.start()

    def place(expert):
        return pl.ds(pl.multiple_of(expert * padded, 16), padded)

    def result_copy(step):
        other = lax.rem(mine + step, experts)
        came = lax.rem(mine + experts - step, experts)
        return pltpu.make_async_remote_copy(
            src_ref=result_ref.at[place(other)],
            dst_ref=returned.at[place(mine)],
            send_sem=result_send.at[step],
            recv_sem=result_recv.at[step],
            device_id=(other, rep),
            device_id_type=MESH_ID,
        )

    def start_result(step, carry):
        result_copy(step).start()
        return carry

    own_result = pltpu.make_async_copy(
        result_ref.at[place(mine)], returned.at[place(mine)], result_send.at[0]
    )
    own_result.start()
    lax.fori_loop(1, experts, start_result, 0)

    row = lax.broadcasted_iota(jnp.int32, (SLOTS, SLOTS), 0)
    column = lax.broadcasted_iota(jnp.int32, (SLOTS, SLOTS), 1)
    seen = (segment_col[...] == segment_row[...]) & ((live_col[...] == 1) | (row == column))
    bias[...] = jnp.where(seen, 0.0, -1e30)

    for copy in loads[:5]:
        copy.wait()
    tall[...] = jnp.dot(first[...] + second[...], back[...], preferred_element_type=jnp.float32)
    gates_back = [
        jnp.sum(
            lax.dot_general(
                pick[...], terms_ref[...], contract_last, preferred_element_type=jnp.float32
            ),
            axis=1,
            keepdims=True,
        )
        for pick in (first, second)
    ]
    lane = lax.broadcasted_iota(jnp.int32, (SLOTS, LANES), 1)
    hots = [(lane == routes_ref[:, k : k + 1]).astype(jnp.float32) for k in range(2)]
    grad_probs = gates_back[0] * hots[0] + gates_back[1] * hots[1]
    probs = probs_ref[...]
    grad_logits[...] = (
        probs * (grad_probs - jnp.sum(probs * grad_probs, axis=1, keepdims=True))
    ).astype(jnp.bfloat16)
    tall[...] += lax.dot_general(
        grad_logits[...], rest_weight[:, D:], contract_last, preferred_element_type=jnp.float32
    )
    for copy in loads[5:]:
        copy.wait()

    def band(step):
        return pl.ds(pl.multiple_of(step * BAND, 16), BAND)

    def norm_back(inputs, grad, gain):
        center = inputs - jnp.mean(inputs, axis=1, keepdims=True)
        inverse = lax.rsqrt(jnp.mean(center * center, axis=1, keepdims=True) + 1e-06)
        normal = center * inverse
        scaled = grad * gain
        grad_in = inverse * (
            scaled
            - jnp.mean(scaled, axis=1, keepdims=True)
            - normal * jnp.mean(scaled * normal, axis=1, keepdims=True)
        )
        return (grad_in, fold_rows(grad * normal), fold_rows(grad))

    zero = jnp.zeros((8, D), jnp.float32)

    def second_norm(step, carry):
        here = band(step)
        grad_in, grad_gain, grad_bias = norm_back(
            resid[here, :], tall[here, :], vectors_ref[2:3, :]
        )
        total = cotangent[here, :].astype(jnp.float32) + grad_in
        grad_resid[here, :] = total
        grad_attn[here, :] = total.astype(jnp.bfloat16)
        return (carry[0] + grad_gain, carry[1] + grad_bias)

    gain_two, bias_two = lax.fori_loop(0, SLOTS // BAND, second_norm, (zero, zero))

    lines[16:24, :] = gain_two
    lines[24:32, :] = bias_two

    own_bits = bit_count(reps)
    plan = [0] + list(range(own_bits, bits)) + list(range(own_bits - 1, 0, -1))
    my_bit = [lax.rem(lax.div(me, 1 << bit), 2) for bit in range(bits)]
    rows = parts[0].shape[4] if summed else 0
    stride = experts + bits - 1
    first_of = [sum(number for number, _ in chunks[:family]) for family in range(len(chunks))]

    def turned(number):
        length = bits - own_bits - 1
        found = 0
        for bit in range(length):
            found = found + lax.rem(lax.div(number, 1 << bit), 2) * (1 << (length - 1 - bit))
        return found

    def fill(family, c):
        width = chunks[family][1]

        def one(block, carry):
            owner = lax.div(block, reps)
            inner = lax.rem(block, reps)
            parts[family][c, owner, lax.div(inner, 2), lax.rem(inner, 2)] = wide[
                pl.ds(pl.multiple_of(block * rows, rows), rows), :width
            ].astype(jnp.bfloat16)
            return carry

        lax.fori_loop(0, devices, one, 0)

    def first_copy(family, c, expert):
        spot = lax.rem(expert, 2) * (devices // 4) + turned(lax.div(expert, 2)) * half
        index = (first_of[family] + c) * stride + expert
        return pltpu.make_async_remote_copy(
            src_ref=parts[family].at[c, expert, :, 1 - core],
            dst_ref=recvs[family][0].at[c, pl.ds(spot, half)],
            send_sem=dense_send.at[index],
            recv_sem=dense_recv.at[index],
            device_id=(mine, flip(rep, 0)),
            device_id_type=MESH_ID,
        )

    def later_copy(family, c, phase):
        size = devices >> (phase + 1)
        index = (first_of[family] + c) * stride + experts + phase - 1
        return pltpu.make_async_remote_copy(
            src_ref=recvs[family][phase - 1].at[c, pl.ds((1 - my_bit[plan[phase]]) * size, size)],
            dst_ref=recvs[family][phase].at[c],
            send_sem=dense_send.at[index],
            recv_sem=dense_recv.at[index],
            device_id=coordinates(flip(me, plan[phase]), reps),
            device_id_type=MESH_ID,
        )

    def columns_of(c, kind):
        return pl.ds(pl.multiple_of(c * LANES + kind * D, LANES), LANES)

    def send_chunk(family, c):
        if not summed:
            if family == 1:
                for kind in range(3):
                    span = slice(kind * LANES, (kind + 1) * LANES)
                    pltpu.sync_copy(wide.at[:, span], sum_qkv_ref.at[:, columns_of(c, kind)])
            else:
                out = sum_out_ref if family == 0 else sum_small_ref
                pltpu.sync_copy(wide.at[:, : chunks[family][1]], out)
            return
        fill(family, c)

        def one(expert, carry):
            first_copy(family, c, expert).start()
            return carry

        lax.fori_loop(0, experts, one, 0)

    def absorb(family, c, phase):
        if not summed:
            return
        size = devices >> (phase + 1)
        into = recvs[family][phase]
        if phase == 0:

            def arrived(expert, carry):
                first_copy(family, c, expert).wait_recv()
                return carry

            lax.fori_loop(0, experts, arrived, 0)

            def held(i):
                side = lax.div(i, devices // 4)
                rest = lax.rem(i, devices // 4)
                expert = 2 * turned(lax.div(rest, half)) + side
                return parts[family][c, expert, lax.rem(rest, half), core]
        else:
            later_copy(family, c, phase).wait_recv()
            base = my_bit[plan[phase]] * size

            def held(i):
                return recvs[family][phase - 1][c, base + i]

        if phase == bits - 1:
            total = into[c, 0].astype(jnp.float32) + held(0).astype(jnp.float32)
            if family == 1:
                for kind in range(3):
                    sum_qkv_ref[:, columns_of(c, kind)] = total[:, kind * LANES : (kind + 1) * LANES]
            elif family == 0:
                sum_out_ref[...] = total
            else:
                sum_small_ref[...] = total
            return

        def one(i, carry):
            into[c, i] = (into[c, i].astype(jnp.float32) + held(i).astype(jnp.float32)).astype(
                jnp.bfloat16
            )
            return carry

        lax.fori_loop(0, size, one, 0)
        later_copy(family, c, phase + 1).start()

    wide[...] = lax.dot_general(
        mixed[...], grad_attn[...], contract_first, preferred_element_type=jnp.float32
    )
    send_chunk(0, 0)
    grad_mixed[...] = lax.dot_general(
        grad_attn[...], rest_weight[:, :D], contract_last, preferred_element_type=jnp.float32
    ).astype(jnp.bfloat16)

    def complete():
        for move in half_moves:
            move.wait_recv()
        size = 16

        def one(step, carry):
            here = pl.ds(pl.multiple_of(step * size, 16), size)
            total = own_in[here, :].astype(jnp.float32)
            for came in range(half - 1):
                total = total + other_in[came, here, :].astype(jnp.float32)
            own_in[here, :] = total.astype(jnp.bfloat16)
            return carry

        lax.fori_loop(0, own_in.shape[0] // size, one, 0)
        for move in own_moves(1):
            move.start()

    partner = flip(rep, 0)

    def passed_on(kind, step):
        owner = 2 * lax.rem(along + half - step, half) + core
        return spread(kind, landing(kind, owner), owner, (mine, partner), half + step - 1)

    def pass_on(kind):
        for step in range(1, half):
            owner = 2 * lax.rem(along + half - step, half) + core
            spread(kind, landing(kind, owner), owner, (mine, owner), step).wait_recv()
            passed_on(kind, step).start()

    pairs = HEADS // 2

    def attend_back(pair):
        base = pl.multiple_of(pair * 2 * HEAD, 2 * HEAD)
        queries = qkv[:, pl.ds(base, 2 * HEAD)]
        keys = qkv[:, pl.ds(base + D, 2 * HEAD)]
        values = qkv[:, pl.ds(base + 2 * D, 2 * HEAD)]
        grads = grad_mixed[:, pl.ds(base, 2 * HEAD)]
        done = []
        for side in range(2):
            lanes = slice(side * HEAD, (side + 1) * HEAD)
            query, key, value, grad = (
                queries[:, lanes],
                keys[:, lanes],
                values[:, lanes],
                grads[:, lanes],
            )
            scores = lax.dot_general(key, query, contract_last, preferred_element_type=jnp.float32)
            scores = scores * HEAD ** (-0.5) + bias[...]
            expo = jnp.exp(scores - jnp.max(scores, axis=0, keepdims=True))
            weight = expo * (1.0 / jnp.sum(expo, axis=0, keepdims=True))
            grad_weight = lax.dot_general(
                value, grad, contract_last, preferred_element_type=jnp.float32
            )
            product = weight * grad_weight
            delta = jnp.sum(product, axis=0, keepdims=True)
            grad_scores = (product - weight * delta).astype(jnp.bfloat16)
            grad_value = jnp.dot(
                weight.astype(jnp.bfloat16), grad, preferred_element_type=jnp.float32
            )
            grad_key = jnp.dot(grad_scores, query, preferred_element_type=jnp.float32)
            grad_query = lax.dot_general(
                grad_scores, key, contract_first, preferred_element_type=jnp.float32
            )
            done.append(
                (grad_query * HEAD ** (-0.5), grad_key * HEAD ** (-0.5), grad_value)
            )
        block = jnp.concatenate(
            [jnp.concatenate([done[0][kind], done[1][kind]], axis=1) for kind in range(3)], axis=1
        ).astype(jnp.bfloat16)
        for kind in range(3):
            grad_qkv[:, pl.ds(base + kind * D, 2 * HEAD)] = block[:, kind * LANES : (kind + 1) * LANES]
        wide[:, : 3 * LANES] = lax.dot_general(
            normed[...], block, contract_first, preferred_element_type=jnp.float32
        )
        send_chunk(1, pair)

    def finish_tokens():
        tall[...] = lax.dot_general(
            grad_qkv[...], qkv_weight[...], contract_last, preferred_element_type=jnp.float32
        )

        def first_norm(step, carry):
            here = band(step)
            grad_in, grad_gain, grad_bias = norm_back(
                tokens[here, :].astype(jnp.float32), tall[here, :], vectors_ref[0:1, :]
            )
            grad_tokens_ref[here, :] = grad_resid[here, :] + grad_in
            return (carry[0] + grad_gain, carry[1] + grad_bias)

        gain_one, bias_one = lax.fori_loop(0, SLOTS // BAND, first_norm, (zero, zero))
        lines[0:8, :] = gain_one
        lines[8:16, :] = bias_one
        wide[:, :LANES] = lax.dot_general(
            routed[...], grad_logits[...], contract_first, preferred_element_type=jnp.float32
        )
        sums = [jnp.sum(lines[8 * k : 8 * k + 8, :], axis=0, keepdims=True) for k in range(4)]
        lane = lax.broadcasted_iota(jnp.int32, (LANES, LANES), 1)
        for part in range(D // LANES):
            span = slice(part * LANES, (part + 1) * LANES)
            block = wide[span, :LANES]
            for k in range(4):
                block = jnp.where(lane == experts + k, column_of(sums[k][:, span], LANES), block)
            wide[span, :LANES] = block
        send_chunk(2, 0)

    def finish_output():
        own_result.wait()

        def result_arrived(step, carry):
            result_copy(step).wait_recv()
            result_copy(step).wait_send()
            return carry

        lax.fori_loop(1, experts, result_arrived, 0)
        lane = lax.broadcasted_iota(jnp.int32, (SLOTS, LANES), 1)
        probs = probs_ref[...]
        gates = [
            jnp.sum(jnp.where(lane == routes_ref[:, k : k + 1], probs, 0.0), axis=1, keepdims=True)
            for k in range(2)
        ]
        tall[...] = resid[...] + gates[0] * jnp.dot(
            first[...], returned[...], preferred_element_type=jnp.float32
        )
        output_ref[...] = (
            tall[...]
            + gates[1] * jnp.dot(second[...], returned[...], preferred_element_type=jnp.float32)
        ).astype(jnp.bfloat16)

    slack = (0, 1, 4, 5, 8)

    def work(step, carry):
        @pl.when(step == 2)
        def _():
            complete()

        @pl.when(step < pairs)
        def _():
            attend_back(step)

        @pl.when(step == pairs)
        def _():
            finish_tokens()

        @pl.when(step == pairs + 1)
        def _():
            finish_output()

        @pl.when(step == pairs + 4)
        def _():
            pass_on(0)
            pass_on(2)

        for phase in range(bits):
            later = phase + slack[min(phase, 4)]

            @pl.when(step == later)
            def _():
                absorb(0, 0, phase)

            @pl.when(jnp.logical_and(step > later, step <= later + pairs))
            def _():
                absorb(1, step - 1 - later, phase)

            @pl.when(step == pairs + max(1, slack[-1] - 1) + phase)
            def _():
                absorb(2, 0, phase)

        return carry

    lax.fori_loop(0, pairs + bits + max(1, slack[-1]), work, 0)
    pass_on(1)
    for kind in (0, 2, 1):
        spread(kind, landing(kind, partner), partner, (mine, partner), 0).wait_recv()
        for step in range(1, half):
            owner = 2 * lax.rem(along + half - step, half) + 1 - core
            spread(
                kind, landing(kind, owner), owner, (mine, partner), half + step - 1
            ).wait_recv()
        moves = own_moves(kind)
        moves[0].wait()
        for move in moves[1:]:
            move.wait_send()
        for step in range(1, half):
            passed_on(kind, step).wait_send()
    for move in half_moves:
        move.wait_send()

    def dense_sent(family, c):
        def one(expert, carry):
            first_copy(family, c, expert).wait_send()
            return carry

        lax.fori_loop(0, experts, one, 0)
        for phase in range(1, bits):
            later_copy(family, c, phase).wait_send()

    def pair_sent(c, carry):
        dense_sent(1, c)
        return carry

    if summed:
        dense_sent(0, 0)
        lax.fori_loop(0, pairs, pair_sent, 0)
        dense_sent(2, 0)


def run_backward(operands, experts, reps, rows):
    devices = experts * reps
    bits = bit_count(devices)
    half = reps // 2
    (
        back,
        result,
        first,
        second,
        terms,
        probs,
        routes,
        cotangent,
        resid,
        tokens,
        normed,
        routed,
        qkv,
        mixed,
        qkv_weight,
        rest_weight,
        vectors,
        segment_col,
        segment_row,
        live_col,
        half_back,
        half_in,
    ) = operands
    low = jnp.bfloat16
    full = jnp.float32
    piece = half_in.shape[2]
    tail_rows = half_back.shape[0]
    chunks = [(1, D), (HEADS // 2, 3 * LANES), (1, LANES)]
    anywhere = pl.BlockSpec(memory_space=pl.ANY)
    inside = pl.BlockSpec(memory_space=pltpu.VMEM)
    slots = result.shape[0]
    scratch = [
        pltpu.VMEM((slots, D), low),
        pltpu.VMEM((SLOTS, slots), low),
        pltpu.VMEM((SLOTS, slots), low),
        pltpu.VMEM((SLOTS, D), low),
        pltpu.VMEM((SLOTS, D), full),
        pltpu.VMEM((SLOTS, D), low),
        pltpu.VMEM((SLOTS, D), low),
        pltpu.VMEM((SLOTS, D), low),
        pltpu.VMEM((SLOTS, 3 * D), low),
        pltpu.VMEM((SLOTS, D), low),
        pltpu.VMEM(qkv_weight.shape, low),
        pltpu.VMEM(rest_weight.shape, low),
        pltpu.VMEM((slots, D), low),
        pltpu.VMEM((SLOTS, SLOTS), full),
        pltpu.VMEM((D, D), full),
        pltpu.VMEM((SLOTS, D), full),
        pltpu.VMEM((SLOTS, D), full),
        pltpu.VMEM((SLOTS, D), low),
        pltpu.VMEM((SLOTS, D), low),
        pltpu.VMEM((SLOTS, 3 * D), low),
        pltpu.VMEM((SLOTS, LANES), low),
        pltpu.VMEM((D, piece), low),
        pltpu.VMEM((half - 1, D, piece), low),
    ]
    summed = rows % 8 == 0
    scratch.append(pltpu.VMEM((32, D), full))
    for number, width in chunks if summed else ():
        scratch.append(pltpu.VMEM((number, experts, half, 2, rows, width), low))
    for number, width in chunks if summed else ():
        for phase in range(bits):
            scratch.append(pltpu.VMEM((number, devices >> (phase + 1), rows, width), low))
    dense = sum(number for number, _ in chunks) * (experts + bits - 1)
    scratch = scratch + [
        pltpu.SemaphoreType.DMA((13,)),
        pltpu.SemaphoreType.DMA((experts,)),
        pltpu.SemaphoreType.DMA((experts,)),
        pltpu.SemaphoreType.DMA((dense,)),
        pltpu.SemaphoreType.DMA((dense,)),
        pltpu.SemaphoreType.DMA((half - 1,)),
        pltpu.SemaphoreType.DMA((half - 1,)),
        pltpu.SemaphoreType.DMA((3, reps)),
        pltpu.SemaphoreType.DMA((3, reps)),
        pltpu.SemaphoreType.DMA((3,)),
    ]
    call = pl.pallas_call(
        functools.partial(backward_kernel, experts, reps, chunks, summed),
        out_shape=[
            jax.ShapeDtypeStruct((SLOTS, D), low),
            jax.ShapeDtypeStruct((SLOTS, D), full),
            jax.ShapeDtypeStruct((rows if summed else D, 3 * D), full),
            jax.ShapeDtypeStruct((rows if summed else D, D), full),
            jax.ShapeDtypeStruct((rows if summed else D, LANES), full),
            jax.ShapeDtypeStruct((reps * piece, D), low),
            jax.ShapeDtypeStruct((D, reps * piece), low),
            jax.ShapeDtypeStruct((reps, tail_rows - piece, D), low),
        ],
        in_specs=[anywhere] * 4
        + [inside] * 3
        + [anywhere] * 9
        + [inside] * 4
        + [anywhere] * 2,
        out_specs=[inside] * 2 + [inside if summed else anywhere] * 3 + [anywhere] * 3,
        scratch_shapes=scratch,
        compiler_params=pltpu.CompilerParams(
            collective_id=1, has_side_effects=True, vmem_limit_bytes=63 * 1024 * 1024
        ),
        name="backward",
    )
    gradients = list(call(*operands))
    if not summed:
        for index in (2, 3, 4):
            gradients[index] = lax.psum_scatter(
                gradients[index], ("exp", "rep"), scatter_dimension=0, tiled=True
            )
    return gradients


def exchange(blocks):
    return lax.all_to_all(blocks, "exp", split_axis=0, concat_axis=0, tiled=True)


def on_device(
    tokens,
    ln1_gain,
    ln1_bias,
    w_qkv,
    w_out,
    ln2_gain,
    ln2_bias,
    w_router,
    w_in,
    b_in,
    w_back,
    b_back,
    lengths,
    routes,
    priority,
    padding,
    cotangent,
):
    experts = lax.axis_size("exp")
    reps = lax.axis_size("rep")
    devices = experts * reps
    capacity = (TOK_DEV * 210 + experts * 100 - 1) // (experts * 100)
    padded = -(-(capacity + 3) // 16) * 16
    rows = w_qkv.shape[0]
    small = jnp.concatenate(
        [w_router, jnp.stack([ln1_gain, ln1_bias, ln2_gain, ln2_bias], axis=1)], axis=1
    )
    small = jnp.pad(small, ((0, 0), (0, LANES - small.shape[1])))
    rest = jnp.concatenate([w_out, small], axis=1)
    qkv_weight, rest_weight = gather_blocks(w_qkv, rest, devices, reps)
    qkv_weight = qkv_weight.reshape(D, 3 * D)
    rest_weight = rest_weight.reshape(D, rest.shape[1])
    out_weight = rest_weight[:, :D]
    router_weight = rest_weight[:, D : D + experts]
    vectors = rest_weight[:, D + experts : D + experts + 4].T
    gain_one, bias_one, gain_two, bias_two = (vectors[0], vectors[1], vectors[2], vectors[3])

    first_hot, second_hot, pick_first, pick_second = dispatch_tables(
        routes, priority, padding, experts, capacity, padded
    )
    picks = pick_first + pick_second
    grad_blocks = lax.dot_general(picks, cotangent, contract_first, preferred_element_type=jnp.float32)
    grad_blocks = grad_blocks.astype(jnp.bfloat16).reshape(experts, padded, D)
    grad_blocks, gathered_done = lax.optimization_barrier((grad_blocks, qkv_weight))
    qkv_weight = gathered_done
    grad_arrived = exchange(grad_blocks)

    inputs = tokens.astype(jnp.float32)
    normed, normal_one, inverse_one = norm_forward(inputs, gain_one, bias_one)
    normed_low = normed.astype(jnp.bfloat16)
    qkv = (
        jnp.dot(normed_low, qkv_weight, preferred_element_type=jnp.float32)
        .astype(jnp.bfloat16)
        .reshape(ROWS_DEV, SLOTS, 3 * D)
    )
    bounds = jnp.cumsum(lengths[0])
    segments = jnp.sum(
        (jnp.arange(SLOTS, dtype=jnp.int32)[:, None] >= bounds[None, :]).astype(jnp.int32), axis=1
    )
    mixed_low = attend(qkv[0], segments, padding)
    resid = inputs + jnp.dot(mixed_low, out_weight, preferred_element_type=jnp.float32)
    routed_float, normal_two, inverse_two = norm_forward(resid, gain_two, bias_two)
    routed = routed_float.astype(jnp.bfloat16)
    logits = jnp.dot(routed, router_weight, preferred_element_type=jnp.float32)
    probs = jax.nn.softmax(logits, axis=-1)
    gate_first = jnp.sum(probs * first_hot, axis=1)
    gate_second = jnp.sum(probs * second_hot, axis=1)
    buffer = lax.dot_general(picks, routed, contract_first, preferred_element_type=jnp.float32)
    buffer = buffer.astype(jnp.bfloat16).reshape(experts, padded, D)
    slot_gates = jnp.sum(
        pick_first.astype(jnp.float32) * gate_first[:, None]
        + pick_second.astype(jnp.float32) * gate_second[:, None],
        axis=0,
    ).reshape(experts, padded)[:, :capacity]
    high = lax.reduce_precision(slot_gates, 8, 7)
    middle = lax.reduce_precision(slot_gates - high, 8, 7)
    terms = jnp.stack([high, middle, slot_gates - high - middle], axis=1).astype(jnp.bfloat16)
    terms = jnp.pad(terms, ((0, 0), (0, padded - capacity - 3), (0, D - capacity)))
    buffer = lax.dynamic_update_slice(buffer, terms, (0, capacity, 0))
    grad_buffer, result, half_back, half_in = run_experts(
        buffer, grad_arrived, w_in[0], w_back[0], b_in, b_back, capacity, reps
    )
    terms = grad_buffer[:, capacity : capacity + 3, :padded].transpose(1, 0, 2)
    terms = jnp.pad(terms.reshape(3, experts * padded), ((0, 13), (0, 0)))
    (
        output,
        grad_tokens,
        sum_qkv,
        sum_out,
        sum_small,
        all_back,
        all_in,
        all_tail,
    ) = run_backward(
        (
            grad_buffer.reshape(experts * padded, D),
            result,
            pick_first,
            pick_second,
            terms,
            jnp.pad(probs, ((0, 0), (0, LANES - experts))),
            routes,
            cotangent,
            resid,
            tokens,
            normed_low,
            routed,
            qkv[0],
            mixed_low,
            qkv_weight,
            rest_weight,
            vectors.astype(jnp.float32),
            segments.reshape(SLOTS, 1),
            segments.reshape(1, SLOTS),
            padding.reshape(SLOTS, 1),
            half_back,
            half_in,
        ),
        experts,
        reps,
        rows,
    )
    vector_sums = sum_small[:, experts : experts + 4]
    hidden = b_in.shape[1]
    piece = hidden // reps
    return (
        output,
        grad_tokens,
        vector_sums[:, 0],
        vector_sums[:, 1],
        sum_qkv,
        sum_out,
        vector_sums[:, 2],
        vector_sums[:, 3],
        sum_small[:, :experts],
        all_in[None].astype(jnp.float32),
        all_tail[:, 0, :piece].astype(jnp.float32).reshape(1, hidden),
        all_back[None].astype(jnp.float32),
        all_tail[:1, 1, :].astype(jnp.float32),
    )


def solution(mesh):
    return jax.shard_map(
        on_device,
        mesh=mesh,
        in_specs=(
            P(("exp", "rep"), None),
            P(("exp", "rep")),
            P(("exp", "rep")),
            P(("exp", "rep"), None),
            P(("exp", "rep"), None),
            P(("exp", "rep")),
            P(("exp", "rep")),
            P(("exp", "rep"), None),
            P("exp", None, None),
            P("exp", None),
            P("exp", None, None),
            P("exp", None),
            P(("exp", "rep"), None),
            P(("exp", "rep"), None),
            P(("exp", "rep")),
            P(("exp", "rep")),
            P(("exp", "rep"), None),
        ),
        out_specs=(
            P(("exp", "rep"), None),
            P(("exp", "rep"), None),
            P(("exp", "rep")),
            P(("exp", "rep")),
            P(("exp", "rep"), None),
            P(("exp", "rep"), None),
            P(("exp", "rep")),
            P(("exp", "rep")),
            P(("exp", "rep"), None),
            P("exp", None, None),
            P("exp", None),
            P("exp", None, None),
            P("exp", None),
        ),
        check_vma=False,
    )
```

```python
import functools

import jax
import jax.numpy as jnp
from jax import lax
from jax.experimental import pallas as pl
from jax.experimental.pallas import tpu as pltpu
from jax.sharding import PartitionSpec as P

D = 768
HEADS = 12
HEAD = 64
SLOTS = 576
ROWS_DEV = 1
TOK_DEV = 576


root_half = 0.7071067811865476
inverse_root_tau = 0.3989422804014327
contract_first = (((0,), (0,)), ((), ()))
contract_last = (((1,), (1,)), ((), ()))


def norm_forward(inputs, gain, offset):
    center = inputs - jnp.mean(inputs, axis=-1, keepdims=True)
    inverse = lax.rsqrt(jnp.mean(center * center, axis=-1, keepdims=True) + 1e-06)
    normal = center * inverse
    return (normal * gain.astype(jnp.float32) + offset.astype(jnp.float32), normal, inverse)


def dispatch_tables(routes, priority, padding, experts, capacity, padded):
    labels = jnp.arange(experts, dtype=jnp.int32)
    first_hot = (routes[:, 0:1] == labels[None, :]).astype(jnp.bfloat16)
    second_hot = (routes[:, 1:2] == labels[None, :]).astype(jnp.bfloat16)
    live = padding[:, None].astype(jnp.bfloat16)
    earlier = (priority[None, :] < priority[:, None]).astype(jnp.bfloat16)
    before_first = jnp.dot(earlier, first_hot * live, preferred_element_type=jnp.float32)
    first_counts = jnp.sum((first_hot * live).astype(jnp.float32), axis=0)
    before_second = (
        jnp.dot(earlier, second_hot * live, preferred_element_type=jnp.float32)
        + first_counts[None, :]
    )
    place_first = jnp.sum(before_first * first_hot, axis=1).astype(jnp.int32)
    place_second = jnp.sum(before_second * second_hot, axis=1).astype(jnp.int32)
    kept_first = (padding == 1) & (place_first < capacity)
    kept_second = (padding == 1) & (place_second < capacity)
    slot_labels = jnp.arange(experts * padded, dtype=jnp.int32)
    slot_first = routes[:, 0] * padded + place_first
    slot_second = routes[:, 1] * padded + place_second
    pick_first = ((slot_first[:, None] == slot_labels[None, :]) & kept_first[:, None]).astype(
        jnp.bfloat16
    )
    pick_second = ((slot_second[:, None] == slot_labels[None, :]) & kept_second[:, None]).astype(
        jnp.bfloat16
    )
    return (first_hot.astype(jnp.float32), second_hot.astype(jnp.float32), pick_first, pick_second)


LANES = 128
MESH_ID = pl.DeviceIdType.MESH


def bit_count(number):
    return number.bit_length() - 1


def flip(position, bit):
    step = 1 << bit
    return position + (1 - 2 * lax.rem(lax.div(position, step), 2)) * step


def coordinates(position, reps):
    return (lax.div(position, reps), lax.rem(position, reps))


def greet(bits, me, reps):
    barrier = pltpu.get_barrier_semaphore()
    for bit in range(bits):
        pl.semaphore_signal(
            barrier, inc=1, device_id=coordinates(flip(me, bit), reps), device_id_type=MESH_ID
        )
    pl.semaphore_wait(barrier, bits)


def lowest_bit(number):
    return (number & -number).bit_length() - 1


def gather_kernel(devices, reps, pieces, qkv_ref, rest_ref, all_qkv_ref, all_rest_ref, send_sem, recv_sem, local_sem):
    bits = bit_count(devices)
    me = lax.axis_index("exp") * reps + lax.axis_index("rep")
    greet(bits, me, reps)
    own = (qkv_ref, rest_ref)
    everywhere = (all_qkv_ref, all_rest_ref)
    locals_ = [
        pltpu.make_async_copy(own[k], everywhere[k].at[me], local_sem.at[k]) for k in range(2)
    ]
    for copy in locals_:
        copy.start()

    def owner_of(distance, order):
        found = me
        for bit in range(bits):
            if distance >> bit & 1:
                found = flip(found, order[bit])
        return found

    def block(number, owner):
        array, start, width, _ = pieces[number]
        return everywhere[array].at[owner, :, pl.ds(start, width)]

    def transfer(number, distance, bit):
        array, start, width, order = pieces[number]
        owner = owner_of(distance, order)
        index = distance + (1 << bit)
        source = own[array].at[:, pl.ds(start, width)] if distance == 0 else block(number, owner)
        return pltpu.make_async_remote_copy(
            src_ref=source,
            dst_ref=block(number, owner),
            send_sem=send_sem.at[number, index],
            recv_sem=recv_sem.at[number, index],
            device_id=coordinates(flip(me, order[bit]), reps),
            device_id_type=MESH_ID,
        )

    def arrival(number, distance):
        order = pieces[number][3]
        owner = owner_of(distance, order)
        return pltpu.make_async_remote_copy(
            src_ref=block(number, owner),
            dst_ref=block(number, owner),
            send_sem=send_sem.at[number, distance],
            recv_sem=recv_sem.at[number, distance],
            device_id=coordinates(flip(me, order[lowest_bit(distance)]), reps),
            device_id_type=MESH_ID,
        )

    sent = []
    for bit in range(bits):
        for number in range(len(pieces)):
            copy = transfer(number, 0, bit)
            copy.start()
            sent.append(copy)
    sequence = sorted(range(1, devices), key=lambda d: (bin(d).count("1"), -d))
    last = []
    for distance in sequence:
        low = lowest_bit(distance)
        for number in range(len(pieces)):
            if low == 0:
                last.append((number, distance))
                continue
            arrival(number, distance).wait_recv()
            for bit in range(low):
                copy = transfer(number, distance, bit)
                copy.start()
                sent.append(copy)
    for number, distance in last:
        arrival(number, distance).wait_recv()
    for copy in sent:
        copy.wait_send()
    for copy in locals_:
        copy.wait()


def gather_blocks(qkv, rest, devices, reps):
    bits = bit_count(devices)
    plain = list(range(bits))
    low = bit_count(reps)
    turned = list(plain)
    turned[low - 1], turned[low] = (plain[low], plain[low - 1])
    pieces = [(0, 0, 2 * D, plain), (0, 2 * D, D, turned), (1, 0, rest.shape[1], turned)]
    anywhere = pl.BlockSpec(memory_space=pl.ANY)
    return pl.pallas_call(
        functools.partial(gather_kernel, devices, reps, pieces),
        out_shape=[
            jax.ShapeDtypeStruct((devices,) + qkv.shape, qkv.dtype),
            jax.ShapeDtypeStruct((devices,) + rest.shape, rest.dtype),
        ],
        in_specs=[anywhere] * 2,
        out_specs=[anywhere] * 2,
        scratch_shapes=[
            pltpu.SemaphoreType.DMA((len(pieces), devices)),
            pltpu.SemaphoreType.DMA((len(pieces), devices)),
            pltpu.SemaphoreType.DMA((2,)),
        ],
        compiler_params=pltpu.CompilerParams(collective_id=0, has_side_effects=True),
        name="gather_dense",
    )(qkv, rest)


def row_of(column, width):
    count = column.shape[0]
    down = lax.broadcasted_iota(jnp.int32, (count, width), 0)
    across = lax.broadcasted_iota(jnp.int32, (count, width), 1)
    return jnp.sum(jnp.where(down == across, column, 0.0), axis=0, keepdims=True)


def column_of(row, count):
    width = row.shape[1]
    down = lax.broadcasted_iota(jnp.int32, (count, width), 0)
    across = lax.broadcasted_iota(jnp.int32, (count, width), 1)
    return jnp.sum(jnp.where(down == across, row, 0.0), axis=1, keepdims=True)


def three_terms(value):
    high = value.astype(jnp.bfloat16).astype(jnp.float32)
    rest = value - high
    middle = rest.astype(jnp.bfloat16).astype(jnp.float32)
    return (high, middle, rest - middle)


def expert_kernel(
    experts,
    capacity,
    padded,
    block,
    send_ref,
    grad_ref,
    w_in_ref,
    w_back_ref,
    b_in_ref,
    b_back_ref,
    return_ref,
    result_ref,
    half_back_ref,
    half_in_ref,
    slots,
    grads,
    gated,
    weight_in,
    weight_back,
    active,
    grad_pre,
    back_rows,
    result_rows,
    result_total,
    back_total,
    away_back,
    away_in,
    other_back,
    other_in,
    came_back,
    load_sem,
    send_sem,
    recv_sem,
    return_send_sem,
    return_recv_sem,
    result_sem,
    core_send,
    core_recv,
    along_send,
    along_recv,
    stage_sem,
):
    mine = lax.axis_index("exp")
    rep = lax.axis_index("rep")
    bits = bit_count(experts)
    groups = experts // 2
    hidden = weight_in.shape[1]
    steps = hidden // block
    lanes = 256 if capacity <= 256 else D
    gate_row = capacity - (padded - 16)

    barrier = pltpu.get_barrier_semaphore()

    def greet_one(step, carry):
        other = lax.rem(mine + step, experts)
        pl.semaphore_signal(barrier, inc=1, device_id=(other, rep), device_id_type=MESH_ID)
        return carry

    lax.fori_loop(1, experts, greet_one, 0)
    core = lax.rem(rep, 2)
    partner = (mine, flip(rep, 0))
    pl.semaphore_signal(barrier, inc=1, device_id=partner, device_id_type=MESH_ID)
    half = away_in.shape[0]
    along = lax.div(rep, 2)

    def greet_along(step, carry):
        other = 2 * lax.rem(along + step, half) + core
        pl.semaphore_signal(barrier, inc=1, device_id=(mine, other), device_id_type=MESH_ID)
        return carry

    lax.fori_loop(1, half, greet_along, 0)

    def group_of(index):
        half = lax.div(mine, 2)
        found = half
        for bit in range(bits - 1):
            found = found + lax.rem(lax.div(index, 1 << bit), 2) * (
                (1 - 2 * lax.rem(lax.div(half, 1 << bit), 2)) * (1 << bit)
            )
        return found

    def place(expert):
        return pl.ds(pl.multiple_of(expert * padded, 16), padded)

    def outgoing(expert):
        return pltpu.make_async_remote_copy(
            src_ref=send_ref.at[expert],
            dst_ref=slots.at[place(mine)],
            send_sem=send_sem.at[expert],
            recv_sem=recv_sem.at[mine],
            device_id=(expert, rep),
            device_id_type=MESH_ID,
        )

    def incoming(expert):
        return pltpu.make_async_remote_copy(
            src_ref=send_ref.at[mine],
            dst_ref=slots.at[place(expert)],
            send_sem=send_sem.at[expert],
            recv_sem=recv_sem.at[expert],
            device_id=(expert, rep),
            device_id_type=MESH_ID,
        )

    def going_back(expert):
        return pltpu.make_async_remote_copy(
            src_ref=back_rows.at[place(expert)],
            dst_ref=return_ref.at[mine],
            send_sem=return_send_sem.at[expert],
            recv_sem=return_recv_sem.at[mine],
            device_id=(expert, rep),
            device_id_type=MESH_ID,
        )

    def coming_back(expert):
        return pltpu.make_async_remote_copy(
            src_ref=back_rows.at[place(expert)],
            dst_ref=return_ref.at[expert],
            send_sem=return_send_sem.at[expert],
            recv_sem=return_recv_sem.at[expert],
            device_id=(expert, rep),
            device_id_type=MESH_ID,
        )

    neighbour = flip(mine, 0)
    side = lax.rem(mine, 2)
    loads = [
        pltpu.make_async_copy(send_ref.at[mine], slots.at[place(mine)], load_sem.at[0]),
        pltpu.make_async_copy(grad_ref, grads, load_sem.at[1]),
        pltpu.make_async_copy(w_in_ref, weight_in, load_sem.at[2]),
        pltpu.make_async_copy(w_back_ref, weight_back, load_sem.at[3]),
    ]
    for copy in loads:
        copy.start()
    pl.semaphore_wait(barrier, experts + half - 1)

    def send_group(index):
        pair = group_of(index)
        outgoing(2 * pair + side).start()
        outgoing(2 * pair + 1 - side).start()

    half_pair = lax.div(mine, 2)
    inner = lax.rem(lax.rem(half_pair, 2) + lax.div(half_pair, 2), 2)

    def turn(index):
        if groups != 4:
            return index
        high, low = (lax.div(index, 2), lax.rem(index, 2))
        return inner * (2 * high + lax.rem(low + high, 2)) + (1 - inner) * (2 * low + high)

    outgoing(neighbour).start()

    def send_step(step, carry):
        if groups == 4:
            send_group(inner * (lax.rem(step + 1, 3) + 1) + (1 - inner) * (step + 1))
        else:
            send_group(step + 1)
        return carry

    lax.fori_loop(0, groups - 1, send_step, 0)
    for copy in loads:
        copy.wait()

    def send_back_group(index):
        pair = group_of(index)
        going_back(2 * pair + side).start()
        going_back(2 * pair + 1 - side).start()

    def gate_columns(expert):
        tail = slots[pl.ds(pl.multiple_of(expert * padded + padded - 16, 16), 16), :].astype(jnp.float32)
        row = jnp.sum(tail[gate_row : gate_row + 3, :lanes], axis=0, keepdims=True)
        return column_of(row, padded)

    def group_step(index, carry):
        pair = group_of(turn(index))

        @pl.when(index == 0)
        def _():
            incoming(neighbour).wait_recv()

        @pl.when(index > 0)
        def _():
            incoming(2 * pair).wait_recv()
            incoming(2 * pair + 1).wait_recv()

        @pl.when(index == 1)
        def _():
            going_back(neighbour).start()

        @pl.when(index > 1)
        def _():
            send_back_group(turn(index - 1))

        here = pl.ds(pl.multiple_of(pair * 2 * padded, 16), 2 * padded)
        for member in range(2):
            spot = place(2 * pair + member)
            gate = gate_columns(2 * pair + member)
            gated[spot, :] = (gate * grads[spot, :].astype(jnp.float32)).astype(jnp.bfloat16)

        def hidden_step(step, inner):
            columns = pl.ds(pl.multiple_of(step * block, block), block)
            pre = (
                jnp.dot(slots[here, :], weight_in[:, columns], preferred_element_type=jnp.float32)
                + b_in_ref[:, columns]
            )
            grad_active = lax.dot_general(
                gated[here, :],
                weight_back[columns, :],
                contract_last,
                preferred_element_type=jnp.float32,
            )
            cumulative = 0.5 * (1.0 + lax.erf(pre * root_half))
            slope = cumulative + pre * inverse_root_tau * jnp.exp(-0.5 * pre * pre)
            active_low = (pre * cumulative).astype(jnp.bfloat16)
            grad_low = (grad_active * slope).astype(jnp.bfloat16)
            active[here, columns] = active_low
            grad_pre[here, columns] = grad_low
            result_part = jnp.dot(
                active_low, weight_back[columns, :], preferred_element_type=jnp.float32
            )
            back_part = lax.dot_general(
                grad_low, weight_in[:, columns], contract_last, preferred_element_type=jnp.float32
            )

            @pl.when(step == 0)
            def _():
                result_total[...] = result_part
                back_total[...] = back_part

            @pl.when(step > 0)
            def _():
                result_total[...] += result_part
                back_total[...] += back_part

            return inner

        lax.fori_loop(0, steps, hidden_step, 0)
        for member in range(2):
            expert = 2 * pair + member
            span = slice(member * padded, (member + 1) * padded)
            spot = place(expert)
            result_low = (result_total[span, :] + b_back_ref[...]).astype(jnp.bfloat16)
            result_rows[spot, :] = result_low
            grad_gate = jnp.sum(
                grads[spot, :].astype(jnp.float32) * result_low.astype(jnp.float32),
                axis=1,
                keepdims=True,
            )
            gate_line = row_of(
                jnp.where(
                    lax.broadcasted_iota(jnp.int32, (padded, 1), 0) < capacity, grad_gate, 0.0
                ),
                lanes,
            )
            if lanes < D:
                gate_line = jnp.concatenate(
                    [gate_line, jnp.zeros((1, D - lanes), jnp.float32)], axis=1
                )
            high, middle, lowest = three_terms(gate_line)
            row = lax.broadcasted_iota(jnp.int32, (padded, D), 0)
            value = back_total[span, :]
            value = jnp.where(row == capacity, high, value)
            value = jnp.where(row == capacity + 1, middle, value)
            value = jnp.where(row == capacity + 2, lowest, value)
            back_rows[spot, :] = value.astype(jnp.bfloat16)
        return carry

    lax.fori_loop(0, groups, group_step, 0)
    own_back = pltpu.make_async_copy(back_rows.at[place(mine)], return_ref.at[mine], load_sem.at[0])
    own_back.start()
    results = pltpu.make_async_copy(result_rows, result_ref, result_sem)
    results.start()

    piece = away_in.shape[2]
    bias_back = jnp.sum(gated[...].astype(jnp.float32), axis=0, keepdims=True)

    def columns_of(number):
        return pl.ds(pl.multiple_of(number * piece, LANES), piece)

    def back_sums(number):
        columns = columns_of(number)
        back = lax.dot_general(
            active[:, columns], gated[...], contract_first, preferred_element_type=jnp.float32
        )
        bias_in = jnp.sum(grad_pre[:, columns].astype(jnp.float32), axis=0, keepdims=True)
        if piece < D:
            bias_in = jnp.concatenate([bias_in, jnp.zeros((1, D - piece), jnp.float32)], axis=1)
        row = lax.broadcasted_iota(jnp.int32, (16, D), 0)
        extra = jnp.where(row == 0, bias_in, jnp.where(row == 1, bias_back, 0.0))
        return (back, extra)

    def in_sums(number):
        return lax.dot_general(
            slots[...],
            grad_pre[:, columns_of(number)],
            contract_first,
            preferred_element_type=jnp.float32,
        )

    def core_copy(kind, index):
        source, target = ((away_back, other_back), (away_in, other_in))[kind]
        return pltpu.make_async_remote_copy(
            src_ref=source.at[index],
            dst_ref=target.at[index],
            send_sem=core_send.at[kind, index],
            recv_sem=core_recv.at[kind, index],
            device_id=partner,
            device_id_type=MESH_ID,
        )

    def along_copy(step):
        other = lax.rem(along + step, half)
        return pltpu.make_async_remote_copy(
            src_ref=other_back.at[other],
            dst_ref=came_back.at[step - 1],
            send_sem=along_send.at[step - 1],
            recv_sem=along_recv.at[step - 1],
            device_id=(mine, 2 * other + core),
            device_id_type=MESH_ID,
        )

    def away_back_step(step, carry):
        index = lax.rem(along + step, half)
        back, extra = back_sums(2 * index + 1 - core)
        away_back[index, :piece, :] = back.astype(jnp.bfloat16)
        away_back[index, piece:, :] = extra.astype(jnp.bfloat16)
        core_copy(0, index).start()
        return carry

    def kept_back_step(step, carry):
        index = lax.rem(along + step, half)
        back, extra = back_sums(2 * index + core)
        core_copy(0, index).wait_recv()
        other_back[index, :piece, :] = (
            back + other_back[index, :piece, :].astype(jnp.float32)
        ).astype(jnp.bfloat16)
        other_back[index, piece:, :] = (
            extra + other_back[index, piece:, :].astype(jnp.float32)
        ).astype(jnp.bfloat16)

        @pl.when(step < half)
        def _():
            along_copy(step).start()

        return carry

    def away_in_step(index, carry):
        away_in[index] = in_sums(2 * index + 1 - core).astype(jnp.bfloat16)
        core_copy(1, index).start()
        return carry

    def kept_in_copy(index):
        return pltpu.make_async_copy(other_in.at[index], half_in_ref.at[index], stage_sem.at[index])

    def kept_in_step(index, carry):
        inward = in_sums(2 * index + core)
        core_copy(1, index).wait_recv()
        other_in[index] = (inward + other_in[index].astype(jnp.float32)).astype(jnp.bfloat16)
        kept_in_copy(index).start()
        return carry


    def back_step(step, carry):
        away_back_step(step, 0)
        kept_back_step(step, 0)
        return carry

    lax.fori_loop(1, half + 1, back_step, 0)
    if groups > 1:
        send_back_group(turn(groups - 1))
    else:
        going_back(neighbour).start()
    lax.fori_loop(0, half, away_in_step, 0)
    lax.fori_loop(0, half, kept_in_step, 0)
    for step in range(1, half):
        along_copy(step).wait_recv()

    def along_sum(step, carry):
        here = pl.ds(pl.multiple_of(step * 16, 16), 16)
        total = other_back[along, here, :].astype(jnp.float32)
        for came in range(half - 1):
            total = total + came_back[came, here, :].astype(jnp.float32)
        other_back[along, here, :] = total.astype(jnp.bfloat16)
        return carry

    lax.fori_loop(0, (piece + 16) // 16, along_sum, 0)
    sum_back = pltpu.make_async_copy(other_back.at[along], half_back_ref, stage_sem.at[half])
    sum_back.start()
    sum_back.wait()
    for step in range(1, half):
        along_copy(step).wait_send()
    for index in range(half):
        kept_in_copy(index).wait()
        for kind in range(2):
            core_copy(kind, index).wait_send()
    own_back.wait()
    results.wait()

    def finish(step, carry):
        other = lax.rem(mine + step, experts)
        outgoing(other).wait_send()
        going_back(other).wait_send()
        coming_back(other).wait_recv()
        return carry

    lax.fori_loop(1, experts, finish, 0)


def run_experts(buffer, grads, w_in, w_back, b_in, b_back, capacity, reps):
    experts, padded = (buffer.shape[0], buffer.shape[1])
    hidden = w_in.shape[1]
    block = 512
    rows = experts * padded
    half = reps // 2
    piece = hidden // reps
    low = jnp.bfloat16
    anywhere = pl.BlockSpec(memory_space=pl.ANY)
    inside = pl.BlockSpec(memory_space=pltpu.VMEM)
    return pl.pallas_call(
        functools.partial(expert_kernel, experts, capacity, padded, block),
        out_shape=[
            jax.ShapeDtypeStruct((experts, padded, D), low),
            jax.ShapeDtypeStruct((rows, D), low),
            jax.ShapeDtypeStruct((piece + 16, D), low),
            jax.ShapeDtypeStruct((half, D, piece), low),
        ],
        in_specs=[anywhere, anywhere, anywhere, anywhere, inside, inside],
        out_specs=[anywhere, anywhere, anywhere, anywhere],
        scratch_shapes=[
            pltpu.VMEM((rows, D), low),
            pltpu.VMEM((rows, D), low),
            pltpu.VMEM((rows, D), low),
            pltpu.VMEM((D, hidden), low),
            pltpu.VMEM((hidden, D), low),
            pltpu.VMEM((rows, hidden), low),
            pltpu.VMEM((rows, hidden), low),
            pltpu.VMEM((rows, D), low),
            pltpu.VMEM((rows, D), low),
            pltpu.VMEM((2 * padded, D), jnp.float32),
            pltpu.VMEM((2 * padded, D), jnp.float32),
            pltpu.VMEM((half, piece + 16, D), low),
            pltpu.VMEM((half, D, piece), low),
            pltpu.VMEM((half, piece + 16, D), low),
            pltpu.VMEM((half, D, piece), low),
            pltpu.VMEM((half - 1, piece + 16, D), low),
            pltpu.SemaphoreType.DMA((4,)),
            pltpu.SemaphoreType.DMA((experts,)),
            pltpu.SemaphoreType.DMA((experts,)),
            pltpu.SemaphoreType.DMA((experts,)),
            pltpu.SemaphoreType.DMA((experts,)),
            pltpu.SemaphoreType.DMA,
            pltpu.SemaphoreType.DMA((2, half)),
            pltpu.SemaphoreType.DMA((2, half)),
            pltpu.SemaphoreType.DMA((half - 1,)),
            pltpu.SemaphoreType.DMA((half - 1,)),
            pltpu.SemaphoreType.DMA((half + 1,)),
        ],
        compiler_params=pltpu.CompilerParams(
            collective_id=2, has_side_effects=True, vmem_limit_bytes=63 * 1024 * 1024
        ),
        cost_estimate=pl.CostEstimate(
            flops=12 * rows * D * hidden, bytes_accessed=40 << 20, transcendentals=2 * rows * hidden
        ),
        name="experts",
    )(buffer, grads.reshape(rows, D), w_in, w_back, b_in.astype(jnp.float32), b_back.astype(jnp.float32))


def attend_kernel(segment_col, segment_row, live_row, query_ref, keys_ref, values_ref, mixed_ref, bias):
    @pl.when(pl.program_id(0) == 0)
    def _():
        row = lax.broadcasted_iota(jnp.int32, (SLOTS, SLOTS), 0)
        column = lax.broadcasted_iota(jnp.int32, (SLOTS, SLOTS), 1)
        seen = (segment_col[...] == segment_row[...]) & ((live_row[...] == 1) | (row == column))
        bias[...] = jnp.where(seen, 0.0, -1e30)

    for side in range(2):
        lanes = slice(side * HEAD, (side + 1) * HEAD)
        scores = lax.dot_general(
            query_ref[:, lanes], keys_ref[:, lanes], contract_last, preferred_element_type=jnp.float32
        )
        scores = scores * HEAD ** (-0.5) + bias[...]
        expo = jnp.exp(scores - jnp.max(scores, axis=1, keepdims=True))
        total = jnp.sum(expo, axis=1, keepdims=True)
        probs = (expo * (1.0 / total)).astype(jnp.bfloat16)
        mixed = jnp.dot(probs, values_ref[:, lanes], preferred_element_type=jnp.float32)
        mixed_ref[:, lanes] = mixed.astype(jnp.bfloat16)


def attend(qkv, segments, live):
    pairs = HEADS // 2
    return pl.pallas_call(
        attend_kernel,
        grid=(pairs,),
        out_shape=jax.ShapeDtypeStruct((SLOTS, D), jnp.bfloat16),
        in_specs=[
            pl.BlockSpec((SLOTS, 1), lambda i: (0, 0)),
            pl.BlockSpec((1, SLOTS), lambda i: (0, 0)),
            pl.BlockSpec((1, SLOTS), lambda i: (0, 0)),
            pl.BlockSpec((SLOTS, 2 * HEAD), lambda i: (0, i)),
            pl.BlockSpec((SLOTS, 2 * HEAD), lambda i: (0, pairs + i)),
            pl.BlockSpec((SLOTS, 2 * HEAD), lambda i: (0, 2 * pairs + i)),
        ],
        out_specs=pl.BlockSpec((SLOTS, 2 * HEAD), lambda i: (0, i)),
        scratch_shapes=[pltpu.VMEM((SLOTS, SLOTS), jnp.float32)],
        cost_estimate=pl.CostEstimate(
            flops=16 * HEADS * SLOTS * SLOTS * HEAD, bytes_accessed=4 << 20, transcendentals=HEADS * SLOTS * SLOTS
        ),
        name="attend",
    )(segments.reshape(SLOTS, 1), segments.reshape(1, SLOTS), live.reshape(1, SLOTS), qkv, qkv, qkv)


BAND = 48


def fold_rows(values):
    return jnp.sum(values.reshape(BAND // 8, 8, values.shape[1]), axis=0)


def backward_kernel(
    experts,
    reps,
    chunks,
    summed,
    back_ref,
    result_ref,
    first_ref,
    second_ref,
    terms_ref,
    probs_ref,
    routes_ref,
    cotangent_ref,
    resid_ref,
    tokens_ref,
    normed_ref,
    routed_ref,
    qkv_ref,
    mixed_ref,
    qkv_weight_ref,
    rest_weight_ref,
    vectors_ref,
    segment_col,
    segment_row,
    live_col,
    half_back_ref,
    half_in_ref,
    output_ref,
    grad_tokens_ref,
    sum_qkv_ref,
    sum_out_ref,
    sum_small_ref,
    all_back_ref,
    all_in_ref,
    all_tail_ref,
    *refs,
):
    devices = experts * reps
    bits = bit_count(devices)
    half = reps // 2
    mine = lax.axis_index("exp")
    rep = lax.axis_index("rep")
    me = mine * reps + rep
    core = lax.rem(rep, 2)
    along = lax.div(rep, 2)
    (
        back,
        first,
        second,
        cotangent,
        resid,
        tokens,
        normed,
        routed,
        qkv,
        mixed,
        qkv_weight,
        rest_weight,
        returned,
        bias,
        wide,
        tall,
        grad_resid,
        grad_attn,
        grad_mixed,
        grad_qkv,
        grad_logits,
        own_in,
        other_in,
    ) = refs[:23]
    refs = refs[23:]
    lines, refs = (refs[0], refs[1:])
    count = len(chunks) if summed else 0
    parts, refs = (refs[:count], refs[count:])
    recvs, refs = ([refs[c * bits : (c + 1) * bits] for c in range(count)], refs[count * bits :])
    (
        load_sem,
        result_send,
        result_recv,
        dense_send,
        dense_recv,
        half_send,
        half_recv,
        all_send,
        all_recv,
        own_sem,
    ) = refs
    padded = result_ref.shape[0] // experts
    piece = half_in_ref.shape[2]

    barrier = pltpu.get_barrier_semaphore()

    def greet_expert(step, carry):
        other = lax.rem(mine + step, experts)
        pl.semaphore_signal(barrier, inc=1, device_id=(other, rep), device_id_type=MESH_ID)
        return carry

    def greet_rep(step, carry):
        other = lax.rem(rep + step, reps)
        pl.semaphore_signal(barrier, inc=1, device_id=(mine, other), device_id_type=MESH_ID)
        return carry

    lax.fori_loop(1, experts, greet_expert, 0)
    lax.fori_loop(1, reps, greet_rep, 0)

    sources = [
        (back_ref, back),
        (first_ref, first),
        (second_ref, second),
        (routed_ref, routed),
        (rest_weight_ref, rest_weight),
        (resid_ref, resid),
        (cotangent_ref, cotangent),
        (mixed_ref, mixed),
        (qkv_ref, qkv),
        (normed_ref, normed),
        (tokens_ref, tokens),
        (qkv_weight_ref, qkv_weight),
        (half_in_ref.at[along], own_in),
    ]
    loads = [
        pltpu.make_async_copy(source, target, load_sem.at[i])
        for i, (source, target) in enumerate(sources)
    ]
    for copy in loads:
        copy.start()
    pl.semaphore_wait(barrier, experts - 1 + reps - 1)

    def half_copy(step):
        other = lax.rem(along + step, half)
        return pltpu.make_async_remote_copy(
            src_ref=half_in_ref.at[other],
            dst_ref=other_in.at[step - 1],
            send_sem=half_send.at[step - 1],
            recv_sem=half_recv.at[step - 1],
            device_id=(mine, 2 * other + core),
            device_id_type=MESH_ID,
        )

    half_moves = [half_copy(step) for step in range(1, half)]
    for move in half_moves:
        move.start()

    def own_part(kind):
        return (half_back_ref.at[pl.ds(0, piece), :], own_in, half_back_ref.at[pl.ds(piece, 16), :])[kind]

    def landing(kind, owner):
        if kind == 0:
            return all_back_ref.at[pl.ds(pl.multiple_of(owner * piece, 16), piece), :]
        if kind == 1:
            return all_in_ref.at[:, pl.ds(pl.multiple_of(owner * piece, LANES), piece)]
        return all_tail_ref.at[owner]

    def spread(kind, source, owner, device, step):
        return pltpu.make_async_remote_copy(
            src_ref=source,
            dst_ref=landing(kind, owner),
            send_sem=all_send.at[kind, step],
            recv_sem=all_recv.at[kind, step],
            device_id=device,
            device_id_type=MESH_ID,
        )

    def own_moves(kind):
        moves = [pltpu.make_async_copy(own_part(kind), landing(kind, rep), own_sem.at[kind])]
        for step in range(1, half):
            other = lax.rem(along + step, half)
            moves.append(spread(kind, own_part(kind), rep, (mine, 2 * other + core), step))
        moves.append(spread(kind, own_part(kind), rep, (mine, flip(rep, 0)), 0))
        return moves

    for kind in (0, 2):
        for move in own_moves(kind):
            move.start()

    def place(expert):
        return pl.ds(pl.multiple_of(expert * padded, 16), padded)

    def result_copy(step):
        other = lax.rem(mine + step, experts)
        came = lax.rem(mine + experts - step, experts)
        return pltpu.make_async_remote_copy(
            src_ref=result_ref.at[place(other)],
            dst_ref=returned.at[place(mine)],
            send_sem=result_send.at[step],
            recv_sem=result_recv.at[step],
            device_id=(other, rep),
            device_id_type=MESH_ID,
        )

    def start_result(step, carry):
        result_copy(step).start()
        return carry

    own_result = pltpu.make_async_copy(
        result_ref.at[place(mine)], returned.at[place(mine)], result_send.at[0]
    )
    own_result.start()
    lax.fori_loop(1, experts, start_result, 0)

    row = lax.broadcasted_iota(jnp.int32, (SLOTS, SLOTS), 0)
    column = lax.broadcasted_iota(jnp.int32, (SLOTS, SLOTS), 1)
    seen = (segment_col[...] == segment_row[...]) & ((live_col[...] == 1) | (row == column))
    bias[...] = jnp.where(seen, 0.0, -1e30)

    for copy in loads[:5]:
        copy.wait()
    tall[...] = jnp.dot(first[...] + second[...], back[...], preferred_element_type=jnp.float32)
    gates_back = [
        jnp.sum(
            lax.dot_general(
                pick[...], terms_ref[...], contract_last, preferred_element_type=jnp.float32
            ),
            axis=1,
            keepdims=True,
        )
        for pick in (first, second)
    ]
    lane = lax.broadcasted_iota(jnp.int32, (SLOTS, LANES), 1)
    hots = [(lane == routes_ref[:, k : k + 1]).astype(jnp.float32) for k in range(2)]
    grad_probs = gates_back[0] * hots[0] + gates_back[1] * hots[1]
    probs = probs_ref[...]
    grad_logits[...] = (
        probs * (grad_probs - jnp.sum(probs * grad_probs, axis=1, keepdims=True))
    ).astype(jnp.bfloat16)
    tall[...] += lax.dot_general(
        grad_logits[...], rest_weight[:, D:], contract_last, preferred_element_type=jnp.float32
    )
    for copy in loads[5:]:
        copy.wait()

    def band(step):
        return pl.ds(pl.multiple_of(step * BAND, 16), BAND)

    def norm_back(inputs, grad, gain):
        center = inputs - jnp.mean(inputs, axis=1, keepdims=True)
        inverse = lax.rsqrt(jnp.mean(center * center, axis=1, keepdims=True) + 1e-06)
        normal = center * inverse
        scaled = grad * gain
        grad_in = inverse * (
            scaled
            - jnp.mean(scaled, axis=1, keepdims=True)
            - normal * jnp.mean(scaled * normal, axis=1, keepdims=True)
        )
        return (grad_in, fold_rows(grad * normal), fold_rows(grad))

    zero = jnp.zeros((8, D), jnp.float32)

    def second_norm(step, carry):
        here = band(step)
        grad_in, grad_gain, grad_bias = norm_back(
            resid[here, :], tall[here, :], vectors_ref[2:3, :]
        )
        total = cotangent[here, :].astype(jnp.float32) + grad_in
        grad_resid[here, :] = total
        grad_attn[here, :] = total.astype(jnp.bfloat16)
        return (carry[0] + grad_gain, carry[1] + grad_bias)

    gain_two, bias_two = lax.fori_loop(0, SLOTS // BAND, second_norm, (zero, zero))

    lines[16:24, :] = gain_two
    lines[24:32, :] = bias_two

    own_bits = bit_count(reps)
    plan = [0] + list(range(own_bits, bits)) + list(range(own_bits - 1, 0, -1))
    my_bit = [lax.rem(lax.div(me, 1 << bit), 2) for bit in range(bits)]
    rows = parts[0].shape[4] if summed else 0
    stride = experts + bits - 1
    first_of = [sum(number for number, _ in chunks[:family]) for family in range(len(chunks))]

    def turned(number):
        length = bits - own_bits - 1
        found = 0
        for bit in range(length):
            found = found + lax.rem(lax.div(number, 1 << bit), 2) * (1 << (length - 1 - bit))
        return found

    def fill(family, c):
        width = chunks[family][1]

        def one(block, carry):
            owner = lax.div(block, reps)
            inner = lax.rem(block, reps)
            parts[family][c, owner, lax.div(inner, 2), lax.rem(inner, 2)] = wide[
                pl.ds(pl.multiple_of(block * rows, rows), rows), :width
            ].astype(jnp.bfloat16)
            return carry

        lax.fori_loop(0, devices, one, 0)

    def first_copy(family, c, expert):
        spot = lax.rem(expert, 2) * (devices // 4) + turned(lax.div(expert, 2)) * half
        index = (first_of[family] + c) * stride + expert
        return pltpu.make_async_remote_copy(
            src_ref=parts[family].at[c, expert, :, 1 - core],
            dst_ref=recvs[family][0].at[c, pl.ds(spot, half)],
            send_sem=dense_send.at[index],
            recv_sem=dense_recv.at[index],
            device_id=(mine, flip(rep, 0)),
            device_id_type=MESH_ID,
        )

    def later_copy(family, c, phase):
        size = devices >> (phase + 1)
        index = (first_of[family] + c) * stride + experts + phase - 1
        return pltpu.make_async_remote_copy(
            src_ref=recvs[family][phase - 1].at[c, pl.ds((1 - my_bit[plan[phase]]) * size, size)],
            dst_ref=recvs[family][phase].at[c],
            send_sem=dense_send.at[index],
            recv_sem=dense_recv.at[index],
            device_id=coordinates(flip(me, plan[phase]), reps),
            device_id_type=MESH_ID,
        )

    def columns_of(c, kind):
        return pl.ds(pl.multiple_of(c * LANES + kind * D, LANES), LANES)

    def send_chunk(family, c):
        if not summed:
            if family == 1:
                for kind in range(3):
                    span = slice(kind * LANES, (kind + 1) * LANES)
                    pltpu.sync_copy(wide.at[:, span], sum_qkv_ref.at[:, columns_of(c, kind)])
            else:
                out = sum_out_ref if family == 0 else sum_small_ref
                pltpu.sync_copy(wide.at[:, : chunks[family][1]], out)
            return
        fill(family, c)

        def one(expert, carry):
            first_copy(family, c, expert).start()
            return carry

        lax.fori_loop(0, experts, one, 0)

    def absorb(family, c, phase):
        if not summed:
            return
        size = devices >> (phase + 1)
        into = recvs[family][phase]
        if phase == 0:

            def arrived(expert, carry):
                first_copy(family, c, expert).wait_recv()
                return carry

            lax.fori_loop(0, experts, arrived, 0)

            def held(i):
                side = lax.div(i, devices // 4)
                rest = lax.rem(i, devices // 4)
                expert = 2 * turned(lax.div(rest, half)) + side
                return parts[family][c, expert, lax.rem(rest, half), core]
        else:
            later_copy(family, c, phase).wait_recv()
            base = my_bit[plan[phase]] * size

            def held(i):
                return recvs[family][phase - 1][c, base + i]

        if phase == bits - 1:
            total = into[c, 0].astype(jnp.float32) + held(0).astype(jnp.float32)
            if family == 1:
                for kind in range(3):
                    sum_qkv_ref[:, columns_of(c, kind)] = total[:, kind * LANES : (kind + 1) * LANES]
            elif family == 0:
                sum_out_ref[...] = total
            else:
                sum_small_ref[...] = total
            return

        def one(i, carry):
            into[c, i] = (into[c, i].astype(jnp.float32) + held(i).astype(jnp.float32)).astype(
                jnp.bfloat16
            )
            return carry

        lax.fori_loop(0, size, one, 0)
        later_copy(family, c, phase + 1).start()

    wide[...] = lax.dot_general(
        mixed[...], grad_attn[...], contract_first, preferred_element_type=jnp.float32
    )
    send_chunk(0, 0)
    grad_mixed[...] = lax.dot_general(
        grad_attn[...], rest_weight[:, :D], contract_last, preferred_element_type=jnp.float32
    ).astype(jnp.bfloat16)

    def complete():
        for move in half_moves:
            move.wait_recv()
        size = 16

        def one(step, carry):
            here = pl.ds(pl.multiple_of(step * size, 16), size)
            total = own_in[here, :].astype(jnp.float32)
            for came in range(half - 1):
                total = total + other_in[came, here, :].astype(jnp.float32)
            own_in[here, :] = total.astype(jnp.bfloat16)
            return carry

        lax.fori_loop(0, own_in.shape[0] // size, one, 0)
        for move in own_moves(1):
            move.start()

    partner = flip(rep, 0)

    def passed_on(kind, step):
        owner = 2 * lax.rem(along + half - step, half) + core
        return spread(kind, landing(kind, owner), owner, (mine, partner), half + step - 1)

    def pass_on(kind):
        for step in range(1, half):
            owner = 2 * lax.rem(along + half - step, half) + core
            spread(kind, landing(kind, owner), owner, (mine, owner), step).wait_recv()
            passed_on(kind, step).start()

    pairs = HEADS // 2

    def attend_back(pair):
        base = pl.multiple_of(pair * 2 * HEAD, 2 * HEAD)
        queries = qkv[:, pl.ds(base, 2 * HEAD)]
        keys = qkv[:, pl.ds(base + D, 2 * HEAD)]
        values = qkv[:, pl.ds(base + 2 * D, 2 * HEAD)]
        grads = grad_mixed[:, pl.ds(base, 2 * HEAD)]
        done = []
        for side in range(2):
            lanes = slice(side * HEAD, (side + 1) * HEAD)
            query, key, value, grad = (
                queries[:, lanes],
                keys[:, lanes],
                values[:, lanes],
                grads[:, lanes],
            )
            scores = lax.dot_general(key, query, contract_last, preferred_element_type=jnp.float32)
            scores = scores * HEAD ** (-0.5) + bias[...]
            expo = jnp.exp(scores - jnp.max(scores, axis=0, keepdims=True))
            weight = expo * (1.0 / jnp.sum(expo, axis=0, keepdims=True))
            grad_weight = lax.dot_general(
                value, grad, contract_last, preferred_element_type=jnp.float32
            )
            product = weight * grad_weight
            delta = jnp.sum(product, axis=0, keepdims=True)
            grad_scores = (product - weight * delta).astype(jnp.bfloat16)
            grad_value = jnp.dot(
                weight.astype(jnp.bfloat16), grad, preferred_element_type=jnp.float32
            )
            grad_key = jnp.dot(grad_scores, query, preferred_element_type=jnp.float32)
            grad_query = lax.dot_general(
                grad_scores, key, contract_first, preferred_element_type=jnp.float32
            )
            done.append(
                (grad_query * HEAD ** (-0.5), grad_key * HEAD ** (-0.5), grad_value)
            )
        block = jnp.concatenate(
            [jnp.concatenate([done[0][kind], done[1][kind]], axis=1) for kind in range(3)], axis=1
        ).astype(jnp.bfloat16)
        for kind in range(3):
            grad_qkv[:, pl.ds(base + kind * D, 2 * HEAD)] = block[:, kind * LANES : (kind + 1) * LANES]
        wide[:, : 3 * LANES] = lax.dot_general(
            normed[...], block, contract_first, preferred_element_type=jnp.float32
        )
        send_chunk(1, pair)

    def finish_tokens():
        tall[...] = lax.dot_general(
            grad_qkv[...], qkv_weight[...], contract_last, preferred_element_type=jnp.float32
        )

        def first_norm(step, carry):
            here = band(step)
            grad_in, grad_gain, grad_bias = norm_back(
                tokens[here, :].astype(jnp.float32), tall[here, :], vectors_ref[0:1, :]
            )
            grad_tokens_ref[here, :] = grad_resid[here, :] + grad_in
            return (carry[0] + grad_gain, carry[1] + grad_bias)

        gain_one, bias_one = lax.fori_loop(0, SLOTS // BAND, first_norm, (zero, zero))
        lines[0:8, :] = gain_one
        lines[8:16, :] = bias_one
        wide[:, :LANES] = lax.dot_general(
            routed[...], grad_logits[...], contract_first, preferred_element_type=jnp.float32
        )
        sums = [jnp.sum(lines[8 * k : 8 * k + 8, :], axis=0, keepdims=True) for k in range(4)]
        lane = lax.broadcasted_iota(jnp.int32, (LANES, LANES), 1)
        for part in range(D // LANES):
            span = slice(part * LANES, (part + 1) * LANES)
            block = wide[span, :LANES]
            for k in range(4):
                block = jnp.where(lane == experts + k, column_of(sums[k][:, span], LANES), block)
            wide[span, :LANES] = block
        send_chunk(2, 0)

    def finish_output():
        own_result.wait()

        def result_arrived(step, carry):
            result_copy(step).wait_recv()
            result_copy(step).wait_send()
            return carry

        lax.fori_loop(1, experts, result_arrived, 0)
        lane = lax.broadcasted_iota(jnp.int32, (SLOTS, LANES), 1)
        probs = probs_ref[...]
        gates = [
            jnp.sum(jnp.where(lane == routes_ref[:, k : k + 1], probs, 0.0), axis=1, keepdims=True)
            for k in range(2)
        ]
        tall[...] = resid[...] + gates[0] * jnp.dot(
            first[...], returned[...], preferred_element_type=jnp.float32
        )
        output_ref[...] = (
            tall[...]
            + gates[1] * jnp.dot(second[...], returned[...], preferred_element_type=jnp.float32)
        ).astype(jnp.bfloat16)

    slack = (0, 1, 4, 5, 8)

    def work(step, carry):
        @pl.when(step == 2)
        def _():
            complete()

        @pl.when(step < pairs)
        def _():
            attend_back(step)

        @pl.when(step == pairs)
        def _():
            finish_tokens()

        @pl.when(step == pairs + 1)
        def _():
            finish_output()

        @pl.when(step == pairs + 4)
        def _():
            pass_on(0)
            pass_on(2)

        for phase in range(bits):
            later = phase + slack[min(phase, 4)]

            @pl.when(step == later)
            def _():
                absorb(0, 0, phase)

            @pl.when(jnp.logical_and(step > later, step <= later + pairs))
            def _():
                absorb(1, step - 1 - later, phase)

            @pl.when(step == pairs + max(1, slack[-1] - 1) + phase)
            def _():
                absorb(2, 0, phase)

        return carry

    lax.fori_loop(0, pairs + bits + max(1, slack[-1]), work, 0)
    pass_on(1)
    for kind in (0, 2, 1):
        spread(kind, landing(kind, partner), partner, (mine, partner), 0).wait_recv()
        for step in range(1, half):
            owner = 2 * lax.rem(along + half - step, half) + 1 - core
            spread(
                kind, landing(kind, owner), owner, (mine, partner), half + step - 1
            ).wait_recv()
        moves = own_moves(kind)
        moves[0].wait()
        for move in moves[1:]:
            move.wait_send()
        for step in range(1, half):
            passed_on(kind, step).wait_send()
    for move in half_moves:
        move.wait_send()

    def dense_sent(family, c):
        def one(expert, carry):
            first_copy(family, c, expert).wait_send()
            return carry

        lax.fori_loop(0, experts, one, 0)
        for phase in range(1, bits):
            later_copy(family, c, phase).wait_send()

    def pair_sent(c, carry):
        dense_sent(1, c)
        return carry

    if summed:
        dense_sent(0, 0)
        lax.fori_loop(0, pairs, pair_sent, 0)
        dense_sent(2, 0)


def run_backward(operands, experts, reps, rows):
    devices = experts * reps
    bits = bit_count(devices)
    half = reps // 2
    (
        back,
        result,
        first,
        second,
        terms,
        probs,
        routes,
        cotangent,
        resid,
        tokens,
        normed,
        routed,
        qkv,
        mixed,
        qkv_weight,
        rest_weight,
        vectors,
        segment_col,
        segment_row,
        live_col,
        half_back,
        half_in,
    ) = operands
    low = jnp.bfloat16
    full = jnp.float32
    piece = half_in.shape[2]
    tail_rows = half_back.shape[0]
    chunks = [(1, D), (HEADS // 2, 3 * LANES), (1, LANES)]
    anywhere = pl.BlockSpec(memory_space=pl.ANY)
    inside = pl.BlockSpec(memory_space=pltpu.VMEM)
    slots = result.shape[0]
    scratch = [
        pltpu.VMEM((slots, D), low),
        pltpu.VMEM((SLOTS, slots), low),
        pltpu.VMEM((SLOTS, slots), low),
        pltpu.VMEM((SLOTS, D), low),
        pltpu.VMEM((SLOTS, D), full),
        pltpu.VMEM((SLOTS, D), low),
        pltpu.VMEM((SLOTS, D), low),
        pltpu.VMEM((SLOTS, D), low),
        pltpu.VMEM((SLOTS, 3 * D), low),
        pltpu.VMEM((SLOTS, D), low),
        pltpu.VMEM(qkv_weight.shape, low),
        pltpu.VMEM(rest_weight.shape, low),
        pltpu.VMEM((slots, D), low),
        pltpu.VMEM((SLOTS, SLOTS), full),
        pltpu.VMEM((D, D), full),
        pltpu.VMEM((SLOTS, D), full),
        pltpu.VMEM((SLOTS, D), full),
        pltpu.VMEM((SLOTS, D), low),
        pltpu.VMEM((SLOTS, D), low),
        pltpu.VMEM((SLOTS, 3 * D), low),
        pltpu.VMEM((SLOTS, LANES), low),
        pltpu.VMEM((D, piece), low),
        pltpu.VMEM((half - 1, D, piece), low),
    ]
    summed = rows % 8 == 0
    scratch.append(pltpu.VMEM((32, D), full))
    for number, width in chunks if summed else ():
        scratch.append(pltpu.VMEM((number, experts, half, 2, rows, width), low))
    for number, width in chunks if summed else ():
        for phase in range(bits):
            scratch.append(pltpu.VMEM((number, devices >> (phase + 1), rows, width), low))
    dense = sum(number for number, _ in chunks) * (experts + bits - 1)
    scratch = scratch + [
        pltpu.SemaphoreType.DMA((13,)),
        pltpu.SemaphoreType.DMA((experts,)),
        pltpu.SemaphoreType.DMA((experts,)),
        pltpu.SemaphoreType.DMA((dense,)),
        pltpu.SemaphoreType.DMA((dense,)),
        pltpu.SemaphoreType.DMA((half - 1,)),
        pltpu.SemaphoreType.DMA((half - 1,)),
        pltpu.SemaphoreType.DMA((3, reps)),
        pltpu.SemaphoreType.DMA((3, reps)),
        pltpu.SemaphoreType.DMA((3,)),
    ]
    call = pl.pallas_call(
        functools.partial(backward_kernel, experts, reps, chunks, summed),
        out_shape=[
            jax.ShapeDtypeStruct((SLOTS, D), low),
            jax.ShapeDtypeStruct((SLOTS, D), full),
            jax.ShapeDtypeStruct((rows if summed else D, 3 * D), full),
            jax.ShapeDtypeStruct((rows if summed else D, D), full),
            jax.ShapeDtypeStruct((rows if summed else D, LANES), full),
            jax.ShapeDtypeStruct((reps * piece, D), low),
            jax.ShapeDtypeStruct((D, reps * piece), low),
            jax.ShapeDtypeStruct((reps, tail_rows - piece, D), low),
        ],
        in_specs=[anywhere] * 4
        + [inside] * 3
        + [anywhere] * 9
        + [inside] * 4
        + [anywhere] * 2,
        out_specs=[inside] * 2 + [inside if summed else anywhere] * 3 + [anywhere] * 3,
        scratch_shapes=scratch,
        compiler_params=pltpu.CompilerParams(
            collective_id=1, has_side_effects=True, vmem_limit_bytes=63 * 1024 * 1024
        ),
        name="backward",
    )
    gradients = list(call(*operands))
    if not summed:
        for index in (2, 3, 4):
            gradients[index] = lax.psum_scatter(
                gradients[index], ("exp", "rep"), scatter_dimension=0, tiled=True
            )
    return gradients


def exchange(blocks):
    return lax.all_to_all(blocks, "exp", split_axis=0, concat_axis=0, tiled=True)


def on_device(
    tokens,
    ln1_gain,
    ln1_bias,
    w_qkv,
    w_out,
    ln2_gain,
    ln2_bias,
    w_router,
    w_in,
    b_in,
    w_back,
    b_back,
    lengths,
    routes,
    priority,
    padding,
    cotangent,
):
    experts = lax.axis_size("exp")
    reps = lax.axis_size("rep")
    devices = experts * reps
    capacity = (TOK_DEV * 210 + experts * 100 - 1) // (experts * 100)
    padded = -(-(capacity + 3) // 16) * 16
    rows = w_qkv.shape[0]
    small = jnp.concatenate(
        [w_router, jnp.stack([ln1_gain, ln1_bias, ln2_gain, ln2_bias], axis=1)], axis=1
    )
    small = jnp.pad(small, ((0, 0), (0, LANES - small.shape[1])))
    rest = jnp.concatenate([w_out, small], axis=1)
    qkv_weight, rest_weight = gather_blocks(w_qkv, rest, devices, reps)
    qkv_weight = qkv_weight.reshape(D, 3 * D)
    rest_weight = rest_weight.reshape(D, rest.shape[1])
    out_weight = rest_weight[:, :D]
    router_weight = rest_weight[:, D : D + experts]
    vectors = rest_weight[:, D + experts : D + experts + 4].T
    gain_one, bias_one, gain_two, bias_two = (vectors[0], vectors[1], vectors[2], vectors[3])

    first_hot, second_hot, pick_first, pick_second = dispatch_tables(
        routes, priority, padding, experts, capacity, padded
    )
    picks = pick_first + pick_second
    grad_blocks = lax.dot_general(picks, cotangent, contract_first, preferred_element_type=jnp.float32)
    grad_blocks = grad_blocks.astype(jnp.bfloat16).reshape(experts, padded, D)
    grad_blocks, gathered_done = lax.optimization_barrier((grad_blocks, qkv_weight))
    qkv_weight = gathered_done
    grad_arrived = exchange(grad_blocks)

    inputs = tokens.astype(jnp.float32)
    normed, normal_one, inverse_one = norm_forward(inputs, gain_one, bias_one)
    normed_low = normed.astype(jnp.bfloat16)
    qkv = (
        jnp.dot(normed_low, qkv_weight, preferred_element_type=jnp.float32)
        .astype(jnp.bfloat16)
        .reshape(ROWS_DEV, SLOTS, 3 * D)
    )
    bounds = jnp.cumsum(lengths[0])
    segments = jnp.sum(
        (jnp.arange(SLOTS, dtype=jnp.int32)[:, None] >= bounds[None, :]).astype(jnp.int32), axis=1
    )
    mixed_low = attend(qkv[0], segments, padding)
    resid = inputs + jnp.dot(mixed_low, out_weight, preferred_element_type=jnp.float32)
    routed_float, normal_two, inverse_two = norm_forward(resid, gain_two, bias_two)
    routed = routed_float.astype(jnp.bfloat16)
    logits = jnp.dot(routed, router_weight, preferred_element_type=jnp.float32)
    probs = jax.nn.softmax(logits, axis=-1)
    gate_first = jnp.sum(probs * first_hot, axis=1)
    gate_second = jnp.sum(probs * second_hot, axis=1)
    buffer = lax.dot_general(picks, routed, contract_first, preferred_element_type=jnp.float32)
    buffer = buffer.astype(jnp.bfloat16).reshape(experts, padded, D)
    slot_gates = jnp.sum(
        pick_first.astype(jnp.float32) * gate_first[:, None]
        + pick_second.astype(jnp.float32) * gate_second[:, None],
        axis=0,
    ).reshape(experts, padded)[:, :capacity]
    high = lax.reduce_precision(slot_gates, 8, 7)
    middle = lax.reduce_precision(slot_gates - high, 8, 7)
    terms = jnp.stack([high, middle, slot_gates - high - middle], axis=1).astype(jnp.bfloat16)
    terms = jnp.pad(terms, ((0, 0), (0, padded - capacity - 3), (0, D - capacity)))
    buffer = lax.dynamic_update_slice(buffer, terms, (0, capacity, 0))
    grad_buffer, result, half_back, half_in = run_experts(
        buffer, grad_arrived, w_in[0], w_back[0], b_in, b_back, capacity, reps
    )
    terms = grad_buffer[:, capacity : capacity + 3, :padded].transpose(1, 0, 2)
    terms = jnp.pad(terms.reshape(3, experts * padded), ((0, 13), (0, 0)))
    (
        output,
        grad_tokens,
        sum_qkv,
        sum_out,
        sum_small,
        all_back,
        all_in,
        all_tail,
    ) = run_backward(
        (
            grad_buffer.reshape(experts * padded, D),
            result,
            pick_first,
            pick_second,
            terms,
            jnp.pad(probs, ((0, 0), (0, LANES - experts))),
            routes,
            cotangent,
            resid,
            tokens,
            normed_low,
            routed,
            qkv[0],
            mixed_low,
            qkv_weight,
            rest_weight,
            vectors.astype(jnp.float32),
            segments.reshape(SLOTS, 1),
            segments.reshape(1, SLOTS),
            padding.reshape(SLOTS, 1),
            half_back,
            half_in,
        ),
        experts,
        reps,
        rows,
    )
    vector_sums = sum_small[:, experts : experts + 4]
    hidden = b_in.shape[1]
    piece = hidden // reps
    return (
        output,
        grad_tokens,
        vector_sums[:, 0],
        vector_sums[:, 1],
        sum_qkv,
        sum_out,
        vector_sums[:, 2],
        vector_sums[:, 3],
        sum_small[:, :experts],
        all_in[None].astype(jnp.float32),
        all_tail[:, 0, :piece].astype(jnp.float32).reshape(1, hidden),
        all_back[None].astype(jnp.float32),
        all_tail[:1, 1, :].astype(jnp.float32),
    )


def solution(mesh):
    return jax.shard_map(
        on_device,
        mesh=mesh,
        in_specs=(
            P(("exp", "rep"), None),
            P(("exp", "rep")),
            P(("exp", "rep")),
            P(("exp", "rep"), None),
            P(("exp", "rep"), None),
            P(("exp", "rep")),
            P(("exp", "rep")),
            P(("exp", "rep"), None),
            P("exp", None, None),
            P("exp", None),
            P("exp", None, None),
            P("exp", None),
            P(("exp", "rep"), None),
            P(("exp", "rep"), None),
            P(("exp", "rep")),
            P(("exp", "rep")),
            P(("exp", "rep"), None),
        ),
        out_specs=(
            P(("exp", "rep"), None),
            P(("exp", "rep"), None),
            P(("exp", "rep")),
            P(("exp", "rep")),
            P(("exp", "rep"), None),
            P(("exp", "rep"), None),
            P(("exp", "rep")),
            P(("exp", "rep")),
            P(("exp", "rep"), None),
            P("exp", None, None),
            P("exp", None),
            P("exp", None, None),
            P("exp", None),
        ),
        check_vma=False,
    )
```
